32 devices in a mesh: tile: 8 (over z, x), mem: 4 (over y, core).
Axes of the slice: x: 2, y: 2, z: 4, core: 2. Of those that a mesh axis runs over, the one named last changes fastest.
Arguments:
- alpha: float32 [4, 16, 64, 1024], P('mem', None, None, 'tile'), may hold values from -6 to 6
- members: bfloat16 [4, 16, 64, 1024], P('mem', None, None, 'tile'), may hold values from -6 to 6
- mem_weight: float32 [4], P('mem'), may hold values from 0.5 to 2
- kappa: float32 [64, 1024], P(None, 'tile'), may hold values from 0.04 to 0.24
- norm_scale: float32 [64, 1024], P(None, 'tile'), may hold values from 0.8 to 1.25
- land_sea: int32 [64, 1024], P(None, 'tile'), may hold values 0 or 1
- obs_cell: int32 [16384], P('tile'), may hold values from 0 to 131071
- obs_weight: float32 [16384], P('tile'), may hold values from 0.5 to 4
Outputs:
- product: float32 [4, 16, 64, 1024], P('mem', None, None, 'tile')
The draws below stay inside these ranges and needn't reach their ends.
Inputs may be any that keep to these rules, and one draw needn't show every extreme that they name: `obs_cell`: observations o of tile t = o // 2048 index a cell of that tile; several may share a cell.
All inputs are finite; a program needn't handle non-finite values. No bound on the sum of `land_sea` on one device may be relied on, other than what follows from the above.
Results may differ from the reference program's by a relative error of at most 0.0003.
Values sent between devices are 32-bit elements; how exact they have to be, the bound alone decides.
No kernel may reach another device: no remote copies, remote signals or barrier semaphores. Data moves between devices by JAX's collectives and lax.ppermute only.
A program may use at most 64 MiB of HBM per device.

```python
import math
import jax
import jax.numpy as jnp
from jax import lax

LEV = 16
NY = 64
NXT = 128
STEPS = 8
OBS_DEV = 2048
MEM = 4
NX = 1024
N_TILE = 8


def with_ends(drawn, rng, least, high):
    place = [jax.random.randint(jax.random.fold_in(rng, axis), (), 0, length) for axis, length in enumerate(drawn.shape)]
    main_axis = drawn.shape.index(max(drawn.shape))
    next_to = place[:main_axis] + [(place[main_axis] + 1) % drawn.shape[main_axis]] + place[main_axis + 1:]
    return drawn.at[tuple(place)].set(least).at[tuple(next_to)].set(high)


def block_levels(own_key, shape, shards, low, largest):
    factor_of, own = 1.0, jax.random.fold_in(own_key, 6)
    for dim, blocks in shards:
        draws = jnp.exp(jax.random.uniform(jax.random.fold_in(own, dim), (blocks,), jnp.float32, low / len(shards), largest / len(shards)))
        factor_of = factor_of * jnp.repeat(draws, shape[dim] // blocks).reshape([-1 if axis == dim else 1 for axis in range(len(shape))])
    return factor_of


def bell_draw(rng, shape, deviation, bound, pieces=(), held_as=jnp.bfloat16):
    level = block_levels(rng, shape, pieces, -0.22, 0.18) if pieces else 1.0
    values = jax.random.normal(rng, shape, jnp.float32) * deviation * level
    return jnp.minimum(jnp.maximum(values, -bound), bound).astype(held_as)


def setup_inputs(seed: int = 0) -> dict:
    splits = jax.random.split(jax.random.key(seed), 9)
    return {
        "alpha": bell_draw(splits[0], (MEM, LEV, NY, NX), 1.0, 6.0, ((0, 4), (3, 8)), jnp.float32),
        "members": bell_draw(splits[1], (MEM, LEV, NY, NX), 1.0, 6.0, ((0, 4), (3, 8))),
        "mem_weight": jnp.clip(jnp.exp(math.log(2.0) - 1.3862944 * jax.random.uniform(splits[2], (MEM,), jnp.float32) ** block_levels(splits[2], (MEM,), ((0, 4),), -0.2, 0.2)), 0.5, 2.0),
        "kappa": jnp.clip(0.04 + 0.19999999552965164 * jax.random.uniform(splits[3], (NY, NX), jnp.float32) ** block_levels(splits[3], (NY, NX), ((1, 8),), -0.2, 0.2), 0.04, 0.24),
        "norm_scale": jnp.clip(0.8 + 0.45 * jax.random.uniform(splits[4], (NY, NX), jnp.float32) ** block_levels(splits[4], (NY, NX), ((1, 8),), -0.2, 0.2), 0.8, 1.25),
        "land_sea": with_ends((jax.random.randint(splits[5], (NY, NX), 0, 5) < 4).astype(jnp.int32), jax.random.fold_in(splits[5], 1), 0, 1),
        "obs_cell": with_ends(jax.random.randint(splits[6], (N_TILE * OBS_DEV,), 0, LEV * NY * NXT), jax.random.fold_in(splits[6], 1), 0, (LEV * NY * NXT) - 1).astype(jnp.int32),
        "obs_weight": jnp.clip(jnp.exp(math.log(4.0) - 2.0794415 * jax.random.uniform(splits[7], (N_TILE * OBS_DEV,), jnp.float32) ** block_levels(splits[7], (N_TILE * OBS_DEV,), ((0, 8),), -0.2, 0.2)), 0.5, 4.0),
    }


def shift_up(u):
    return jnp.concatenate([u[..., 1:, :], jnp.zeros_like(u[..., :1, :])], -2)


def shift_down(u):
    return jnp.concatenate([jnp.zeros_like(u[..., :1, :]), u[..., :-1, :]], -2)


def faces(kappa, land_sea):
    ocean = land_sea.astype(jnp.float32)
    east = 0.5 * (kappa + jnp.roll(kappa, -1, 1)) * ocean * jnp.roll(ocean, -1, 1)
    north = 0.5 * (kappa[:-1] + kappa[1:]) * ocean[:-1] * ocean[1:]
    north = jnp.concatenate([north, jnp.zeros((1, north.shape[1]), jnp.float32)], 0)
    return east, north


def smooth(u, east, north):
    across = east * (jnp.roll(u, -1, -1) - u) - jnp.roll(east, 1, 1) * (u - jnp.roll(u, 1, -1))
    along = north * (shift_up(u) - u) - shift_down(north) * (u - shift_down(u))
    return u + across + along


def reference(alpha, members, mem_weight, kappa, norm_scale, land_sea, obs_cell, obs_weight):
    east, north = faces(kappa, land_sea)

    def forward(u):
        for step in range(STEPS):
            u = smooth(norm_scale * u, east, north)
        return u

    def adjoint(u):
        for step in range(STEPS):
            u = norm_scale * smooth(u, east, north)
        return u

    def accumulate(total, item):
        field, member, weight = item
        return total + weight * member.astype(jnp.float32) * forward(field), None

    start = jnp.zeros((LEV, NY, NX), jnp.float32)
    increment, unused = lax.scan(accumulate, start, (alpha, members, mem_weight))
    owner = (jnp.arange(N_TILE * OBS_DEV, dtype=jnp.int32) // OBS_DEV).astype(jnp.int32)
    level = obs_cell // (NY * NXT)
    row = (obs_cell // NXT) % NY
    column = obs_cell % NXT + owner * NXT
    flat = ((level * NY + row) * NX + column).astype(jnp.int32)
    obs_field = jnp.zeros((LEV * NY * NX,), jnp.float32).at[flat].add(obs_weight).reshape(LEV, NY, NX)
    gradient = obs_field * increment

    def finish(item):
        field, member, weight = item
        return field + adjoint(weight * member.astype(jnp.float32) * gradient)

    return lax.map(finish, (alpha, members, mem_weight))
```

```python
import functools

import jax
import jax.numpy as jnp
from jax import lax
from jax.experimental import pallas as pl
from jax.experimental.pallas import tpu as pltpu
from jax.sharding import PartitionSpec as P

STEPS = 8
SUB = 8
EDGE = 2 * STEPS
F32 = jnp.float32
BF16 = jnp.bfloat16


def div_mod(value, size):
    if size & (size - 1) == 0:
        return value >> (size.bit_length() - 1), value & (size - 1)
    return lax.div(value, size), lax.rem(value, size)


def roll(value, shift, axis=1):
    shift %= value.shape[axis]
    return pltpu.roll(value, shift, axis) if shift else value


def lanes(shape=(SUB, 128)):
    return lax.broadcasted_iota(jnp.int32, shape, len(shape) - 1)


def split(value):
    high = value.astype(BF16)
    return high, (value - high.astype(F32)).astype(BF16)


class Sizes:
    def __init__(self, levels, rows, columns, obs):
        self.levels, self.rows, self.columns, self.obs = levels, rows, columns, obs
        self.groups = levels // SUB
        self.half = rows // 2
        assert columns == 128 and self.groups == 2 and rows % 16 == 0
        assert levels % SUB == 0 and obs % 256 == 0 and STEPS == 8
        self.tall = rows * SUB
        self.at_coeff = self.half * SUB
        self.at_obs = self.at_coeff + self.half
        self.obs_rows = obs // 128
        self.payload = self.at_obs + 2 * self.obs_rows
        self.quarter = rows // 4
        self.short = self.quarter * SUB


def level_rows(z, group, row):
    return pl.ds(group * SUB * z.rows + row, SUB, stride=z.rows)


def pack_kernel(z, alpha, members, kappa, scale, ocean, cell, weight, out_a, out_b, wide):
    even = lax.rem(lax.axis_index("tile"), 2) == 0
    wide[...] = members[...].astype(F32)
    lane = lanes()

    def put(where, right, left):
        out_a[where, :] = jnp.where(even, right, left)
        out_b[where, :] = jnp.where(even, left, right)

    for q in range(z.half):
        right = left = None
        for h in range(2):
            for g in range(2):
                rows = level_rows(z, g, q + h * z.half)
                a, m = alpha[rows, :], wide[rows, :]
                base = 64 * g + 32 * h
                r_part = roll(jnp.where(lane >= 128 - EDGE, a, roll(m, -EDGE)), base - (128 - 2 * EDGE))
                l_part = roll(jnp.where(lane < EDGE, m, roll(a, EDGE)), base)
                if right is None:
                    right, left = r_part, l_part
                else:
                    here = (lane >= base) & (lane < base + 32)
                    right, left = jnp.where(here, r_part, right), jnp.where(here, l_part, left)
        put(pl.ds(q * SUB, SUB), right, left)
    lane = lanes((z.half, 128))
    right = left = None
    for h in range(2):
        rows = pl.ds(h * z.half, z.half)
        for k, ref in enumerate((kappa, scale, ocean)):
            value = ref[rows, :].astype(F32)
            base = 64 * h + EDGE * k
            r_part, l_part = roll(value, base - (128 - EDGE)), roll(value, base)
            if right is None:
                right, left = r_part, l_part
            else:
                here = (lane >= base) & (lane < base + EDGE)
                right, left = jnp.where(here, r_part, right), jnp.where(here, l_part, left)
    put(pl.ds(z.at_coeff, z.half), right, left)
    n = z.obs_rows
    for at, value in ((z.at_obs, cell[...].astype(F32)), (z.at_obs + n, weight[...])):
        out_a[pl.ds(at, n), :] = value
        out_b[pl.ds(at, n), :] = value


def up(value):
    return roll(value, -1, 0)


def down(value):
    return roll(value, 1, 0)


def coefficients(kappa, scale, ocean, forward):
    row = lax.broadcasted_iota(jnp.int32, kappa.shape, 0)
    north = 0.5 * (kappa + up(kappa)) * ocean * up(ocean)
    north = jnp.where(row == kappa.shape[0] - 1, 0.0, north)
    east = 0.5 * (kappa + roll(kappa, -1)) * ocean * roll(ocean, -1)
    west, south = roll(east, 1), down(north)
    centre = 1.0 - (east + west) - (north + south)
    if forward:
        return (
            centre * scale,
            east * roll(scale, -1),
            west * roll(scale, 1),
            north * up(scale),
            south * down(scale),
        )
    return tuple(scale * c for c in (centre, east, west, north, south))


def put_coefficients(ref, values):
    rows = values[0].shape[0]
    for k, value in enumerate(values):
        for r in range(rows):
            ref[k, pl.ds(r * SUB, SUB), :] = jnp.broadcast_to(value[r : r + 1, :], (SUB, value.shape[1]))


def step_rows(x, coeff, rows, blocks):
    at = lambda r, b: (pl.ds(r * SUB, SUB), pl.ds(b * 128, 128))
    before = [None] * blocks
    here = [x[at(0, b)] for b in range(blocks)]
    for r in range(rows):
        c = [coeff[k, pl.ds(r * SUB, SUB), :] for k in range(5)]
        for b in range(blocks):
            u = here[b]
            new = c[0] * u + (c[1] * roll(u, -1) + c[2] * roll(u, 1))
            after = x[at(r + 1, b)] if r + 1 < rows else None
            if after is not None:
                new = new + c[3] * after
            if before[b] is not None:
                new = new + c[4] * before[b]
            x[at(r, b)] = new
            before[b], here[b] = u, after


def main_kernel(z, alpha, members, weight, kappa, scale, ocean, out, coeff, wide):
    wide[...] = members[...].astype(F32) * weight[0]
    put_coefficients(coeff, coefficients(kappa[...], scale[...], ocean[...].astype(F32), True))
    for r in range(z.rows):
        for g in range(2):
            out[pl.ds(r * SUB, SUB), pl.ds(128 * g, 128)] = alpha[level_rows(z, g, r), :]

    def step(_, carry):
        step_rows(out, coeff, z.rows, 2)
        return carry

    lax.fori_loop(0, STEPS, step, 0)
    for r in range(z.rows):
        for g in range(2):
            at = (pl.ds(r * SUB, SUB), pl.ds(128 * g, 128))
            out[at] = out[at] * wide[level_rows(z, g, r), :]


def own_index(z, cell):
    level, rest = div_mod(cell, z.rows * z.columns)
    row, column = div_mod(rest, z.columns)
    return row * SUB + (level & (SUB - 1)), (level >> 3) * 128 + column


def beside_index(z, cell, left):
    level, rest = div_mod(cell, z.rows * z.columns)
    row, column = div_mod(rest, z.columns)
    quarter, row = div_mod(row, z.quarter)
    first = z.columns - STEPS if left else 0
    inside = (column >= first) & (column < first + STEPS)
    lane = (40 if left else 16) + (column - first) + 64 * (level >> 3) + 16 * quarter
    return jnp.where(inside, row * SUB + (level & (SUB - 1)), -1), lane & 127


def quarter_mask(lane, k):
    unit = lane >> 3
    return (((unit & 1) == 0) & ((((unit - 2) >> 1) & 3) == k)) | (
        ((unit & 1) == 1) & ((((unit - 5) >> 1) & 3) == k)
    )


def one_hot(index, size):
    rows = lax.broadcasted_iota(jnp.int32, (size, index.shape[1]), 0)
    return jnp.where(rows == index, 1.0, 0.0).astype(BF16)


def read_off(field_high, field_low, i, j):
    hot = one_hot(i, field_high.shape[0])
    dims = (((0,), (0,)), ((), ()))
    value = lax.dot_general(field_high, hot, dims, preferred_element_type=F32)
    value = value + lax.dot_general(field_low, hot, dims, preferred_element_type=F32)
    rows = lax.broadcasted_iota(jnp.int32, value.shape, 0)
    return jnp.sum(jnp.where(rows == j, value, 0.0), axis=0, keepdims=True)


CHUNK = 256


def strip_kernel(z, main, sent_a, sent_b, got_a, got_b, cell, weight, out, strip_members, strip_coeff, x, coeff, beside, merged):
    even = lax.rem(lax.axis_index("tile"), 2) == 0
    lane = lanes()

    def parts(rows):
        sa, sb, ga, gb = sent_a[rows, :], sent_b[rows, :], got_a[rows, :], got_b[rows, :]
        pick = lambda p, q: jnp.where(even, p, q)
        return pick(sa, sb), pick(ga, gb), pick(gb, ga), pick(sb, sa)

    for q in range(z.half):
        four = parts(pl.ds(q * SUB, SUB))
        for h in range(2):
            at = pl.ds((q + h * z.half) * SUB, SUB)
            for ref, offset in ((strip_members, 0), (x, -EDGE)):
                value = None
                for p, part in enumerate(four):
                    piece = roll(part, EDGE * p - 32 * h + offset)
                    value = piece if p == 0 else jnp.where(((lane >> 4) & 3) == p, piece, value)
                ref[at, :] = value * weight[0] if offset == 0 else value
    four = parts(pl.ds(z.at_coeff, z.half))
    lane = lanes((z.half, 128))
    for k in range(3):
        for h in range(2):
            value = None
            for g in range(2):
                for p, part in enumerate(four):
                    piece = roll(part, EDGE * p + 64 * g - 64 * h - EDGE * k)
                    value = piece if value is None else jnp.where((lane >> 4) == 4 * g + p, piece, value)
            strip_coeff[k, pl.ds(h * z.half, z.half), :] = value
    put_coefficients(coeff, coefficients(strip_coeff[0], strip_coeff[1], strip_coeff[2], True))

    def step(_, carry):
        step_rows(x, coeff, z.rows, 1)
        return carry

    lax.fori_loop(0, STEPS, step, 0)
    lane = lanes()
    for r in range(z.rows):
        at = pl.ds(r * SUB, SUB)
        value = x[at, :] * strip_members[at, :]
        x[at, :] = value
        for g in range(2):
            here = (at, pl.ds(128 * g, 128))
            fixed = jnp.where(lane >= z.columns - STEPS, roll(value, 112 - 64 * g), main[here])
            merged[here] = jnp.where(lane < STEPS, roll(value, -48 - 64 * g), fixed)
    for q in range(z.quarter):
        value = None
        for k in range(4):
            piece = roll(x[pl.ds((k * z.quarter + q) * SUB, SUB), :], 16 * k)
            value = piece if k == 0 else jnp.where(quarter_mask(lane, k), piece, value)
        beside[pl.ds(q * SUB, SUB), :] = value

    def gather(at, index, high, low, i_j):
        for n in range(z.obs_rows // 2):
            row = jnp.concatenate([index[2 * n : 2 * n + 1, :], index[2 * n + 1 : 2 * n + 2, :]], axis=1)
            value = read_off(high, low, *i_j(row))
            out[at + 2 * n : at + 2 * n + 1, :] = value[:, :128]
            out[at + 2 * n + 1 : at + 2 * n + 2, :] = value[:, 128:]

    high, low = split(merged[...])
    gather(0, cell[...], high, low, lambda c: own_index(z, c))
    high, low = split(beside[...])
    rows = pl.ds(z.at_obs, z.obs_rows)
    _, right, left, _ = parts(rows)
    gather(z.obs_rows, right.astype(jnp.int32), high, low, lambda c: beside_index(z, c, False))
    gather(2 * z.obs_rows, left.astype(jnp.int32), high, low, lambda c: beside_index(z, c, True))


def adjoint_kernel(
    z, alpha, members, weight, kappa, scale, ocean, cell, obs_weight, got_a, got_b, strip_members, strip_coeff,
    v0, v1, v2, v3, out, x, coeff, strip, strip_c, beside, wide, hot, spread,
):
    even = lax.rem(lax.axis_index("tile"), 2) == 0
    lane = lanes()
    wide[...] = members[...].astype(F32) * weight[0]
    put_coefficients(coeff, coefficients(kappa[...], scale[...], ocean[...].astype(F32), False))
    put_coefficients(strip_c, coefficients(strip_coeff[0], strip_coeff[1], strip_coeff[2], False))
    value = (v0[...] + v1[...]) + (v2[...] + v3[...])
    n = z.obs_rows
    pick = lambda p, q: jnp.where(even, p, q)
    cells, weights = pl.ds(z.at_obs, n), pl.ds(z.at_obs + n, n)
    right = pick(got_a[cells, :], got_b[cells, :]).astype(jnp.int32)
    left = pick(got_b[cells, :], got_a[cells, :]).astype(jnp.int32)
    right_weight = pick(got_a[weights, :], got_b[weights, :])
    left_weight = pick(got_b[weights, :], got_a[weights, :])

    def spread_out(groups, tall, wide_):
        at = 0
        for index, amount, i_j in groups:
            for r in range(n):
                i, j = i_j(index[r : r + 1, :])
                hot[:tall, pl.ds(at * 128, 128)] = one_hot(i, tall)
                rows = lax.broadcasted_iota(jnp.int32, (wide_, 128), 0)
                high, low = split(jnp.where(rows == j, amount[r : r + 1, :], 0.0))
                spread[:wide_, pl.ds(at * 128, 128)] = high
                spread[pl.ds(wide_, wide_), pl.ds(at * 128, 128)] = low
                at += 1
        dims = (((1,), (1,)), ((), ()))
        value = lax.dot_general(hot[:tall, : at * 128], spread[: 2 * wide_, : at * 128], dims, preferred_element_type=F32)
        return value[:, :wide_] + value[:, wide_:]

    x[...] = spread_out([(cell[...], obs_weight[...] * value[:n], lambda c: own_index(z, c))], z.tall, 256)
    beside[...] = spread_out(
        [
            (right, right_weight * value[n : 2 * n], lambda c: beside_index(z, c, False)),
            (left, left_weight * value[2 * n :], lambda c: beside_index(z, c, True)),
        ],
        z.short,
        128,
    )
    part = (lane >> 4) & 3
    within = lane & 15
    outer = ((part == 1) & (within < STEPS)) | ((part == 2) & (within >= STEPS))
    for r in range(z.rows):
        at = pl.ds(r * SUB, SUB)
        k, q = divmod(r, z.quarter)
        value = jnp.where(outer, roll(beside[pl.ds(q * SUB, SUB), :], -16 * k), 0.0)
        for g in range(2):
            here = (at, pl.ds(128 * g, 128))
            field = x[here]
            mine = (lane >> 6) == g
            value = jnp.where(mine & (part == 0), roll(field, EDGE + 64 * g), value)
            value = jnp.where(mine & (part == 3), roll(field, 48 + 64 * g), value)
            x[here] = field * wide[level_rows(z, g, r), :]
        strip[at, :] = value * strip_members[at, :]

    def step(_, carry):
        step_rows(x, coeff, z.rows, 2)
        step_rows(strip, strip_c, z.rows, 1)
        return carry

    lax.fori_loop(0, STEPS, step, 0)
    for r in range(z.rows):
        at = pl.ds(r * SUB, SUB)
        value = strip[at, :]
        for g in range(2):
            fixed = jnp.where(lane >= z.columns - STEPS, roll(value, 112 - 64 * g), x[at, pl.ds(128 * g, 128)])
            fixed = jnp.where(lane < STEPS, roll(value, -48 - 64 * g), fixed)
            rows = level_rows(z, g, r)
            out[rows, :] = alpha[rows, :] + fixed


def local(alpha, members, mem_weight, kappa, norm_scale, land_sea, obs_cell, obs_weight):
    shape = alpha.shape
    z = Sizes(shape[1], shape[2], shape[3], obs_cell.shape[0])
    tiles, holders = lax.axis_size("tile"), lax.axis_size("mem")
    assert tiles % 2 == 0 and holders == 4 and shape[0] == 1
    alpha = alpha.reshape(z.levels * z.rows, z.columns)
    members = members.reshape(z.levels * z.rows, z.columns)
    cell = obs_cell.reshape(z.obs_rows, 128)
    weight = obs_weight.reshape(z.obs_rows, 128)
    smem = pl.BlockSpec(memory_space=pltpu.SMEM)
    whole = pl.BlockSpec(memory_space=pltpu.VMEM)
    sds = jax.ShapeDtypeStruct
    field = pltpu.VMEM((z.levels * z.rows, z.columns), F32)
    coeff = pltpu.VMEM((5, z.tall, 128), F32)
    payload = sds((z.payload, 128), F32)
    sent_a, sent_b = pl.pallas_call(
        functools.partial(pack_kernel, z),
        out_shape=(payload, payload),
        scratch_shapes=[field],
        name="pack",
    )(alpha, members, kappa, norm_scale, land_sea, cell, weight)
    near = [(i, i ^ 1) for i in range(tiles)]
    far = [(i, (i + 1) % tiles if i % 2 else (i - 1) % tiles) for i in range(tiles)]
    got_a = lax.ppermute(sent_a, "tile", near)
    got_b = lax.ppermute(sent_b, "tile", far)
    main = pl.pallas_call(
        functools.partial(main_kernel, z),
        out_shape=sds((z.tall, 256), F32),
        in_specs=[whole, whole, smem, whole, whole, whole],
        scratch_shapes=[coeff, field],
        name="main",
    )(alpha, members, mem_weight, kappa, norm_scale, land_sea)
    values, strip_members, strip_coeff = pl.pallas_call(
        functools.partial(strip_kernel, z),
        out_shape=(sds((3 * z.obs_rows, 128), F32), sds((z.tall, 128), F32), sds((3, z.rows, 128), F32)),
        in_specs=[whole] * 6 + [smem],
        scratch_shapes=[
            pltpu.VMEM((z.tall, 128), F32),
            coeff,
            pltpu.VMEM((z.short, 128), F32),
            pltpu.VMEM((z.tall, 256), F32),
        ],
        name="strip",
    )(main, sent_a, sent_b, got_a, got_b, cell, mem_weight)
    others = [lax.ppermute(values, "mem", [(i, i ^ k) for i in range(holders)]) for k in range(1, holders)]
    product = pl.pallas_call(
        functools.partial(adjoint_kernel, z),
        out_shape=sds((z.levels * z.rows, z.columns), F32),
        in_specs=[whole, whole, smem] + [whole] * 13,
        scratch_shapes=[
            pltpu.VMEM((z.tall, 256), F32),
            coeff,
            pltpu.VMEM((z.tall, 128), F32),
            coeff,
            pltpu.VMEM((z.short, 128), F32),
            field,
            pltpu.VMEM((z.tall, 2 * z.obs), BF16),
            pltpu.VMEM((512, 2 * z.obs), BF16),
        ],
        name="adjoint",
    )(alpha, members, mem_weight, kappa, norm_scale, land_sea, cell, weight, got_a, got_b, strip_members, strip_coeff, values, *others)
    return product.reshape(shape)


def solution(mesh):
    placed = (
        P("mem", None, None, "tile"),
        P("mem", None, None, "tile"),
        P("mem"),
        P(None, "tile"),
        P(None, "tile"),
        P(None, "tile"),
        P("tile"),
        P("tile"),
    )
    return jax.shard_map(
        local, mesh=mesh, in_specs=placed, out_specs=P("mem", None, None, "tile"), check_vma=False
    )
```

```python
import functools

import jax
import jax.numpy as jnp
from jax import lax
from jax.experimental import pallas as pl
from jax.experimental.pallas import tpu as pltpu
from jax.sharding import PartitionSpec as P

STEPS = 8
SUB = 8
EDGE = 2 * STEPS
F32 = jnp.float32
BF16 = jnp.bfloat16


def div_mod(value, size):
    if size & (size - 1) == 0:
        return value >> (size.bit_length() - 1), value & (size - 1)
    return lax.div(value, size), lax.rem(value, size)


def roll(value, shift, axis=1):
    shift %= value.shape[axis]
    return pltpu.roll(value, shift, axis) if shift else value


def lanes(rows):
    return lax.broadcasted_iota(jnp.int32, (rows, 128), 1)


def split(value):
    high = value.astype(BF16)
    return high, (value - high.astype(F32)).astype(BF16)


class Sizes:
    def __init__(self, levels, rows, columns, obs):
        self.levels, self.rows, self.columns, self.obs = levels, rows, columns, obs
        assert columns == 128 and levels == 16 and rows % 16 == 0 and obs % 256 == 0 and STEPS == 8
        self.field = levels * rows
        self.group = self.field // 2
        self.half = self.field // 4
        self.short = self.field // 8
        self.at_coeff = self.half
        self.at_obs = self.at_coeff + rows // 2
        self.obs_rows = obs // 128
        self.payload = self.at_obs + 2 * self.obs_rows


def overlay(pieces, window):
    value = pieces[0]
    for k in range(1, len(pieces)):
        value = jnp.where(window == k, pieces[k], value)
    return value


def pack_kernel(z, alpha, members, kappa, scale, ocean, cell, weight, out_a, out_b):
    even = lax.rem(lax.axis_index("tile"), 2) == 0

    def put(where, right, left):
        out_a[where, :] = jnp.where(even, right, left)
        out_b[where, :] = jnp.where(even, left, right)

    block = 2 * SUB
    lane = lanes(block)
    for q in range(z.half // block):
        right, left = [], []
        for g in range(2):
            for h in range(2):
                rows = pl.ds(g * z.group + h * z.half + q * block, block)
                a, m = alpha[rows, :], members[rows, :].astype(F32)
                base = 64 * g + 32 * h
                right.append(roll(jnp.where(lane >= 128 - EDGE, a, roll(m, -EDGE)), base - (128 - 2 * EDGE)))
                left.append(roll(jnp.where(lane < EDGE, m, roll(a, EDGE)), base))
        put(pl.ds(q * block, block), overlay(right, lane >> 5), overlay(left, lane >> 5))
    half = z.rows // 2
    lane = lanes(half)
    right, left = [], []
    for h in range(2):
        rows = pl.ds(h * half, half)
        for k, ref in enumerate((kappa, scale, ocean)):
            value = ref[rows, :].astype(F32)
            base = 64 * h + EDGE * k
            right.append(roll(value, base - (128 - EDGE)))
            left.append(roll(value, base))
        right.append(right[-1])
        left.append(left[-1])
    put(pl.ds(z.at_coeff, half), overlay(right, lane >> 4), overlay(left, lane >> 4))
    n = z.obs_rows
    for at, value in ((z.at_obs, cell[...].astype(F32)), (z.at_obs + n, weight[...])):
        out_a[pl.ds(at, n), :] = value
        out_b[pl.ds(at, n), :] = value


def up(value):
    return roll(value, -1, 0)


def down(value):
    return roll(value, 1, 0)


def coefficients(kappa, scale, ocean, forward):
    row = lax.broadcasted_iota(jnp.int32, kappa.shape, 0)
    north = 0.5 * (kappa + up(kappa)) * ocean * up(ocean)
    north = jnp.where(row == kappa.shape[0] - 1, 0.0, north)
    east = 0.5 * (kappa + roll(kappa, -1)) * ocean * roll(ocean, -1)
    west, south = roll(east, 1), down(north)
    centre = 1.0 - (east + west) - (north + south)
    if forward:
        return (
            centre * scale,
            east * roll(scale, -1),
            west * roll(scale, 1),
            north * up(scale),
            south * down(scale),
        )
    return tuple(scale * c for c in (centre, east, west, north, south))


def put_coefficients(ref, values):
    for k, value in enumerate(values):
        ref[k] = value


def step_rows(source, target, coeff, rows, levels):
    for t in range(rows // SUB):
        c = [coeff[k, pl.ds(t * SUB, SUB), :] for k in range(5)]
        for level in range(levels):
            at = SUB + level * rows + t * SUB
            u = source[pl.ds(at, SUB), :]
            along = c[3] * source[pl.ds(at + 1, SUB), :] + c[4] * source[pl.ds(at - 1, SUB), :]
            across = c[1] * roll(u, -1) + c[2] * roll(u, 1)
            target[pl.ds(at, SUB), :] = c[0] * u + across + along


def clear_ends(*buffers):
    for ref in buffers:
        zero = jnp.zeros((SUB, 128), F32)
        ref[pl.ds(0, SUB), :] = zero
        ref[pl.ds(ref.shape[0] - SUB, SUB), :] = zero


def sweep(fields, rows):
    def two_steps(_, carry):
        for x, y, coeff, levels in fields:
            step_rows(x, y, coeff, rows, levels)
        for x, y, coeff, levels in fields:
            step_rows(y, x, coeff, rows, levels)
        return carry

    lax.fori_loop(0, STEPS // 2, two_steps, 0)


def cell_parts(z, cell):
    level, rest = div_mod(cell, z.rows * z.columns)
    row, column = div_mod(rest, z.columns)
    return level >> 3, level & 7, row, column


def own_index(z, cell):
    group, part, row, column = cell_parts(z, cell)
    return part * z.rows + row, group * 128 + column


def edge_index(z, cell, windows):
    group, part, row, column = cell_parts(z, cell)
    inside, lane = False, 0
    for first, at in windows:
        here = (column >= first) & (column < first + STEPS)
        inside = here | inside
        lane = jnp.where(here, at - first, lane)
    lane = lane + column + 64 * group + 16 * (part >> 1)
    return jnp.where(inside, (part & 1) * z.rows + row, -1), lane & 127


def own_edges(z):
    return (0, 48), (z.columns - STEPS, 8)


def windows_of(z):
    return own_edges(z), ((0, 16),), ((z.columns - STEPS, 40),)


def quarters(unit, first, second):
    even, odd = (first, second) if first % 2 == 0 else (second, first)
    return jnp.where((unit & 1) == 0, ((unit - even) >> 1) & 3, ((unit - odd) >> 1) & 3)


def one_hot(index, size):
    rows = lax.broadcasted_iota(jnp.int32, (size, index.shape[1]), 0)
    return jnp.where(rows == index, 1.0, 0.0).astype(BF16)


def read_off(field, i, j):
    hot = one_hot(i, field.shape[0])
    value = lax.dot_general(field, hot, (((0,), (0,)), ((), ())), preferred_element_type=F32)
    n = value.shape[0] // 2
    value = value[:n] + value[n:]
    rows = lax.broadcasted_iota(jnp.int32, value.shape, 0)
    return jnp.sum(jnp.where(rows == j, value, 0.0), axis=0, keepdims=True)


def gather(z, out, at, field, cell, index):
    for n in range(z.obs_rows // 2):
        row = jnp.concatenate([cell[2 * n : 2 * n + 1, :], cell[2 * n + 1 : 2 * n + 2, :]], axis=1)
        value = read_off(field, *index(row))
        out[at + 2 * n : at + 2 * n + 1, :] = value[:, :128]
        out[at + 2 * n + 1 : at + 2 * n + 2, :] = value[:, 128:]


def main_kernel(z, alpha, members, weight, kappa, scale, ocean, cell, out, coeff, x, y, both):
    put_coefficients(coeff, coefficients(kappa[...], scale[...], ocean[...].astype(F32), True))
    clear_ends(x, y)
    x[pl.ds(SUB, z.field), :] = alpha[...]
    sweep([(x, y, coeff, z.levels)], z.rows)
    lane = lanes(z.group)
    inner = (lane >= STEPS) & (lane < z.columns - STEPS)
    for g in range(2):
        rows = pl.ds(g * z.group, z.group)
        value = x[pl.ds(SUB + g * z.group, z.group), :] * (members[rows, :].astype(F32) * weight[0])
        high, low = split(jnp.where(inner, value, 0.0))
        both[:, pl.ds(g * 128, 128)] = high
        both[:, pl.ds(256 + g * 128, 128)] = low
    gather(z, out, 0, both[...], cell[...], lambda c: own_index(z, c))


def strip_kernel(
    z, inner, sent_a, sent_b, got_a, got_b, cell, weight, out, strip_members, strip_coeff, coeff, x, y, outer, beside
):
    even = lax.rem(lax.axis_index("tile"), 2) == 0

    def parts(rows):
        sa, sb, ga, gb = sent_a[rows, :], sent_b[rows, :], got_a[rows, :], got_b[rows, :]
        pick = lambda p, q: jnp.where(even, p, q)
        return pick(sa, sb), pick(ga, gb), pick(gb, ga), pick(sb, sa)

    clear_ends(x, y)
    lane = lanes(SUB)
    for q in range(z.half // SUB):
        four = parts(pl.ds(q * SUB, SUB))
        for h in range(2):
            at = h * z.half + q * SUB
            for offset in (0, -EDGE):
                pieces = [roll(part, EDGE * p - 32 * h + offset) for p, part in enumerate(four)]
                value = overlay(pieces, (lane >> 4) & 3)
                if offset:
                    x[pl.ds(SUB + at, SUB), :] = value
                else:
                    strip_members[pl.ds(at, SUB), :] = value * weight[0]
    half = z.rows // 2
    four = parts(pl.ds(z.at_coeff, half))
    lane = lanes(half)
    for k in range(3):
        for h in range(2):
            pieces = [roll(four[p], EDGE * p + 64 * g - 64 * h - EDGE * k) for g in range(2) for p in range(4)]
            strip_coeff[k, pl.ds(h * half, half), :] = overlay(pieces, lane >> 4)
    put_coefficients(coeff, coefficients(strip_coeff[0], strip_coeff[1], strip_coeff[2], True))
    sweep([(x, y, coeff, z.levels // 2)], z.rows)
    unit = lanes(z.short) >> 3
    for ref, first, second in ((outer, 1, 6), (beside, 2, 5)):
        quarter = quarters(unit, first, second)
        pieces = []
        for k in range(4):
            rows = pl.ds(k * z.short, z.short)
            pieces.append(roll(x[pl.ds(SUB + k * z.short, z.short), :] * strip_members[rows, :], 16 * k))
        high, low = split(overlay(pieces, quarter))
        ref[:, :128] = high
        ref[:, 128:] = low
    _, right, left, _ = parts(pl.ds(z.at_obs, z.obs_rows))
    n = z.obs_rows
    for k, (field, cells) in enumerate(
        ((outer, cell[...]), (beside, right.astype(jnp.int32)), (beside, left.astype(jnp.int32)))
    ):
        gather(z, out, k * n, field[...], cells, lambda c: edge_index(z, c, windows_of(z)[k]))
    out[:n, :] = out[:n, :] + inner[...]


def adjoint_kernel(
    z, alpha, members, weight, kappa, scale, ocean, cell, obs_weight, got_a, got_b, strip_members, strip_coeff,
    v0, v1, v2, v3, out, x, y, coeff, strip, spare, strip_c, beside, hot, spread,
):
    even = lax.rem(lax.axis_index("tile"), 2) == 0
    clear_ends(x, y, strip, spare)
    put_coefficients(coeff, coefficients(kappa[...], scale[...], ocean[...].astype(F32), False))
    put_coefficients(strip_c, coefficients(strip_coeff[0], strip_coeff[1], strip_coeff[2], False))
    value = (v0[...] + v1[...]) + (v2[...] + v3[...])
    n = z.obs_rows
    pick = lambda p, q: jnp.where(even, p, q)
    cells, weights = pl.ds(z.at_obs, n), pl.ds(z.at_obs + n, n)
    right = pick(got_a[cells, :], got_b[cells, :]).astype(jnp.int32)
    left = pick(got_b[cells, :], got_a[cells, :]).astype(jnp.int32)
    right_weight = pick(got_a[weights, :], got_b[weights, :])
    left_weight = pick(got_b[weights, :], got_a[weights, :])

    def spread_out(groups, tall, wide):
        at = 0
        for index, amount, place in groups:
            for r in range(n):
                i, j = place(index[r : r + 1, :])
                hot[:tall, pl.ds(at * 128, 128)] = one_hot(i, tall)
                rows = lax.broadcasted_iota(jnp.int32, (wide, 128), 0)
                high, low = split(jnp.where(rows == j, amount[r : r + 1, :], 0.0))
                spread[:wide, pl.ds(at * 128, 128)] = high
                spread[pl.ds(wide, wide), pl.ds(at * 128, 128)] = low
                at += 1
        dims = (((1,), (1,)), ((), ()))
        total = lax.dot_general(
            hot[:tall, : at * 128], spread[: 2 * wide, : at * 128], dims, preferred_element_type=F32
        )
        return total[:, :wide] + total[:, wide:]

    field = spread_out([(cell[...], obs_weight[...] * value[:n], lambda c: own_index(z, c))], z.group, 256)
    for g in range(2):
        x[pl.ds(SUB + g * z.group, z.group), :] = field[:, g * 128 : (g + 1) * 128]
    _, right_window, left_window = windows_of(z)
    beside[...] = spread_out(
        [
            (right, right_weight * value[n : 2 * n], lambda c: edge_index(z, c, right_window)),
            (left, left_weight * value[2 * n :], lambda c: edge_index(z, c, left_window)),
        ],
        z.short,
        128,
    )
    lane = lanes(SUB)
    part = (lane >> 4) & 3
    within = lane & 15
    outside = ((part == 1) & (within < STEPS)) | ((part == 2) & (within >= STEPS))
    for q in range(z.group // SUB):
        k, rest = divmod(q * SUB, z.short)
        value = jnp.where(outside, roll(beside[pl.ds(rest, SUB), :], -16 * k), 0.0)
        for g in range(2):
            at = g * z.group + q * SUB
            here = pl.ds(SUB + at, SUB)
            field = x[here, :]
            mine = (lane >> 6) == g
            value = jnp.where(mine & (part == 0), roll(field, EDGE + 64 * g), value)
            value = jnp.where(mine & (part == 3), roll(field, 48 + 64 * g), value)
        strip[pl.ds(SUB + q * SUB, SUB), :] = value * strip_members[pl.ds(q * SUB, SUB), :]
    here = pl.ds(SUB, z.field)
    x[here, :] = x[here, :] * (members[...].astype(F32) * weight[0])
    sweep([(x, y, coeff, z.levels), (strip, spare, strip_c, z.levels // 2)], z.rows)
    for q in range(z.group // SUB):
        value = strip[pl.ds(SUB + q * SUB, SUB), :]
        for g in range(2):
            at = g * z.group + q * SUB
            fixed = x[pl.ds(SUB + at, SUB), :]
            fixed = jnp.where(lane >= z.columns - STEPS, roll(value, 112 - 64 * g), fixed)
            fixed = jnp.where(lane < STEPS, roll(value, -48 - 64 * g), fixed)
            out[pl.ds(at, SUB), :] = alpha[pl.ds(at, SUB), :] + fixed


def local(alpha, members, mem_weight, kappa, norm_scale, land_sea, obs_cell, obs_weight):
    shape = alpha.shape
    z = Sizes(shape[1], shape[2], shape[3], obs_cell.shape[0])
    tiles, holders = lax.axis_size("tile"), lax.axis_size("mem")
    assert tiles % 2 == 0 and holders == 4 and shape[0] == 1
    alpha = alpha.reshape(z.field, z.columns)
    members = members.reshape(z.field, z.columns)
    cell = obs_cell.reshape(z.obs_rows, 128)
    weight = obs_weight.reshape(z.obs_rows, 128)
    smem = pl.BlockSpec(memory_space=pltpu.SMEM)
    whole = pl.BlockSpec(memory_space=pltpu.VMEM)
    sds = jax.ShapeDtypeStruct
    main_field = pltpu.VMEM((z.field + 2 * SUB, 128), F32)
    strip_field = pltpu.VMEM((z.group + 2 * SUB, 128), F32)
    coeff = pltpu.VMEM((5, z.rows, 128), F32)
    payload = sds((z.payload, 128), F32)
    sent_a, sent_b = pl.pallas_call(
        functools.partial(pack_kernel, z),
        out_shape=(payload, payload),
        name="pack",
    )(alpha, members, kappa, norm_scale, land_sea, cell, weight)
    near = [(i, i ^ 1) for i in range(tiles)]
    far = [(i, (i + 1) % tiles if i % 2 else (i - 1) % tiles) for i in range(tiles)]
    got_b = lax.ppermute(sent_b, "tile", far)
    got_a = lax.ppermute(sent_a, "tile", near)
    inner = pl.pallas_call(
        functools.partial(main_kernel, z),
        out_shape=sds((z.obs_rows, 128), F32),
        in_specs=[whole, whole, smem, whole, whole, whole, whole],
        scratch_shapes=[coeff, main_field, main_field, pltpu.VMEM((z.group, 512), BF16)],
        name="main",
    )(alpha, members, mem_weight, kappa, norm_scale, land_sea, cell)
    packed = pltpu.VMEM((z.short, 256), BF16)
    values, strip_members, strip_coeff = pl.pallas_call(
        functools.partial(strip_kernel, z),
        out_shape=(sds((3 * z.obs_rows, 128), F32), sds((z.group, 128), F32), sds((3, z.rows, 128), F32)),
        in_specs=[whole] * 6 + [smem],
        scratch_shapes=[coeff, strip_field, strip_field, packed, packed],
        name="strip",
    )(inner, sent_a, sent_b, got_a, got_b, cell, mem_weight)
    others = [lax.ppermute(values, "mem", [(i, i ^ k) for i in range(holders)]) for k in range(1, holders)]
    product = pl.pallas_call(
        functools.partial(adjoint_kernel, z),
        out_shape=sds((z.field, z.columns), F32),
        in_specs=[whole, whole, smem] + [whole] * 13,
        scratch_shapes=[
            main_field,
            main_field,
            coeff,
            strip_field,
            strip_field,
            coeff,
            pltpu.VMEM((z.short, 128), F32),
            pltpu.VMEM((z.group, 2 * z.obs), BF16),
            pltpu.VMEM((512, 2 * z.obs), BF16),
        ],
        name="adjoint",
    )(
        alpha, members, mem_weight, kappa, norm_scale, land_sea, cell, weight,
        got_a, got_b, strip_members, strip_coeff, values, *others,
    )
    return product.reshape(shape)


def solution(mesh):
    placed = (
        P("mem", None, None, "tile"),
        P("mem", None, None, "tile"),
        P("mem"),
        P(None, "tile"),
        P(None, "tile"),
        P(None, "tile"),
        P("tile"),
        P("tile"),
    )
    return jax.shard_map(
        local, mesh=mesh, in_specs=placed, out_specs=P("mem", None, None, "tile"), check_vma=False
    )
```

```python
import functools

import jax
import jax.numpy as jnp
from jax import lax
from jax.experimental import pallas as pl
from jax.experimental.pallas import tpu as pltpu
from jax.sharding import PartitionSpec as P

STEPS = 8
SUB = 8
EDGE = 2 * STEPS
F32 = jnp.float32
BF16 = jnp.bfloat16


def div_mod(value, size):
    if size & (size - 1) == 0:
        return value >> (size.bit_length() - 1), value & (size - 1)
    return lax.div(value, size), lax.rem(value, size)


def roll(value, shift, axis=1):
    shift %= value.shape[axis]
    return pltpu.roll(value, shift, axis) if shift else value


def lanes(rows):
    return lax.broadcasted_iota(jnp.int32, (rows, 128), 1)


def split(value):
    high = value.astype(BF16)
    return high, (value - high.astype(F32)).astype(BF16)


class Sizes:
    def __init__(self, levels, rows, columns, obs):
        self.levels, self.rows, self.columns, self.obs = levels, rows, columns, obs
        assert columns == 128 and levels == 16 and rows % 16 == 0 and obs % 256 == 0 and STEPS == 8
        self.field = levels * rows
        self.group = self.field // 2
        self.half = self.field // 4
        self.short = self.field // 8
        self.at_coeff = self.half
        self.at_obs = self.at_coeff + rows // 2
        self.obs_rows = obs // 128
        self.payload = self.at_obs + 2 * self.obs_rows


def overlay(pieces, window):
    value = pieces[0]
    for k in range(1, len(pieces)):
        value = jnp.where(window == k, pieces[k], value)
    return value


def pack_kernel(z, alpha, members, kappa, scale, ocean, cell, weight, out_a, out_b):
    even = lax.rem(lax.axis_index("tile"), 2) == 0

    def put(where, right, left):
        out_a[where, :] = jnp.where(even, right, left)
        out_b[where, :] = jnp.where(even, left, right)

    block = 4 * SUB
    lane = lanes(block)
    for q in range(z.half // block):
        right, left = [], []
        for g in range(2):
            for h in range(2):
                rows = pl.ds(g * z.group + h * z.half + q * block, block)
                a, m = alpha[rows, :], members[rows, :].astype(F32)
                base = 64 * g + 32 * h
                right += [roll(m, base + EDGE), roll(a, base + 2 * EDGE)]
                left += [roll(m, base), roll(a, base + EDGE)]
        put(pl.ds(q * block, block), overlay(right, lane >> 4), overlay(left, lane >> 4))
    half = z.rows // 2
    lane = lanes(half)
    right, left = [], []
    for h in range(2):
        rows = pl.ds(h * half, half)
        for k, ref in enumerate((kappa, scale, ocean)):
            value = ref[rows, :].astype(F32)
            base = 64 * h + EDGE * k
            right.append(roll(value, base - (128 - EDGE)))
            left.append(roll(value, base))
        right.append(right[-1])
        left.append(left[-1])
    put(pl.ds(z.at_coeff, half), overlay(right, lane >> 4), overlay(left, lane >> 4))
    n = z.obs_rows
    for at, value in ((z.at_obs, cell[...].astype(F32)), (z.at_obs + n, weight[...])):
        out_a[pl.ds(at, n), :] = value
        out_b[pl.ds(at, n), :] = value


def up(value):
    return roll(value, -1, 0)


def down(value):
    return roll(value, 1, 0)


def coefficients(kappa, scale, ocean, forward):
    row = lax.broadcasted_iota(jnp.int32, kappa.shape, 0)
    north = 0.5 * (kappa + up(kappa)) * ocean * up(ocean)
    north = jnp.where(row == kappa.shape[0] - 1, 0.0, north)
    east = 0.5 * (kappa + roll(kappa, -1)) * ocean * roll(ocean, -1)
    west, south = roll(east, 1), down(north)
    centre = 1.0 - (east + west) - (north + south)
    if forward:
        return (
            centre * scale,
            east * roll(scale, -1),
            west * roll(scale, 1),
            north * up(scale),
            south * down(scale),
        )
    return tuple(scale * c for c in (centre, east, west, north, south))


def put_coefficients(ref, values):
    for k, value in enumerate(values):
        ref[k] = value


def step_rows(source, target, coeff, rows, levels):
    for t in range(rows // SUB):
        c = [coeff[k, pl.ds(t * SUB, SUB), :] for k in range(5)]
        for level in range(levels):
            at = SUB + level * rows + t * SUB
            u = source[pl.ds(at, SUB), :]
            along = c[3] * source[pl.ds(at + 1, SUB), :] + c[4] * source[pl.ds(at - 1, SUB), :]
            across = c[1] * roll(u, -1) + c[2] * roll(u, 1)
            target[pl.ds(at, SUB), :] = c[0] * u + across + along


def clear_ends(*buffers):
    for ref in buffers:
        zero = jnp.zeros((SUB, 128), F32)
        ref[pl.ds(0, SUB), :] = zero
        ref[pl.ds(ref.shape[0] - SUB, SUB), :] = zero


def sweep(fields, rows):
    def two_steps(_, carry):
        for x, y, coeff, levels in fields:
            step_rows(x, y, coeff, rows, levels)
        for x, y, coeff, levels in fields:
            step_rows(y, x, coeff, rows, levels)
        return carry

    lax.fori_loop(0, STEPS // 2, two_steps, 0)


def cell_parts(z, cell):
    level, rest = div_mod(cell, z.rows * z.columns)
    row, column = div_mod(rest, z.columns)
    return level >> 3, level & 7, row, column


def own_index(z, cell):
    group, part, row, column = cell_parts(z, cell)
    return part * z.rows + row, group * 128 + column


def edge_index(z, cell, windows):
    group, part, row, column = cell_parts(z, cell)
    inside, lane = False, 0
    for first, at in windows:
        here = (column >= first) & (column < first + STEPS)
        inside = here | inside
        lane = jnp.where(here, at - first, lane)
    lane = lane + column + 64 * group + 16 * (part >> 1)
    return jnp.where(inside, (part & 1) * z.rows + row, -1), lane & 127


def own_edges(z):
    return (0, 48), (z.columns - STEPS, 8)


def windows_of(z):
    return own_edges(z), ((0, 16),), ((z.columns - STEPS, 40),)


def quarters(unit, first, second):
    even, odd = (first, second) if first % 2 == 0 else (second, first)
    return jnp.where((unit & 1) == 0, ((unit - even) >> 1) & 3, ((unit - odd) >> 1) & 3)


def one_hot(index, size):
    rows = lax.broadcasted_iota(jnp.int32, (size, index.shape[1]), 0)
    return jnp.where(rows == index, 1.0, 0.0).astype(BF16)


def read_off(field, i, j):
    hot = one_hot(i, field.shape[0])
    value = lax.dot_general(field, hot, (((0,), (0,)), ((), ())), preferred_element_type=F32)
    n = value.shape[0] // 2
    value = value[:n] + value[n:]
    rows = lax.broadcasted_iota(jnp.int32, value.shape, 0)
    return jnp.sum(jnp.where(rows == j, value, 0.0), axis=0, keepdims=True)


def gather(z, out, at, field, cell, index):
    for n in range(z.obs_rows // 2):
        row = jnp.concatenate([cell[2 * n : 2 * n + 1, :], cell[2 * n + 1 : 2 * n + 2, :]], axis=1)
        value = read_off(field, *index(row))
        out[at + 2 * n : at + 2 * n + 1, :] = value[:, :128]
        out[at + 2 * n + 1 : at + 2 * n + 2, :] = value[:, 128:]


def main_kernel(z, alpha, members, weight, kappa, scale, ocean, cell, out, coeff, x, y, both):
    put_coefficients(coeff, coefficients(kappa[...], scale[...], ocean[...].astype(F32), True))
    clear_ends(x, y)
    x[pl.ds(SUB, z.field), :] = alpha[...]
    sweep([(x, y, coeff, z.levels)], z.rows)
    lane = lanes(z.group)
    inner = (lane >= STEPS) & (lane < z.columns - STEPS)
    for g in range(2):
        rows = pl.ds(g * z.group, z.group)
        value = x[pl.ds(SUB + g * z.group, z.group), :] * (members[rows, :].astype(F32) * weight[0])
        high, low = split(jnp.where(inner, value, 0.0))
        both[:, pl.ds(g * 128, 128)] = high
        both[:, pl.ds(256 + g * 128, 128)] = low
    gather(z, out, 0, both[...], cell[...], lambda c: own_index(z, c))


def strip_kernel(
    z, inner, sent_a, sent_b, got_a, got_b, cell, weight, out, strip_members, strip_coeff, coeff, x, y, outer, beside
):
    even = lax.rem(lax.axis_index("tile"), 2) == 0

    def parts(rows):
        sa, sb, ga, gb = sent_a[rows, :], sent_b[rows, :], got_a[rows, :], got_b[rows, :]
        pick = lambda p, q: jnp.where(even, p, q)
        return pick(sa, sb), pick(ga, gb), pick(gb, ga), pick(sb, sa)

    clear_ends(x, y)
    lane = lanes(SUB)
    for q in range(z.half // SUB):
        four = parts(pl.ds(q * SUB, SUB))
        for h in range(2):
            at = h * z.half + q * SUB
            for offset in (0, -EDGE):
                pieces = [roll(part, EDGE * p - 32 * h + offset) for p, part in enumerate(four)]
                value = overlay(pieces, (lane >> 4) & 3)
                if offset:
                    x[pl.ds(SUB + at, SUB), :] = value
                else:
                    strip_members[pl.ds(at, SUB), :] = value * weight[0]
    half = z.rows // 2
    four = parts(pl.ds(z.at_coeff, half))
    lane = lanes(half)
    for k in range(3):
        for h in range(2):
            pieces = [roll(four[p], EDGE * p + 64 * g - 64 * h - EDGE * k) for g in range(2) for p in range(4)]
            strip_coeff[k, pl.ds(h * half, half), :] = overlay(pieces, lane >> 4)
    put_coefficients(coeff, coefficients(strip_coeff[0], strip_coeff[1], strip_coeff[2], True))
    sweep([(x, y, coeff, z.levels // 2)], z.rows)
    unit = lanes(z.short) >> 3
    for ref, first, second in ((outer, 1, 6), (beside, 2, 5)):
        quarter = quarters(unit, first, second)
        pieces = []
        for k in range(4):
            rows = pl.ds(k * z.short, z.short)
            pieces.append(roll(x[pl.ds(SUB + k * z.short, z.short), :] * strip_members[rows, :], 16 * k))
        high, low = split(overlay(pieces, quarter))
        ref[:, :128] = high
        ref[:, 128:] = low
    _, right, left, _ = parts(pl.ds(z.at_obs, z.obs_rows))
    n = z.obs_rows
    for k, (field, cells) in enumerate(
        ((outer, cell[...]), (beside, right.astype(jnp.int32)), (beside, left.astype(jnp.int32)))
    ):
        gather(z, out, k * n, field[...], cells, lambda c: edge_index(z, c, windows_of(z)[k]))
    out[:n, :] = out[:n, :] + inner[...]


def adjoint_kernel(
    z, alpha, members, weight, kappa, scale, ocean, cell, obs_weight, got_a, got_b, strip_members, strip_coeff,
    v0, v1, v2, v3, out, x, y, coeff, strip, spare, strip_c, beside, hot, spread,
):
    even = lax.rem(lax.axis_index("tile"), 2) == 0
    clear_ends(x, y, strip, spare)
    put_coefficients(coeff, coefficients(kappa[...], scale[...], ocean[...].astype(F32), False))
    put_coefficients(strip_c, coefficients(strip_coeff[0], strip_coeff[1], strip_coeff[2], False))
    value = (v0[...] + v1[...]) + (v2[...] + v3[...])
    n = z.obs_rows
    pick = lambda p, q: jnp.where(even, p, q)
    cells, weights = pl.ds(z.at_obs, n), pl.ds(z.at_obs + n, n)
    right = pick(got_a[cells, :], got_b[cells, :]).astype(jnp.int32)
    left = pick(got_b[cells, :], got_a[cells, :]).astype(jnp.int32)
    right_weight = pick(got_a[weights, :], got_b[weights, :])
    left_weight = pick(got_b[weights, :], got_a[weights, :])

    def spread_out(groups, tall, wide):
        at = 0
        for index, amount, place in groups:
            for r in range(n):
                i, j = place(index[r : r + 1, :])
                hot[:tall, pl.ds(at * 128, 128)] = one_hot(i, tall)
                rows = lax.broadcasted_iota(jnp.int32, (wide, 128), 0)
                high, low = split(jnp.where(rows == j, amount[r : r + 1, :], 0.0))
                spread[:wide, pl.ds(at * 128, 128)] = high
                spread[pl.ds(wide, wide), pl.ds(at * 128, 128)] = low
                at += 1
        dims = (((1,), (1,)), ((), ()))
        total = lax.dot_general(
            hot[:tall, : at * 128], spread[: 2 * wide, : at * 128], dims, preferred_element_type=F32
        )
        return total[:, :wide] + total[:, wide:]

    field = spread_out([(cell[...], obs_weight[...] * value[:n], lambda c: own_index(z, c))], z.group, 256)
    for g in range(2):
        x[pl.ds(SUB + g * z.group, z.group), :] = field[:, g * 128 : (g + 1) * 128]
    _, right_window, left_window = windows_of(z)
    beside[...] = spread_out(
        [
            (right, right_weight * value[n : 2 * n], lambda c: edge_index(z, c, right_window)),
            (left, left_weight * value[2 * n :], lambda c: edge_index(z, c, left_window)),
        ],
        z.short,
        128,
    )
    lane = lanes(SUB)
    part = (lane >> 4) & 3
    within = lane & 15
    outside = ((part == 1) & (within < STEPS)) | ((part == 2) & (within >= STEPS))
    for q in range(z.group // SUB):
        k, rest = divmod(q * SUB, z.short)
        value = jnp.where(outside, roll(beside[pl.ds(rest, SUB), :], -16 * k), 0.0)
        for g in range(2):
            at = g * z.group + q * SUB
            here = pl.ds(SUB + at, SUB)
            field = x[here, :]
            mine = (lane >> 6) == g
            value = jnp.where(mine & (part == 0), roll(field, EDGE + 64 * g), value)
            value = jnp.where(mine & (part == 3), roll(field, 48 + 64 * g), value)
        strip[pl.ds(SUB + q * SUB, SUB), :] = value * strip_members[pl.ds(q * SUB, SUB), :]
    here = pl.ds(SUB, z.field)
    x[here, :] = x[here, :] * (members[...].astype(F32) * weight[0])
    sweep([(x, y, coeff, z.levels), (strip, spare, strip_c, z.levels // 2)], z.rows)
    for q in range(z.group // SUB):
        value = strip[pl.ds(SUB + q * SUB, SUB), :]
        for g in range(2):
            at = g * z.group + q * SUB
            fixed = x[pl.ds(SUB + at, SUB), :]
            fixed = jnp.where(lane >= z.columns - STEPS, roll(value, 112 - 64 * g), fixed)
            fixed = jnp.where(lane < STEPS, roll(value, -48 - 64 * g), fixed)
            out[pl.ds(at, SUB), :] = alpha[pl.ds(at, SUB), :] + fixed


def local(alpha, members, mem_weight, kappa, norm_scale, land_sea, obs_cell, obs_weight):
    shape = alpha.shape
    z = Sizes(shape[1], shape[2], shape[3], obs_cell.shape[0])
    tiles, holders = lax.axis_size("tile"), lax.axis_size("mem")
    assert tiles % 2 == 0 and holders == 4 and shape[0] == 1
    alpha = alpha.reshape(z.field, z.columns)
    members = members.reshape(z.field, z.columns)
    cell = obs_cell.reshape(z.obs_rows, 128)
    weight = obs_weight.reshape(z.obs_rows, 128)
    smem = pl.BlockSpec(memory_space=pltpu.SMEM)
    whole = pl.BlockSpec(memory_space=pltpu.VMEM)
    sds = jax.ShapeDtypeStruct
    main_field = pltpu.VMEM((z.field + 2 * SUB, 128), F32)
    strip_field = pltpu.VMEM((z.group + 2 * SUB, 128), F32)
    coeff = pltpu.VMEM((5, z.rows, 128), F32)
    payload = sds((z.payload, 128), F32)
    sent_a, sent_b = pl.pallas_call(
        functools.partial(pack_kernel, z),
        out_shape=(payload, payload),
        name="pack",
    )(alpha, members, kappa, norm_scale, land_sea, cell, weight)
    near = [(i, i ^ 1) for i in range(tiles)]
    far = [(i, (i + 1) % tiles if i % 2 else (i - 1) % tiles) for i in range(tiles)]
    got_b = lax.ppermute(sent_b, "tile", far)
    got_a = lax.ppermute(sent_a, "tile", near)
    inner = pl.pallas_call(
        functools.partial(main_kernel, z),
        out_shape=sds((z.obs_rows, 128), F32),
        in_specs=[whole, whole, smem, whole, whole, whole, whole],
        scratch_shapes=[coeff, main_field, main_field, pltpu.VMEM((z.group, 512), BF16)],
        name="main",
    )(alpha, members, mem_weight, kappa, norm_scale, land_sea, cell)
    packed = pltpu.VMEM((z.short, 256), BF16)
    values, strip_members, strip_coeff = pl.pallas_call(
        functools.partial(strip_kernel, z),
        out_shape=(sds((3 * z.obs_rows, 128), F32), sds((z.group, 128), F32), sds((3, z.rows, 128), F32)),
        in_specs=[whole] * 6 + [smem],
        scratch_shapes=[coeff, strip_field, strip_field, packed, packed],
        name="strip",
    )(inner, sent_a, sent_b, got_a, got_b, cell, mem_weight)
    others = [lax.ppermute(values, "mem", [(i, i ^ k) for i in range(holders)]) for k in range(1, holders)]
    product = pl.pallas_call(
        functools.partial(adjoint_kernel, z),
        out_shape=sds((z.field, z.columns), F32),
        in_specs=[whole, whole, smem] + [whole] * 13,
        scratch_shapes=[
            main_field,
            main_field,
            coeff,
            strip_field,
            strip_field,
            coeff,
            pltpu.VMEM((z.short, 128), F32),
            pltpu.VMEM((z.group, 2 * z.obs), BF16),
            pltpu.VMEM((512, 2 * z.obs), BF16),
        ],
        name="adjoint",
    )(
        alpha, members, mem_weight, kappa, norm_scale, land_sea, cell, weight,
        got_a, got_b, strip_members, strip_coeff, values, *others,
    )
    return product.reshape(shape)


def solution(mesh):
    placed = (
        P("mem", None, None, "tile"),
        P("mem", None, None, "tile"),
        P("mem"),
        P(None, "tile"),
        P(None, "tile"),
        P(None, "tile"),
        P("tile"),
        P("tile"),
    )
    return jax.shard_map(
        local, mesh=mesh, in_specs=placed, out_specs=P("mem", None, None, "tile"), check_vma=False
    )
```

```python
import functools

import jax
import jax.numpy as jnp
from jax import lax
from jax.experimental import pallas as pl
from jax.experimental.pallas import tpu as pltpu
from jax.sharding import PartitionSpec as P

STEPS = 8
SUB = 8
EDGE = 2 * STEPS
F32 = jnp.float32
BF16 = jnp.bfloat16


def div_mod(value, size):
    if size & (size - 1) == 0:
        return value >> (size.bit_length() - 1), value & (size - 1)
    return lax.div(value, size), lax.rem(value, size)


def roll(value, shift, axis=1):
    shift %= value.shape[axis]
    return pltpu.roll(value, shift, axis) if shift else value


def lanes(rows):
    return lax.broadcasted_iota(jnp.int32, (rows, 128), 1)


def split(value):
    high = value.astype(BF16)
    return high, (value - high.astype(F32)).astype(BF16)


class Sizes:
    def __init__(self, levels, rows, columns, obs):
        self.levels, self.rows, self.columns, self.obs = levels, rows, columns, obs
        assert columns == 128 and levels == 16 and rows % 16 == 0 and obs % 256 == 0 and STEPS == 8
        self.field = levels * rows
        self.group = self.field // 2
        self.half = self.field // 4
        self.short = self.field // 8
        self.at_coeff = self.half
        self.at_obs = self.at_coeff + rows // 2
        self.obs_rows = obs // 128
        self.payload = self.at_obs + 2 * self.obs_rows


def overlay(pieces, window):
    value = pieces[0]
    for k in range(1, len(pieces)):
        value = jnp.where(window == k, pieces[k], value)
    return value


def early(tiles):
    tile = lax.axis_index("tile")
    return (tile == 0) | ((lax.rem(tile, 2) == 1) & (tile != tiles - 1))


def pack_kernel(z, tiles, alpha, members, kappa, scale, ocean, cell, weight, out_a, out_b, x, coeff, y):
    even = lax.rem(lax.axis_index("tile"), 2) == 0

    def put(where, right, left):
        out_a[where, :] = jnp.where(even, right, left)
        out_b[where, :] = jnp.where(even, left, right)

    block = 4 * SUB
    lane = lanes(block)
    for q in range(z.half // block):
        right, left = [], []
        for g in range(2):
            for h in range(2):
                rows = pl.ds(g * z.group + h * z.half + q * block, block)
                a, m = alpha[rows, :], members[rows, :].astype(F32)
                base = 64 * g + 32 * h
                right += [roll(m, base + EDGE), roll(a, base + 2 * EDGE)]
                left += [roll(m, base), roll(a, base + EDGE)]
        put(pl.ds(q * block, block), overlay(right, lane >> 4), overlay(left, lane >> 4))
    half = z.rows // 2
    lane = lanes(half)
    right, left = [], []
    for h in range(2):
        rows = pl.ds(h * half, half)
        for k, ref in enumerate((kappa, scale, ocean)):
            value = ref[rows, :].astype(F32)
            base = 64 * h + EDGE * k
            right.append(roll(value, base - (128 - EDGE)))
            left.append(roll(value, base))
        right.append(right[-1])
        left.append(left[-1])
    put(pl.ds(z.at_coeff, half), overlay(right, lane >> 4), overlay(left, lane >> 4))
    n = z.obs_rows
    for at, value in ((z.at_obs, cell[...].astype(F32)), (z.at_obs + n, weight[...])):
        out_a[pl.ds(at, n), :] = value
        out_b[pl.ds(at, n), :] = value

    @pl.when(early(tiles))
    def _():
        forward_sweep(z, alpha, kappa, scale, ocean, coeff, x, y)


def up(value):
    return roll(value, -1, 0)


def down(value):
    return roll(value, 1, 0)


def coefficients(kappa, scale, ocean, forward):
    row = lax.broadcasted_iota(jnp.int32, kappa.shape, 0)
    north = 0.5 * (kappa + up(kappa)) * ocean * up(ocean)
    north = jnp.where(row == kappa.shape[0] - 1, 0.0, north)
    east = 0.5 * (kappa + roll(kappa, -1)) * ocean * roll(ocean, -1)
    west, south = roll(east, 1), down(north)
    centre = 1.0 - (east + west) - (north + south)
    if forward:
        return (
            centre * scale,
            east * roll(scale, -1),
            west * roll(scale, 1),
            north * up(scale),
            south * down(scale),
        )
    return tuple(scale * c for c in (centre, east, west, north, south))


def put_coefficients(ref, values):
    for k, value in enumerate(values):
        ref[k] = value


def step_rows(source, target, coeff, rows, levels):
    for t in range(rows // SUB):
        c = [coeff[k, pl.ds(t * SUB, SUB), :] for k in range(5)]
        for level in range(levels):
            at = SUB + level * rows + t * SUB
            u = source[pl.ds(at, SUB), :]
            along = c[3] * source[pl.ds(at + 1, SUB), :] + c[4] * source[pl.ds(at - 1, SUB), :]
            across = c[1] * roll(u, -1) + c[2] * roll(u, 1)
            target[pl.ds(at, SUB), :] = c[0] * u + across + along


def clear_ends(*buffers):
    for ref in buffers:
        zero = jnp.zeros((SUB, 128), F32)
        ref[pl.ds(0, SUB), :] = zero
        ref[pl.ds(ref.shape[0] - SUB, SUB), :] = zero


def sweep(fields, rows):
    def two_steps(_, carry):
        for x, y, coeff, levels in fields:
            step_rows(x, y, coeff, rows, levels)
        for x, y, coeff, levels in fields:
            step_rows(y, x, coeff, rows, levels)
        return carry

    lax.fori_loop(0, STEPS // 2, two_steps, 0)


def cell_parts(z, cell):
    level, rest = div_mod(cell, z.rows * z.columns)
    row, column = div_mod(rest, z.columns)
    return level >> 3, level & 7, row, column


def own_index(z, cell):
    group, part, row, column = cell_parts(z, cell)
    return part * z.rows + row, group * 128 + column


def edge_index(z, cell, windows):
    group, part, row, column = cell_parts(z, cell)
    inside, lane = False, 0
    for first, at in windows:
        here = (column >= first) & (column < first + STEPS)
        inside = here | inside
        lane = jnp.where(here, at - first, lane)
    lane = lane + column + 64 * group + 16 * (part >> 1)
    return jnp.where(inside, (part & 1) * z.rows + row, -1), lane & 127


def own_edges(z):
    return (0, 48), (z.columns - STEPS, 8)


def windows_of(z):
    return own_edges(z), ((0, 16),), ((z.columns - STEPS, 40),)


def quarters(unit, first, second):
    even, odd = (first, second) if first % 2 == 0 else (second, first)
    return jnp.where((unit & 1) == 0, ((unit - even) >> 1) & 3, ((unit - odd) >> 1) & 3)


def one_hot(index, size):
    rows = lax.broadcasted_iota(jnp.int32, (size, index.shape[1]), 0)
    return jnp.where(rows == index, 1.0, 0.0).astype(BF16)


def read_off(field, hot, j):
    value = lax.dot_general(field, hot, (((0,), (0,)), ((), ())), preferred_element_type=F32)
    n = value.shape[0] // 2
    value = value[:n] + value[n:]
    rows = lax.broadcasted_iota(jnp.int32, value.shape, 0)
    return jnp.sum(jnp.where(rows == j, value, 0.0), axis=0, keepdims=True)


def gather(z, out, at, field, cell, index, keep=None, start=0):
    for n in range(z.obs_rows // 2):
        row = jnp.concatenate([cell[2 * n : 2 * n + 1, :], cell[2 * n + 1 : 2 * n + 2, :]], axis=1)
        i, j = index(row)
        hot = one_hot(i, field.shape[0])
        if keep is not None:
            keep[:, pl.ds(start + 256 * n, 256)] = hot
        value = read_off(field, hot, j)
        out[at + 2 * n : at + 2 * n + 1, :] = value[:, :128]
        out[at + 2 * n + 1 : at + 2 * n + 2, :] = value[:, 128:]


def forward_sweep(z, alpha, kappa, scale, ocean, coeff, x, y):
    put_coefficients(coeff, coefficients(kappa[...], scale[...], ocean[...].astype(F32), True))
    clear_ends(x, y)
    x[pl.ds(SUB, z.field), :] = alpha[...]
    sweep([(x, y, coeff, z.levels)], z.rows)


def main_kernel(z, tiles, swept, alpha, members, weight, kappa, scale, ocean, cell, out, hot, x, coeff, y, both):
    first = early(tiles)

    @pl.when(first)
    def _():
        x[...] = swept[...]

    @pl.when(jnp.logical_not(first))
    def _():
        forward_sweep(z, alpha, kappa, scale, ocean, coeff, x, y)

    lane = lanes(z.group)
    inner = (lane >= STEPS) & (lane < z.columns - STEPS)
    for g in range(2):
        rows = pl.ds(g * z.group, z.group)
        value = x[pl.ds(SUB + g * z.group, z.group), :] * (members[rows, :].astype(F32) * weight[0])
        high, low = split(jnp.where(inner, value, 0.0))
        both[:, pl.ds(g * 128, 128)] = high
        both[:, pl.ds(256 + g * 128, 128)] = low
    gather(z, out, 0, both[...], cell[...], lambda c: own_index(z, c), hot)


def strip_kernel(
    z, inner, sent_a, sent_b, got_a, got_b, cell, weight, out, strip_members, strip_coeff, hot, coeff, x, y, outer, beside
):
    even = lax.rem(lax.axis_index("tile"), 2) == 0

    def parts(rows):
        sa, sb, ga, gb = sent_a[rows, :], sent_b[rows, :], got_a[rows, :], got_b[rows, :]
        pick = lambda p, q: jnp.where(even, p, q)
        return pick(sa, sb), pick(ga, gb), pick(gb, ga), pick(sb, sa)

    clear_ends(x, y)
    lane = lanes(SUB)
    for q in range(z.half // SUB):
        four = parts(pl.ds(q * SUB, SUB))
        for h in range(2):
            at = h * z.half + q * SUB
            for offset in (0, -EDGE):
                pieces = [roll(part, EDGE * p - 32 * h + offset) for p, part in enumerate(four)]
                value = overlay(pieces, (lane >> 4) & 3)
                if offset:
                    x[pl.ds(SUB + at, SUB), :] = value
                else:
                    strip_members[pl.ds(at, SUB), :] = value * weight[0]
    half = z.rows // 2
    four = parts(pl.ds(z.at_coeff, half))
    lane = lanes(half)
    for k in range(3):
        for h in range(2):
            pieces = [roll(four[p], EDGE * p + 64 * g - 64 * h - EDGE * k) for g in range(2) for p in range(4)]
            strip_coeff[k, pl.ds(h * half, half), :] = overlay(pieces, lane >> 4)
    put_coefficients(coeff, coefficients(strip_coeff[0], strip_coeff[1], strip_coeff[2], True))
    sweep([(x, y, coeff, z.levels // 2)], z.rows)
    unit = lanes(z.short) >> 3
    for ref, first, second in ((outer, 1, 6), (beside, 2, 5)):
        quarter = quarters(unit, first, second)
        pieces = []
        for k in range(4):
            rows = pl.ds(k * z.short, z.short)
            pieces.append(roll(x[pl.ds(SUB + k * z.short, z.short), :] * strip_members[rows, :], 16 * k))
        high, low = split(overlay(pieces, quarter))
        ref[:, :128] = high
        ref[:, 128:] = low
    _, right, left, _ = parts(pl.ds(z.at_obs, z.obs_rows))
    n = z.obs_rows
    for k, (field, cells) in enumerate(
        ((outer, cell[...]), (beside, right.astype(jnp.int32)), (beside, left.astype(jnp.int32)))
    ):
        keep = hot if k else None
        gather(z, out, k * n, field[...], cells, lambda c: edge_index(z, c, windows_of(z)[k]), keep, (k - 1) * z.obs)
    out[:n, :] = out[:n, :] + inner[...]


def beside_rows(z, got_a, got_b, at):
    even = lax.rem(lax.axis_index("tile"), 2) == 0
    a, b = got_a[pl.ds(at, z.obs_rows), :], got_b[pl.ds(at, z.obs_rows), :]
    return jnp.where(even, a, b), jnp.where(even, b, a)


def ready_kernel(z, kappa, scale, ocean, cell, got_a, got_b, strip_coeff, coeff, strip_c, own_lane, beside_lane):
    put_coefficients(coeff, coefficients(kappa[...], scale[...], ocean[...].astype(F32), False))
    put_coefficients(strip_c, coefficients(strip_coeff[0], strip_coeff[1], strip_coeff[2], False))
    _, right_window, left_window = windows_of(z)
    right, left = beside_rows(z, got_a, got_b, z.at_obs)
    n = z.obs_rows
    for r in range(n):
        at = pl.ds(r * 128, 128)
        own_lane[:, at] = one_hot(own_index(z, cell[r : r + 1, :])[1], 256)
        index = right[r : r + 1, :].astype(jnp.int32)
        beside_lane[:, at] = one_hot(edge_index(z, index, right_window)[1], 128)
        index = left[r : r + 1, :].astype(jnp.int32)
        beside_lane[:, pl.ds(z.obs + r * 128, 128)] = one_hot(edge_index(z, index, left_window)[1], 128)


def adjoint_kernel(
    z, alpha_hbm, members_hbm, weight, obs_weight, got_a, got_b, strip_members, coeff, strip_c,
    own_row, own_lane, beside_row, beside_lane, v0, v1, v2, v3,
    out_hbm, x, y, strip, spare, beside, spread, alpha, members, out, sems,
):
    bring_alpha = pltpu.make_async_copy(alpha_hbm, alpha, sems.at[0])
    bring_members = pltpu.make_async_copy(members_hbm, members, sems.at[1])
    bring_members.start()
    bring_alpha.start()
    clear_ends(x, y, strip, spare)
    value = (v0[...] + v1[...]) + (v2[...] + v3[...])
    n = z.obs_rows
    right_weight, left_weight = beside_rows(z, got_a, got_b, z.at_obs + n)

    def spread_out(amounts, row_hot, lane_hot):
        wide = lane_hot.shape[0]
        for group, amount in enumerate(amounts):
            high, low = split(amount)
            for r in range(n):
                at = pl.ds(group * z.obs + r * 128, 128)
                for k, part in enumerate((high, low)):
                    line = jnp.broadcast_to(part[r : r + 1, :].astype(F32), (2 * SUB, 128)).astype(BF16)
                    for t in range(wide // (2 * SUB)):
                        rows = pl.ds(t * 2 * SUB, 2 * SUB)
                        spread[pl.ds(k * wide + t * 2 * SUB, 2 * SUB), at] = lane_hot[rows, at] * line
        dims = (((1,), (1,)), ((), ()))
        total = lax.dot_general(
            row_hot[...], spread[: 2 * wide, : len(amounts) * z.obs], dims, preferred_element_type=F32
        )
        return total[:, :wide] + total[:, wide:]

    field = spread_out([obs_weight[...] * value[:n]], own_row, own_lane)
    for g in range(2):
        x[pl.ds(SUB + g * z.group, z.group), :] = field[:, g * 128 : (g + 1) * 128]
    beside[...] = spread_out(
        [right_weight * value[n : 2 * n], left_weight * value[2 * n :]], beside_row, beside_lane
    )
    lane = lanes(SUB)
    part = (lane >> 4) & 3
    within = lane & 15
    outside = ((part == 1) & (within < STEPS)) | ((part == 2) & (within >= STEPS))
    for q in range(z.group // SUB):
        k, rest = divmod(q * SUB, z.short)
        value = jnp.where(outside, roll(beside[pl.ds(rest, SUB), :], -16 * k), 0.0)
        for g in range(2):
            at = g * z.group + q * SUB
            here = pl.ds(SUB + at, SUB)
            field = x[here, :]
            mine = (lane >> 6) == g
            value = jnp.where(mine & (part == 0), roll(field, EDGE + 64 * g), value)
            value = jnp.where(mine & (part == 3), roll(field, 48 + 64 * g), value)
        strip[pl.ds(SUB + q * SUB, SUB), :] = value * strip_members[pl.ds(q * SUB, SUB), :]
    here = pl.ds(SUB, z.field)
    bring_members.wait()
    x[here, :] = x[here, :] * (members[...].astype(F32) * weight[0])
    sweep([(x, y, coeff, z.levels), (strip, spare, strip_c, z.levels // 2)], z.rows)
    bring_alpha.wait()
    sent = []
    for part in range(z.levels // 2):
        for t in range(z.rows // SUB):
            q = part * z.rows + t * SUB
            value = strip[pl.ds(SUB + q, SUB), :]
            for g in range(2):
                at = g * z.group + q
                fixed = x[pl.ds(SUB + at, SUB), :]
                fixed = jnp.where(lane >= z.columns - STEPS, roll(value, 112 - 64 * g), fixed)
                fixed = jnp.where(lane < STEPS, roll(value, -48 - 64 * g), fixed)
                out[pl.ds(at, SUB), :] = alpha[pl.ds(at, SUB), :] + fixed
        if part % 2:
            for g in range(2):
                rows = pl.ds(g * z.group + (part - 1) * z.rows, 2 * z.rows)
                sent.append(pltpu.make_async_copy(out.at[rows, :], out_hbm.at[rows, :], sems.at[2 + len(sent)]))
                sent[-1].start()
    for copy in sent:
        copy.wait()


def local(alpha, members, mem_weight, kappa, norm_scale, land_sea, obs_cell, obs_weight):
    shape = alpha.shape
    z = Sizes(shape[1], shape[2], shape[3], obs_cell.shape[0])
    tiles, holders = lax.axis_size("tile"), lax.axis_size("mem")
    assert tiles % 2 == 0 and holders == 4 and shape[0] == 1
    alpha = alpha.reshape(z.field, z.columns)
    members = members.reshape(z.field, z.columns)
    cell = obs_cell.reshape(z.obs_rows, 128)
    weight = obs_weight.reshape(z.obs_rows, 128)
    smem = pl.BlockSpec(memory_space=pltpu.SMEM)
    whole = pl.BlockSpec(memory_space=pltpu.VMEM)
    stays = pl.BlockSpec(memory_space=pl.ANY)
    sds = jax.ShapeDtypeStruct
    main_field = pltpu.VMEM((z.field + 2 * SUB, 128), F32)
    strip_field = pltpu.VMEM((z.group + 2 * SUB, 128), F32)
    coeff = pltpu.VMEM((5, z.rows, 128), F32)
    packed = pltpu.VMEM((z.short, 256), BF16)
    payload = sds((z.payload, 128), F32)
    limit = pltpu.CompilerParams(vmem_limit_bytes=24 << 20)
    call = functools.partial(pl.pallas_call, compiler_params=limit)
    sent_a, sent_b, swept = call(
        functools.partial(pack_kernel, z, tiles),
        out_shape=(payload, payload, sds((z.field + 2 * SUB, 128), F32)),
        out_specs=(whole, whole, whole),
        scratch_shapes=[coeff, main_field],
        name="pack",
    )(alpha, members, kappa, norm_scale, land_sea, cell, weight)
    near = [(i, i ^ 1) for i in range(tiles)]
    far = [(i, (i + 1) % tiles if i % 2 else (i - 1) % tiles) for i in range(tiles)]
    got_b = lax.ppermute(sent_b, "tile", far)
    got_a = lax.ppermute(sent_a, "tile", near)
    inner, own_row = call(
        functools.partial(main_kernel, z, tiles),
        out_shape=(sds((z.obs_rows, 128), F32), sds((z.group, z.obs), BF16)),
        in_specs=[whole] * 3 + [smem] + [whole] * 4,
        out_specs=(whole, whole),
        scratch_shapes=[main_field, coeff, main_field, pltpu.VMEM((z.group, 512), BF16)],
        name="main",
    )(swept, alpha, members, mem_weight, kappa, norm_scale, land_sea, cell)
    values, strip_members, strip_coeff, beside_row = call(
        functools.partial(strip_kernel, z),
        out_shape=(
            sds((3 * z.obs_rows, 128), F32),
            sds((z.group, 128), F32),
            sds((3, z.rows, 128), F32),
            sds((z.short, 2 * z.obs), BF16),
        ),
        in_specs=[whole] * 6 + [smem],
        out_specs=(whole,) * 4,
        scratch_shapes=[coeff, strip_field, strip_field, packed, packed],
        name="strip",
    )(inner, sent_a, sent_b, got_a, got_b, cell, mem_weight)
    others = [lax.ppermute(values, "mem", [(i, i ^ k) for i in range(holders)]) for k in range(1, holders)]
    main_c, strip_c, own_lane, beside_lane = call(
        functools.partial(ready_kernel, z),
        out_shape=(
            sds((5, z.rows, 128), F32),
            sds((5, z.rows, 128), F32),
            sds((2 * 128, z.obs), BF16),
            sds((128, 2 * z.obs), BF16),
        ),
        in_specs=[whole] * 7,
        out_specs=(whole,) * 4,
        name="ready",
    )(kappa, norm_scale, land_sea, cell, got_a, got_b, strip_coeff)
    product = call(
        functools.partial(adjoint_kernel, z),
        out_shape=sds((z.field, z.columns), F32),
        in_specs=[stays, stays, smem] + [whole] * 14,
        out_specs=stays,
        scratch_shapes=[
            main_field,
            main_field,
            strip_field,
            strip_field,
            pltpu.VMEM((z.short, 128), F32),
            pltpu.VMEM((512, 2 * z.obs), BF16),
            pltpu.VMEM((z.field, 128), F32),
            pltpu.VMEM((z.field, 128), BF16),
            pltpu.VMEM((z.field, 128), F32),
            pltpu.SemaphoreType.DMA((2 + z.levels // 2,)),
        ],
        name="adjoint",
    )(
        alpha, members, mem_weight, weight, got_a, got_b, strip_members, main_c, strip_c,
        own_row, own_lane, beside_row, beside_lane, values, *others,
    )
    return product.reshape(shape)


def solution(mesh):
    placed = (
        P("mem", None, None, "tile"),
        P("mem", None, None, "tile"),
        P("mem"),
        P(None, "tile"),
        P(None, "tile"),
        P(None, "tile"),
        P("tile"),
        P("tile"),
    )
    return jax.shard_map(
        local, mesh=mesh, in_specs=placed, out_specs=P("mem", None, None, "tile"), check_vma=False
    )
```

```python
import functools

import jax
import jax.numpy as jnp
from jax import lax
from jax.experimental import pallas as pl
from jax.experimental.pallas import tpu as pltpu
from jax.sharding import PartitionSpec as P

STEPS = 8
SUB = 8
EDGE = 2 * STEPS
F32 = jnp.float32
BF16 = jnp.bfloat16


def div_mod(value, size):
    if size & (size - 1) == 0:
        return value >> (size.bit_length() - 1), value & (size - 1)
    return lax.div(value, size), lax.rem(value, size)


def roll(value, shift, axis=1):
    shift %= value.shape[axis]
    return pltpu.roll(value, shift, axis) if shift else value


def lanes(rows):
    return lax.broadcasted_iota(jnp.int32, (rows, 128), 1)


def split(value):
    high = value.astype(BF16)
    return high, (value - high.astype(F32)).astype(BF16)


class Sizes:
    def __init__(self, levels, rows, columns, obs):
        self.levels, self.rows, self.columns, self.obs = levels, rows, columns, obs
        assert columns == 128 and levels == 16 and rows % 16 == 0 and obs % 256 == 0 and STEPS == 8
        self.field = levels * rows
        self.group = self.field // 2
        self.short = self.field // 8
        self.tiles = rows // SUB
        assert self.tiles == 8
        self.at_members = self.short
        self.at_coeff = self.at_members + rows
        self.at_obs = self.at_coeff + 3 * SUB
        self.obs_rows = obs // 128
        self.payload = self.at_obs + 2 * self.obs_rows


def overlay(pieces, window):
    value = pieces[0]
    for k in range(1, len(pieces)):
        value = jnp.where(window == k, pieces[k], value)
    return value


def pack_kernel(
    z, alpha_hbm, members_hbm, kappa_hbm, scale_hbm, ocean_hbm, cell_hbm, weight_hbm,
    out_far, out_near, alpha, members, kappa, scale, ocean, cell, weight, sems,
):
    pairs = (
        (members_hbm, members), (alpha_hbm, alpha), (kappa_hbm, kappa), (scale_hbm, scale), (ocean_hbm, ocean),
        (cell_hbm, cell), (weight_hbm, weight),
    )
    copies = [pltpu.make_async_copy(a, b, sems.at[k]) for k, (a, b) in enumerate(pairs)]
    for copy in copies:
        copy.start()
    even = lax.rem(lax.axis_index("tile"), 2) == 0

    def put(where, right, left):
        out_near[where, :] = jnp.where(even, right, left)
        out_far[where, :] = jnp.where(even, left, right)

    for copy in copies[2:]:
        copy.wait()
    lane = lanes(SUB)
    for k, ref in enumerate((kappa, scale, ocean)):
        right, left = [], []
        for t in range(z.tiles):
            value = ref[pl.ds(t * SUB, SUB), :].astype(F32)
            right.append(roll(value, EDGE * (t + 1)))
            left.append(roll(value, EDGE * t))
        put(pl.ds(z.at_coeff + k * SUB, SUB), overlay(right, lane >> 4), overlay(left, lane >> 4))
    n = z.obs_rows
    for at, value in ((z.at_obs, cell[...].astype(F32)), (z.at_obs + n, weight[...])):
        out_near[pl.ds(at, n), :] = value
        out_far[pl.ds(at, n), :] = value
    copies[0].wait()
    block = 2 * SUB
    lane = lanes(block)
    for t in range(z.rows // block):
        right, left = [], []
        for g in range(2):
            for part in range(SUB):
                value = members[pl.ds(g * z.group + part * z.rows + t * block, block), :].astype(F32)
                base = 64 * g + STEPS * part
                right.append(roll(value, base + STEPS))
                left.append(roll(value, base))
        put(pl.ds(z.at_members + t * block, block), overlay(right, lane >> 3), overlay(left, lane >> 3))
    copies[1].wait()
    for t in range(z.short // block):
        right, left = [], []
        for g in range(2):
            for h in range(4):
                value = alpha[pl.ds(g * z.group + h * z.short + t * block, block), :]
                base = 64 * g + EDGE * h
                right.append(roll(value, base + EDGE))
                left.append(roll(value, base))
        put(pl.ds(t * block, block), overlay(right, lane >> 4), overlay(left, lane >> 4))


def up(value):
    return roll(value, -1, 0)


def down(value):
    return roll(value, 1, 0)


def coefficients(kappa, scale, ocean, forward):
    row = lax.broadcasted_iota(jnp.int32, kappa.shape, 0)
    north = 0.5 * (kappa + up(kappa)) * ocean * up(ocean)
    north = jnp.where(row == kappa.shape[0] - 1, 0.0, north)
    east = 0.5 * (kappa + roll(kappa, -1)) * ocean * roll(ocean, -1)
    west, south = roll(east, 1), down(north)
    centre = 1.0 - (east + west) - (north + south)
    if forward:
        return (
            centre * scale,
            east * roll(scale, -1),
            west * roll(scale, 1),
            north * up(scale),
            south * down(scale),
        )
    return tuple(scale * c for c in (centre, east, west, north, south))


def put_coefficients(ref, values):
    for k, value in enumerate(values):
        ref[k] = value


def step_rows(source, target, coeff, rows, levels):
    for t in range(rows // SUB):
        c = [coeff[k, pl.ds(t * SUB, SUB), :] for k in range(5)]
        for level in range(levels):
            at = SUB + level * rows + t * SUB
            u = source[pl.ds(at, SUB), :]
            along = c[3] * source[pl.ds(at + 1, SUB), :] + c[4] * source[pl.ds(at - 1, SUB), :]
            across = c[1] * roll(u, -1) + c[2] * roll(u, 1)
            target[pl.ds(at, SUB), :] = c[0] * u + across + along


def clear_ends(*buffers):
    for ref in buffers:
        zero = jnp.zeros((SUB, 128), F32)
        ref[pl.ds(0, SUB), :] = zero
        ref[pl.ds(ref.shape[0] - SUB, SUB), :] = zero


def sweep(fields, rows):
    def two_steps(_, carry):
        for x, y, coeff, levels in fields:
            step_rows(x, y, coeff, rows, levels)
        for x, y, coeff, levels in fields:
            step_rows(y, x, coeff, rows, levels)
        return carry

    lax.fori_loop(0, STEPS // 2, two_steps, 0)


def cell_parts(z, cell):
    level, rest = div_mod(cell, z.rows * z.columns)
    row, column = div_mod(rest, z.columns)
    return level >> 3, level & 7, row, column


def own_index(z, cell):
    group, part, row, column = cell_parts(z, cell)
    return part * z.rows + row, group * 128 + column


def edge_index(z, cell, windows):
    group, part, row, column = cell_parts(z, cell)
    inside, lane = False, 0
    for first, at in windows:
        here = (column >= first) & (column < first + STEPS)
        inside = here | inside
        lane = jnp.where(here, at - first, lane)
    lane = lane + column + 64 * group + 16 * (part >> 1)
    return jnp.where(inside, (part & 1) * z.rows + row, -1), lane & 127


def own_edges(z):
    return (0, 48), (z.columns - STEPS, 8)


def windows_of(z):
    return own_edges(z), ((0, 16),), ((z.columns - STEPS, 40),)


def quarters(unit, first, second):
    even, odd = (first, second) if first % 2 == 0 else (second, first)
    return jnp.where((unit & 1) == 0, ((unit - even) >> 1) & 3, ((unit - odd) >> 1) & 3)


def one_hot(index, size):
    rows = lax.broadcasted_iota(jnp.int32, (size, index.shape[1]), 0)
    return jnp.where(rows == index, 1.0, 0.0).astype(BF16)


def read_off(field, hot, j):
    value = lax.dot_general(field, hot, (((0,), (0,)), ((), ())), preferred_element_type=F32)
    n = value.shape[0] // 2
    value = value[:n] + value[n:]
    rows = lax.broadcasted_iota(jnp.int32, value.shape, 0)
    return jnp.sum(jnp.where(rows == j, value, 0.0), axis=0, keepdims=True)


def gather(z, out, at, field, cell, index, keep=None, start=0):
    for n in range(z.obs_rows // 2):
        row = jnp.concatenate([cell[2 * n : 2 * n + 1, :], cell[2 * n + 1 : 2 * n + 2, :]], axis=1)
        i, j = index(row)
        hot = one_hot(i, field.shape[0])
        if keep is not None:
            keep[:, pl.ds(start + 256 * n, 256)] = hot
        value = read_off(field, hot, j)
        out[at + 2 * n : at + 2 * n + 1, :] = value[:, :128]
        out[at + 2 * n + 1 : at + 2 * n + 2, :] = value[:, 128:]


def forward_sweep(z, alpha, kappa, scale, ocean, coeff, x, y):
    put_coefficients(coeff, coefficients(kappa[...], scale[...], ocean[...].astype(F32), True))
    clear_ends(x, y)
    x[pl.ds(SUB, z.field), :] = alpha[...]
    sweep([(x, y, coeff, z.levels)], z.rows)


def main_kernel(z, alpha, members, weight, kappa, scale, ocean, cell, out, hot, x, coeff, y, both):
    forward_sweep(z, alpha, kappa, scale, ocean, coeff, x, y)
    lane = lanes(z.group)
    inner = (lane >= STEPS) & (lane < z.columns - STEPS)
    for g in range(2):
        rows = pl.ds(g * z.group, z.group)
        value = x[pl.ds(SUB + g * z.group, z.group), :] * (members[rows, :].astype(F32) * weight[0])
        high, low = split(jnp.where(inner, value, 0.0))
        both[:, pl.ds(g * 128, 128)] = high
        both[:, pl.ds(256 + g * 128, 128)] = low
    gather(z, out, 0, both[...], cell[...], lambda c: own_index(z, c), hot)


def strip_kernel(
    z, inner, members, sent_far, sent_near, got_far, got_near, cell, weight,
    out, strip_members, strip_coeff, hot, coeff, x, y, outer, beside,
):
    even = lax.rem(lax.axis_index("tile"), 2) == 0

    def parts(rows):
        pick = lambda p, q: jnp.where(even, p[rows, :], q[rows, :])
        return (
            pick(sent_near, sent_far),
            pick(got_near, got_far),
            pick(got_far, got_near),
            pick(sent_far, sent_near),
        )

    clear_ends(x, y)
    lane = lanes(SUB)
    part_of, side = (lane >> 4) & 3, lane >> 6
    for k in range(3):
        four = parts(pl.ds(z.at_coeff + k * SUB, SUB))
        for t in range(z.tiles):
            pieces = [roll(four[p], EDGE * p + 64 * g - EDGE * t) for g in range(2) for p in range(4)]
            strip_coeff[k, pl.ds(t * SUB, SUB), :] = overlay(pieces, lane >> 4)
    for q in range(z.short // SUB):
        four = parts(pl.ds(q * SUB, SUB))
        for h in range(4):
            pieces = [roll(four[p], EDGE * (p - h)) for p in range(4)]
            x[pl.ds(SUB + h * z.short + q * SUB, SUB), :] = overlay(pieces, part_of)
    block = 2 * SUB
    wide_lane = lanes(block)
    for t in range(z.rows // block):
        rows = pl.ds(z.at_members + t * block, block)
        _, right, left, _ = parts(rows)
        for part in range(SUB):
            at = part * z.rows + t * block
            value = jnp.where(
                (wide_lane & 32) == 0,
                roll(right, EDGE - STEPS * part),
                roll(left, 2 * EDGE + STEPS - STEPS * part),
            )
            for g in range(2):
                own = members[pl.ds(g * z.group + at, block), :].astype(F32)
                mine = (wide_lane >> 6) == g
                inside = (wide_lane >> 4) & 3
                value = jnp.where(mine & (inside == 0), roll(own, EDGE + 64 * g), value)
                value = jnp.where(mine & (inside == 3), roll(own, 48 + 64 * g), value)
            strip_members[pl.ds(at, block), :] = value * weight[0]
    put_coefficients(coeff, coefficients(strip_coeff[0], strip_coeff[1], strip_coeff[2], True))
    sweep([(x, y, coeff, z.levels // 2)], z.rows)
    unit = lanes(z.short) >> 3
    for ref, first, second in ((outer, 1, 6), (beside, 2, 5)):
        quarter = quarters(unit, first, second)
        pieces = []
        for k in range(4):
            rows = pl.ds(k * z.short, z.short)
            pieces.append(roll(x[pl.ds(SUB + k * z.short, z.short), :] * strip_members[rows, :], 16 * k))
        high, low = split(overlay(pieces, quarter))
        ref[:, :128] = high
        ref[:, 128:] = low
    _, right, left, _ = parts(pl.ds(z.at_obs, z.obs_rows))
    n = z.obs_rows
    for k, (field, cells) in enumerate(
        ((outer, cell[...]), (beside, right.astype(jnp.int32)), (beside, left.astype(jnp.int32)))
    ):
        keep = hot if k else None
        gather(z, out, k * n, field[...], cells, lambda c: edge_index(z, c, windows_of(z)[k]), keep, (k - 1) * z.obs)
    out[:n, :] = out[:n, :] + inner[...]


def beside_rows(z, got_far, got_near, at):
    even = lax.rem(lax.axis_index("tile"), 2) == 0
    far, near = got_far[pl.ds(at, z.obs_rows), :], got_near[pl.ds(at, z.obs_rows), :]
    return jnp.where(even, near, far), jnp.where(even, far, near)


def ready_kernel(z, kappa, scale, ocean, cell, got_far, got_near, strip_coeff, coeff, strip_c, own_lane, beside_lane):
    put_coefficients(coeff, coefficients(kappa[...], scale[...], ocean[...].astype(F32), False))
    put_coefficients(strip_c, coefficients(strip_coeff[0], strip_coeff[1], strip_coeff[2], False))
    _, right_window, left_window = windows_of(z)
    right, left = beside_rows(z, got_far, got_near, z.at_obs)
    n = z.obs_rows
    for r in range(n):
        at = pl.ds(r * 128, 128)
        own_lane[:, at] = one_hot(own_index(z, cell[r : r + 1, :])[1], 256)
        index = right[r : r + 1, :].astype(jnp.int32)
        beside_lane[:, at] = one_hot(edge_index(z, index, right_window)[1], 128)
        index = left[r : r + 1, :].astype(jnp.int32)
        beside_lane[:, pl.ds(z.obs + r * 128, 128)] = one_hot(edge_index(z, index, left_window)[1], 128)


def adjoint_kernel(
    z, alpha, members, weight, obs_weight, got_far, got_near, strip_members, coeff, strip_c,
    own_row, own_lane, beside_row, beside_lane, v0, v1, v2, v3,
    out_hbm, x, y, strip, spare, beside, spread, out, sems,
):
    clear_ends(x, y, strip, spare)
    value = (v0[...] + v1[...]) + (v2[...] + v3[...])
    n = z.obs_rows
    right_weight, left_weight = beside_rows(z, got_far, got_near, z.at_obs + n)

    def spread_out(amounts, row_hot, lane_hot):
        wide = lane_hot.shape[0]
        for group, amount in enumerate(amounts):
            high, low = split(amount)
            for r in range(n):
                at = pl.ds(group * z.obs + r * 128, 128)
                for k, part in enumerate((high, low)):
                    line = jnp.broadcast_to(part[r : r + 1, :].astype(F32), (2 * SUB, 128)).astype(BF16)
                    for t in range(wide // (2 * SUB)):
                        rows = pl.ds(t * 2 * SUB, 2 * SUB)
                        spread[pl.ds(k * wide + t * 2 * SUB, 2 * SUB), at] = lane_hot[rows, at] * line
        dims = (((1,), (1,)), ((), ()))
        total = lax.dot_general(
            row_hot[...], spread[: 2 * wide, : len(amounts) * z.obs], dims, preferred_element_type=F32
        )
        return total[:, :wide] + total[:, wide:]

    field = spread_out([obs_weight[...] * value[:n]], own_row, own_lane)
    for g in range(2):
        x[pl.ds(SUB + g * z.group, z.group), :] = field[:, g * 128 : (g + 1) * 128]
    beside[...] = spread_out(
        [right_weight * value[n : 2 * n], left_weight * value[2 * n :]], beside_row, beside_lane
    )
    lane = lanes(SUB)
    part = (lane >> 4) & 3
    within = lane & 15
    outside = ((part == 1) & (within < STEPS)) | ((part == 2) & (within >= STEPS))
    for q in range(z.group // SUB):
        k, rest = divmod(q * SUB, z.short)
        value = jnp.where(outside, roll(beside[pl.ds(rest, SUB), :], -16 * k), 0.0)
        for g in range(2):
            at = g * z.group + q * SUB
            here = pl.ds(SUB + at, SUB)
            field = x[here, :]
            mine = (lane >> 6) == g
            value = jnp.where(mine & (part == 0), roll(field, EDGE + 64 * g), value)
            value = jnp.where(mine & (part == 3), roll(field, 48 + 64 * g), value)
        strip[pl.ds(SUB + q * SUB, SUB), :] = value * strip_members[pl.ds(q * SUB, SUB), :]
    here = pl.ds(SUB, z.field)
    x[here, :] = x[here, :] * (members[...].astype(F32) * weight[0])
    sweep([(x, y, coeff, z.levels), (strip, spare, strip_c, z.levels // 2)], z.rows)
    sent = []
    for part in range(z.levels // 2):
        for t in range(z.rows // SUB):
            q = part * z.rows + t * SUB
            value = strip[pl.ds(SUB + q, SUB), :]
            for g in range(2):
                at = g * z.group + q
                fixed = x[pl.ds(SUB + at, SUB), :]
                fixed = jnp.where(lane >= z.columns - STEPS, roll(value, 112 - 64 * g), fixed)
                fixed = jnp.where(lane < STEPS, roll(value, -48 - 64 * g), fixed)
                out[pl.ds(at, SUB), :] = alpha[pl.ds(at, SUB), :] + fixed
        if part % 2:
            for g in range(2):
                rows = pl.ds(g * z.group + (part - 1) * z.rows, 2 * z.rows)
                sent.append(pltpu.make_async_copy(out.at[rows, :], out_hbm.at[rows, :], sems.at[len(sent)]))
                sent[-1].start()
    for copy in sent:
        copy.wait()


def local(alpha, members, mem_weight, kappa, norm_scale, land_sea, obs_cell, obs_weight):
    shape = alpha.shape
    z = Sizes(shape[1], shape[2], shape[3], obs_cell.shape[0])
    tiles, holders = lax.axis_size("tile"), lax.axis_size("mem")
    assert tiles % 2 == 0 and holders == 4 and shape[0] == 1
    alpha = alpha.reshape(z.field, z.columns)
    members = members.reshape(z.field, z.columns)
    cell = obs_cell.reshape(z.obs_rows, 128)
    weight = obs_weight.reshape(z.obs_rows, 128)
    smem = pl.BlockSpec(memory_space=pltpu.SMEM)
    whole = pl.BlockSpec(memory_space=pltpu.VMEM)
    stays = pl.BlockSpec(memory_space=pltpu.HBM)
    sds = jax.ShapeDtypeStruct
    main_field = pltpu.VMEM((z.field + 2 * SUB, 128), F32)
    strip_field = pltpu.VMEM((z.group + 2 * SUB, 128), F32)
    coeff = pltpu.VMEM((5, z.rows, 128), F32)
    packed = pltpu.VMEM((z.short, 256), BF16)
    payload = sds((z.payload, 128), F32)
    limit = pltpu.CompilerParams(vmem_limit_bytes=24 << 20)
    call = functools.partial(pl.pallas_call, compiler_params=limit)
    given = (alpha, members, kappa, norm_scale, land_sea, cell, weight)
    sent_far, sent_near, *given = call(
        functools.partial(pack_kernel, z),
        out_shape=(payload, payload, *(sds(v.shape, v.dtype) for v in given)),
        in_specs=[stays] * 7,
        out_specs=(whole,) * 9,
        scratch_shapes=[pltpu.SemaphoreType.DMA((7,))],
        name="pack",
    )(*given)
    alpha, members, kappa, norm_scale, land_sea, cell, weight = given
    near = [(i, i ^ 1) for i in range(tiles)]
    far = [(i, (i + 1) % tiles if i % 2 else (i - 1) % tiles) for i in range(tiles)]
    got_far = lax.ppermute(sent_far, "tile", far)
    got_near = lax.ppermute(sent_near, "tile", near)
    inner, own_row = call(
        functools.partial(main_kernel, z),
        out_shape=(sds((z.obs_rows, 128), F32), sds((z.group, z.obs), BF16)),
        in_specs=[whole] * 2 + [smem] + [whole] * 4,
        out_specs=(whole, whole),
        scratch_shapes=[main_field, coeff, main_field, pltpu.VMEM((z.group, 512), BF16)],
        name="main",
    )(alpha, members, mem_weight, kappa, norm_scale, land_sea, cell)
    values, strip_members, strip_coeff, beside_row = call(
        functools.partial(strip_kernel, z),
        out_shape=(
            sds((3 * z.obs_rows, 128), F32),
            sds((z.group, 128), F32),
            sds((3, z.rows, 128), F32),
            sds((z.short, 2 * z.obs), BF16),
        ),
        in_specs=[whole] * 7 + [smem],
        out_specs=(whole,) * 4,
        scratch_shapes=[coeff, strip_field, strip_field, packed, packed],
        name="strip",
    )(inner, members, sent_far, sent_near, got_far, got_near, cell, mem_weight)
    others = [lax.ppermute(values, "mem", [(i, i ^ k) for i in range(holders)]) for k in range(1, holders)]
    main_c, strip_c, own_lane, beside_lane = call(
        functools.partial(ready_kernel, z),
        out_shape=(
            sds((5, z.rows, 128), F32),
            sds((5, z.rows, 128), F32),
            sds((2 * 128, z.obs), BF16),
            sds((128, 2 * z.obs), BF16),
        ),
        in_specs=[whole] * 7,
        out_specs=(whole,) * 4,
        name="ready",
    )(kappa, norm_scale, land_sea, cell, got_far, got_near, strip_coeff)
    product = call(
        functools.partial(adjoint_kernel, z),
        out_shape=sds((z.field, z.columns), F32),
        in_specs=[whole, whole, smem] + [whole] * 14,
        out_specs=stays,
        scratch_shapes=[
            main_field,
            main_field,
            strip_field,
            strip_field,
            pltpu.VMEM((z.short, 128), F32),
            pltpu.VMEM((512, 2 * z.obs), BF16),
            pltpu.VMEM((z.field, 128), F32),
            pltpu.SemaphoreType.DMA((z.levels // 2,)),
        ],
        name="adjoint",
    )(
        alpha, members, mem_weight, weight, got_far, got_near, strip_members, main_c, strip_c,
        own_row, own_lane, beside_row, beside_lane, values, *others,
    )
    return product.reshape(shape)


def solution(mesh):
    placed = (
        P("mem", None, None, "tile"),
        P("mem", None, None, "tile"),
        P("mem"),
        P(None, "tile"),
        P(None, "tile"),
        P(None, "tile"),
        P("tile"),
        P("tile"),
    )
    return jax.shard_map(
        local, mesh=mesh, in_specs=placed, out_specs=P("mem", None, None, "tile"), check_vma=False
    )
```

```python
import functools

import jax
import jax.numpy as jnp
from jax import lax
from jax.experimental import pallas as pl
from jax.experimental.pallas import tpu as pltpu
from jax.sharding import PartitionSpec as P

STEPS = 8
SUB = 8
EDGE = 2 * STEPS
F32 = jnp.float32
BF16 = jnp.bfloat16


def div_mod(value, size):
    if size & (size - 1) == 0:
        return value >> (size.bit_length() - 1), value & (size - 1)
    return lax.div(value, size), lax.rem(value, size)


def roll(value, shift, axis=1):
    shift %= value.shape[axis]
    return pltpu.roll(value, shift, axis) if shift else value


def lanes(rows):
    return lax.broadcasted_iota(jnp.int32, (rows, 128), 1)


def split(value):
    high = value.astype(BF16)
    return high, (value - high.astype(F32)).astype(BF16)


class Sizes:
    def __init__(self, levels, rows, columns, obs):
        self.levels, self.rows, self.columns, self.obs = levels, rows, columns, obs
        assert columns == 128 and levels == 16 and rows % 16 == 0 and obs % 256 == 0 and STEPS == 8
        self.field = levels * rows
        self.group = self.field // 2
        self.short = self.field // 8
        self.tiles = rows // SUB
        assert self.tiles == 8
        self.at_members = self.short
        self.at_coeff = self.at_members + rows
        self.at_obs = self.at_coeff + 3 * SUB
        self.obs_rows = obs // 128
        self.payload = self.at_obs + 2 * self.obs_rows


def overlay(pieces, window):
    value = pieces[0]
    for k in range(1, len(pieces)):
        value = jnp.where(window == k, pieces[k], value)
    return value


def pack_kernel(
    z, alpha_hbm, members_hbm, kappa_hbm, scale_hbm, ocean_hbm, cell_hbm, weight_hbm,
    out_far, out_near, alpha, members, kappa, scale, ocean, cell, weight, sems,
):
    pairs = (
        (members_hbm, members), (alpha_hbm, alpha), (kappa_hbm, kappa), (scale_hbm, scale), (ocean_hbm, ocean),
        (cell_hbm, cell), (weight_hbm, weight),
    )
    copies = [pltpu.make_async_copy(a, b, sems.at[k]) for k, (a, b) in enumerate(pairs)]
    for copy in copies:
        copy.start()
    even = lax.rem(lax.axis_index("tile"), 2) == 0

    def put(where, right, left):
        out_near[where, :] = jnp.where(even, right, left)
        out_far[where, :] = jnp.where(even, left, right)

    for copy in copies[2:]:
        copy.wait()
    lane = lanes(SUB)
    for k, ref in enumerate((kappa, scale, ocean)):
        right, left = [], []
        for t in range(z.tiles):
            value = ref[pl.ds(t * SUB, SUB), :].astype(F32)
            right.append(roll(value, EDGE * (t + 1)))
            left.append(roll(value, EDGE * t))
        put(pl.ds(z.at_coeff + k * SUB, SUB), overlay(right, lane >> 4), overlay(left, lane >> 4))
    n = z.obs_rows
    for at, value in ((z.at_obs, cell[...].astype(F32)), (z.at_obs + n, weight[...])):
        out_near[pl.ds(at, n), :] = value
        out_far[pl.ds(at, n), :] = value
    copies[0].wait()
    block = 2 * SUB
    lane = lanes(block)
    for t in range(z.rows // block):
        right, left = [], []
        for g in range(2):
            for part in range(SUB):
                value = members[pl.ds(g * z.group + part * z.rows + t * block, block), :].astype(F32)
                base = 64 * g + STEPS * part
                right.append(roll(value, base + STEPS))
                left.append(roll(value, base))
        put(pl.ds(z.at_members + t * block, block), overlay(right, lane >> 3), overlay(left, lane >> 3))
    copies[1].wait()
    for t in range(z.short // block):
        right, left = [], []
        for g in range(2):
            for h in range(4):
                value = alpha[pl.ds(g * z.group + h * z.short + t * block, block), :]
                base = 64 * g + EDGE * h
                right.append(roll(value, base + EDGE))
                left.append(roll(value, base))
        put(pl.ds(t * block, block), overlay(right, lane >> 4), overlay(left, lane >> 4))


def up(value):
    return roll(value, -1, 0)


def down(value):
    return roll(value, 1, 0)


def coefficients(kappa, scale, ocean, forward):
    row = lax.broadcasted_iota(jnp.int32, kappa.shape, 0)
    north = 0.5 * (kappa + up(kappa)) * ocean * up(ocean)
    north = jnp.where(row == kappa.shape[0] - 1, 0.0, north)
    east = 0.5 * (kappa + roll(kappa, -1)) * ocean * roll(ocean, -1)
    west, south = roll(east, 1), down(north)
    centre = 1.0 - (east + west) - (north + south)
    if forward:
        return (
            centre * scale,
            east * roll(scale, -1),
            west * roll(scale, 1),
            north * up(scale),
            south * down(scale),
        )
    return tuple(scale * c for c in (centre, east, west, north, south))


def put_coefficients(ref, values):
    for k, value in enumerate(values):
        ref[k] = value


def step_rows(source, target, coeff, rows, levels):
    for t in range(rows // SUB):
        c = [coeff[k, pl.ds(t * SUB, SUB), :] for k in range(5)]
        for level in range(levels):
            at = SUB + level * rows + t * SUB
            u = source[pl.ds(at, SUB), :]
            along = c[3] * source[pl.ds(at + 1, SUB), :] + c[4] * source[pl.ds(at - 1, SUB), :]
            across = c[1] * roll(u, -1) + c[2] * roll(u, 1)
            target[pl.ds(at, SUB), :] = c[0] * u + across + along


def clear_ends(*buffers):
    for ref in buffers:
        zero = jnp.zeros((SUB, 128), F32)
        ref[pl.ds(0, SUB), :] = zero
        ref[pl.ds(ref.shape[0] - SUB, SUB), :] = zero


def sweep(fields, rows):
    def two_steps(_, carry):
        for x, y, coeff, levels in fields:
            step_rows(x, y, coeff, rows, levels)
        for x, y, coeff, levels in fields:
            step_rows(y, x, coeff, rows, levels)
        return carry

    lax.fori_loop(0, STEPS // 2, two_steps, 0)


def cell_parts(z, cell):
    level, rest = div_mod(cell, z.rows * z.columns)
    row, column = div_mod(rest, z.columns)
    return level >> 3, level & 7, row, column


def own_index(z, cell):
    group, part, row, column = cell_parts(z, cell)
    return part * z.rows + row, group * 128 + column


def edge_index(z, cell, windows):
    group, part, row, column = cell_parts(z, cell)
    inside, lane = False, 0
    for first, at in windows:
        here = (column >= first) & (column < first + STEPS)
        inside = here | inside
        lane = jnp.where(here, at - first, lane)
    lane = lane + column + 64 * group + 16 * (part >> 1)
    return jnp.where(inside, (part & 1) * z.rows + row, -1), lane & 127


def own_edges(z):
    return (0, 48), (z.columns - STEPS, 8)


def windows_of(z):
    return own_edges(z), ((0, 16),), ((z.columns - STEPS, 40),)


def quarters(unit, first, second):
    even, odd = (first, second) if first % 2 == 0 else (second, first)
    return jnp.where((unit & 1) == 0, ((unit - even) >> 1) & 3, ((unit - odd) >> 1) & 3)


def one_hot(index, size):
    rows = lax.broadcasted_iota(jnp.int32, (size, index.shape[1]), 0)
    return jnp.where(rows == index, 1.0, 0.0).astype(BF16)


def read_off(field, hot, j):
    value = lax.dot_general(field, hot, (((0,), (0,)), ((), ())), preferred_element_type=F32)
    n = value.shape[0] // 2
    value = value[:n] + value[n:]
    rows = lax.broadcasted_iota(jnp.int32, value.shape, 0)
    return jnp.sum(jnp.where(rows == j, value, 0.0), axis=0, keepdims=True)


def gather(z, out, at, field, cell, index, keep=None, start=0):
    for n in range(z.obs_rows // 2):
        row = jnp.concatenate([cell[2 * n : 2 * n + 1, :], cell[2 * n + 1 : 2 * n + 2, :]], axis=1)
        i, j = index(row)
        hot = one_hot(i, field.shape[0])
        if keep is not None:
            keep[:, pl.ds(start + 256 * n, 256)] = hot
        value = read_off(field, hot, j)
        out[at + 2 * n : at + 2 * n + 1, :] = value[:, :128]
        out[at + 2 * n + 1 : at + 2 * n + 2, :] = value[:, 128:]


def forward_sweep(z, alpha, kappa, scale, ocean, coeff, x, y):
    put_coefficients(coeff, coefficients(kappa[...], scale[...], ocean[...].astype(F32), True))
    clear_ends(x, y)
    x[pl.ds(SUB, z.field), :] = alpha[...]
    sweep([(x, y, coeff, z.levels)], z.rows)


def main_kernel(z, alpha, members, weight, kappa, scale, ocean, cell, out, hot, x, coeff, y, both):
    forward_sweep(z, alpha, kappa, scale, ocean, coeff, x, y)
    lane = lanes(z.group)
    inner = (lane >= STEPS) & (lane < z.columns - STEPS)
    for g in range(2):
        rows = pl.ds(g * z.group, z.group)
        value = x[pl.ds(SUB + g * z.group, z.group), :] * (members[rows, :].astype(F32) * weight[0:1, :])
        high, low = split(jnp.where(inner, value, 0.0))
        both[:, pl.ds(g * 128, 128)] = high
        both[:, pl.ds(256 + g * 128, 128)] = low
    gather(z, out, 0, both[...], cell[...], lambda c: own_index(z, c), hot)


def strip_kernel(
    z, inner, members, sent_far, sent_near, got_far, got_near, cell, weight,
    out, strip_members, strip_coeff, hot, coeff, x, y, outer, beside,
):
    even = lax.rem(lax.axis_index("tile"), 2) == 0

    def parts(rows):
        pick = lambda p, q: jnp.where(even, p[rows, :], q[rows, :])
        return (
            pick(sent_near, sent_far),
            pick(got_near, got_far),
            pick(got_far, got_near),
            pick(sent_far, sent_near),
        )

    clear_ends(x, y)
    lane = lanes(SUB)
    part_of, side = (lane >> 4) & 3, lane >> 6
    for k in range(3):
        four = parts(pl.ds(z.at_coeff + k * SUB, SUB))
        for t in range(z.tiles):
            pieces = [roll(four[p], EDGE * p + 64 * g - EDGE * t) for g in range(2) for p in range(4)]
            strip_coeff[k, pl.ds(t * SUB, SUB), :] = overlay(pieces, lane >> 4)
    for q in range(z.short // SUB):
        four = parts(pl.ds(q * SUB, SUB))
        for h in range(4):
            pieces = [roll(four[p], EDGE * (p - h)) for p in range(4)]
            x[pl.ds(SUB + h * z.short + q * SUB, SUB), :] = overlay(pieces, part_of)
    block = 2 * SUB
    wide_lane = lanes(block)
    for t in range(z.rows // block):
        rows = pl.ds(z.at_members + t * block, block)
        _, right, left, _ = parts(rows)
        for part in range(SUB):
            at = part * z.rows + t * block
            value = jnp.where(
                (wide_lane & 32) == 0,
                roll(right, EDGE - STEPS * part),
                roll(left, 2 * EDGE + STEPS - STEPS * part),
            )
            for g in range(2):
                own = members[pl.ds(g * z.group + at, block), :].astype(F32)
                mine = (wide_lane >> 6) == g
                inside = (wide_lane >> 4) & 3
                value = jnp.where(mine & (inside == 0), roll(own, EDGE + 64 * g), value)
                value = jnp.where(mine & (inside == 3), roll(own, 48 + 64 * g), value)
            strip_members[pl.ds(at, block), :] = value * weight[0:1, :]
    put_coefficients(coeff, coefficients(strip_coeff[0], strip_coeff[1], strip_coeff[2], True))
    sweep([(x, y, coeff, z.levels // 2)], z.rows)
    unit = lanes(z.short) >> 3
    for ref, first, second in ((outer, 1, 6), (beside, 2, 5)):
        quarter = quarters(unit, first, second)
        pieces = []
        for k in range(4):
            rows = pl.ds(k * z.short, z.short)
            pieces.append(roll(x[pl.ds(SUB + k * z.short, z.short), :] * strip_members[rows, :], 16 * k))
        high, low = split(overlay(pieces, quarter))
        ref[:, :128] = high
        ref[:, 128:] = low
    _, right, left, _ = parts(pl.ds(z.at_obs, z.obs_rows))
    n = z.obs_rows
    for k, (field, cells) in enumerate(
        ((outer, cell[...]), (beside, right.astype(jnp.int32)), (beside, left.astype(jnp.int32)))
    ):
        keep = hot if k else None
        gather(z, out, k * n, field[...], cells, lambda c: edge_index(z, c, windows_of(z)[k]), keep, (k - 1) * z.obs)
    out[:n, :] = out[:n, :] + inner[...]


def beside_rows(z, got_far, got_near, at):
    even = lax.rem(lax.axis_index("tile"), 2) == 0
    far, near = got_far[pl.ds(at, z.obs_rows), :], got_near[pl.ds(at, z.obs_rows), :]
    return jnp.where(even, near, far), jnp.where(even, far, near)


def ready_kernel(z, kappa, scale, ocean, cell, got_far, got_near, strip_coeff, coeff, strip_c, own_lane, beside_lane):
    put_coefficients(coeff, coefficients(kappa[...], scale[...], ocean[...].astype(F32), False))
    put_coefficients(strip_c, coefficients(strip_coeff[0], strip_coeff[1], strip_coeff[2], False))
    _, right_window, left_window = windows_of(z)
    right, left = beside_rows(z, got_far, got_near, z.at_obs)
    n = z.obs_rows
    for r in range(n):
        at = pl.ds(r * 128, 128)
        own_lane[:, at] = one_hot(own_index(z, cell[r : r + 1, :])[1], 256)
        index = right[r : r + 1, :].astype(jnp.int32)
        beside_lane[:, at] = one_hot(edge_index(z, index, right_window)[1], 128)
        index = left[r : r + 1, :].astype(jnp.int32)
        beside_lane[:, pl.ds(z.obs + r * 128, 128)] = one_hot(edge_index(z, index, left_window)[1], 128)


def adjoint_kernel(
    z, alpha, members, weight, obs_weight, got_far, got_near, strip_members, coeff, strip_c,
    own_row, own_lane, beside_row, beside_lane, v0, v1, v2, v3,
    out_hbm, x, y, strip, spare, beside, spread, out, sems,
):
    clear_ends(x, y, strip, spare)
    value = (v0[...] + v1[...]) + (v2[...] + v3[...])
    n = z.obs_rows
    right_weight, left_weight = beside_rows(z, got_far, got_near, z.at_obs + n)

    def spread_out(amounts, row_hot, lane_hot):
        wide = lane_hot.shape[0]
        for group, amount in enumerate(amounts):
            high, low = split(amount)
            for r in range(n):
                at = pl.ds(group * z.obs + r * 128, 128)
                for k, part in enumerate((high, low)):
                    line = jnp.broadcast_to(part[r : r + 1, :].astype(F32), (2 * SUB, 128)).astype(BF16)
                    for t in range(wide // (2 * SUB)):
                        rows = pl.ds(t * 2 * SUB, 2 * SUB)
                        spread[pl.ds(k * wide + t * 2 * SUB, 2 * SUB), at] = lane_hot[rows, at] * line
        dims = (((1,), (1,)), ((), ()))
        total = lax.dot_general(
            row_hot[...], spread[: 2 * wide, : len(amounts) * z.obs], dims, preferred_element_type=F32
        )
        return total[:, :wide] + total[:, wide:]

    field = spread_out([obs_weight[...] * value[:n]], own_row, own_lane)
    for g in range(2):
        x[pl.ds(SUB + g * z.group, z.group), :] = field[:, g * 128 : (g + 1) * 128]
    beside[...] = spread_out(
        [right_weight * value[n : 2 * n], left_weight * value[2 * n :]], beside_row, beside_lane
    )
    lane = lanes(SUB)
    part = (lane >> 4) & 3
    within = lane & 15
    outside = ((part == 1) & (within < STEPS)) | ((part == 2) & (within >= STEPS))
    for q in range(z.group // SUB):
        k, rest = divmod(q * SUB, z.short)
        value = jnp.where(outside, roll(beside[pl.ds(rest, SUB), :], -16 * k), 0.0)
        for g in range(2):
            at = g * z.group + q * SUB
            here = pl.ds(SUB + at, SUB)
            field = x[here, :]
            mine = (lane >> 6) == g
            value = jnp.where(mine & (part == 0), roll(field, EDGE + 64 * g), value)
            value = jnp.where(mine & (part == 3), roll(field, 48 + 64 * g), value)
        strip[pl.ds(SUB + q * SUB, SUB), :] = value * strip_members[pl.ds(q * SUB, SUB), :]
    here = pl.ds(SUB, z.field)
    x[here, :] = x[here, :] * (members[...].astype(F32) * weight[0:1, :])
    sweep([(x, y, coeff, z.levels), (strip, spare, strip_c, z.levels // 2)], z.rows)
    sent = []
    for part in range(z.levels // 2):
        for t in range(z.rows // SUB):
            q = part * z.rows + t * SUB
            value = strip[pl.ds(SUB + q, SUB), :]
            for g in range(2):
                at = g * z.group + q
                fixed = x[pl.ds(SUB + at, SUB), :]
                fixed = jnp.where(lane >= z.columns - STEPS, roll(value, 112 - 64 * g), fixed)
                fixed = jnp.where(lane < STEPS, roll(value, -48 - 64 * g), fixed)
                out[pl.ds(at, SUB), :] = alpha[pl.ds(at, SUB), :] + fixed
        if part % 2:
            for g in range(2):
                rows = pl.ds(g * z.group + (part - 1) * z.rows, 2 * z.rows)
                sent.append(pltpu.make_async_copy(out.at[rows, :], out_hbm.at[rows, :], sems.at[len(sent)]))
                sent[-1].start()
    for copy in sent:
        copy.wait()


def local(alpha, members, mem_weight, kappa, norm_scale, land_sea, obs_cell, obs_weight):
    shape = alpha.shape
    z = Sizes(shape[1], shape[2], shape[3], obs_cell.shape[0])
    tiles, holders = lax.axis_size("tile"), lax.axis_size("mem")
    assert tiles % 2 == 0 and holders == 4 and shape[0] == 1
    alpha = alpha.reshape(z.field, z.columns)
    members = members.reshape(z.field, z.columns)
    cell = obs_cell.reshape(z.obs_rows, 128)
    weight = obs_weight.reshape(z.obs_rows, 128)
    whole = pl.BlockSpec(memory_space=pltpu.VMEM)
    stays = pl.BlockSpec(memory_space=pltpu.HBM)
    sds = jax.ShapeDtypeStruct
    main_field = pltpu.VMEM((z.field + 2 * SUB, 128), F32)
    strip_field = pltpu.VMEM((z.group + 2 * SUB, 128), F32)
    coeff = pltpu.VMEM((5, z.rows, 128), F32)
    packed = pltpu.VMEM((z.short, 256), BF16)
    payload = sds((z.payload, 128), F32)
    limit = pltpu.CompilerParams(vmem_limit_bytes=24 << 20)
    call = functools.partial(pl.pallas_call, compiler_params=limit)
    given = (alpha, members, kappa, norm_scale, land_sea, cell, weight)
    sent_far, sent_near, *given = call(
        functools.partial(pack_kernel, z),
        out_shape=(payload, payload, *(sds(v.shape, v.dtype) for v in given)),
        in_specs=[stays] * 7,
        out_specs=(whole,) * 9,
        scratch_shapes=[pltpu.SemaphoreType.DMA((7,))],
        name="pack",
    )(*(pltpu.with_memory_space_constraint(v, pltpu.HBM) for v in given))
    alpha, members, kappa, norm_scale, land_sea, cell, weight = given
    factor = jnp.broadcast_to(mem_weight, (SUB, 128))
    near = [(i, i ^ 1) for i in range(tiles)]
    far = [(i, (i + 1) % tiles if i % 2 else (i - 1) % tiles) for i in range(tiles)]
    got_far = lax.ppermute(sent_far, "tile", far)
    got_near = lax.ppermute(sent_near, "tile", near)
    inner, own_row = call(
        functools.partial(main_kernel, z),
        out_shape=(sds((z.obs_rows, 128), F32), sds((z.group, z.obs), BF16)),
        in_specs=[whole] * 7,
        out_specs=(whole, whole),
        scratch_shapes=[main_field, coeff, main_field, pltpu.VMEM((z.group, 512), BF16)],
        name="main",
    )(alpha, members, factor, kappa, norm_scale, land_sea, cell)
    values, strip_members, strip_coeff, beside_row = call(
        functools.partial(strip_kernel, z),
        out_shape=(
            sds((3 * z.obs_rows, 128), F32),
            sds((z.group, 128), F32),
            sds((3, z.rows, 128), F32),
            sds((z.short, 2 * z.obs), BF16),
        ),
        in_specs=[whole] * 8,
        out_specs=(whole,) * 4,
        scratch_shapes=[coeff, strip_field, strip_field, packed, packed],
        name="strip",
    )(inner, members, sent_far, sent_near, got_far, got_near, cell, factor)
    others = [lax.ppermute(values, "mem", [(i, i ^ k) for i in range(holders)]) for k in range(1, holders)]
    main_c, strip_c, own_lane, beside_lane = call(
        functools.partial(ready_kernel, z),
        out_shape=(
            sds((5, z.rows, 128), F32),
            sds((5, z.rows, 128), F32),
            sds((2 * 128, z.obs), BF16),
            sds((128, 2 * z.obs), BF16),
        ),
        in_specs=[whole] * 7,
        out_specs=(whole,) * 4,
        name="ready",
    )(kappa, norm_scale, land_sea, cell, got_far, got_near, strip_coeff)
    product = call(
        functools.partial(adjoint_kernel, z),
        out_shape=sds((z.field, z.columns), F32),
        in_specs=[whole] * 17,
        out_specs=stays,
        scratch_shapes=[
            main_field,
            main_field,
            strip_field,
            strip_field,
            pltpu.VMEM((z.short, 128), F32),
            pltpu.VMEM((512, 2 * z.obs), BF16),
            pltpu.VMEM((z.field, 128), F32),
            pltpu.SemaphoreType.DMA((z.levels // 2,)),
        ],
        name="adjoint",
    )(
        alpha, members, factor, weight, got_far, got_near, strip_members, main_c, strip_c,
        own_row, own_lane, beside_row, beside_lane, values, *others,
    )
    return product.reshape(shape)


def solution(mesh):
    placed = (
        P("mem", None, None, "tile"),
        P("mem", None, None, "tile"),
        P("mem"),
        P(None, "tile"),
        P(None, "tile"),
        P(None, "tile"),
        P("tile"),
        P("tile"),
    )
    return jax.shard_map(
        local, mesh=mesh, in_specs=placed, out_specs=P("mem", None, None, "tile"), check_vma=False
    )
```

```python
import functools

import jax
import jax.numpy as jnp
from jax import lax
from jax.experimental import pallas as pl
from jax.experimental.pallas import tpu as pltpu
from jax.sharding import PartitionSpec as P

STEPS = 8
SUB = 8
EDGE = 2 * STEPS
F32 = jnp.float32
BF16 = jnp.bfloat16


def div_mod(value, size):
    if size & (size - 1) == 0:
        return value >> (size.bit_length() - 1), value & (size - 1)
    return lax.div(value, size), lax.rem(value, size)


def roll(value, shift, axis=1):
    shift %= value.shape[axis]
    return pltpu.roll(value, shift, axis) if shift else value


def lanes(rows):
    return lax.broadcasted_iota(jnp.int32, (rows, 128), 1)


def split(value):
    high = value.astype(BF16)
    return high, (value - high.astype(F32)).astype(BF16)


class Sizes:
    def __init__(self, levels, rows, columns, obs):
        self.levels, self.rows, self.columns, self.obs = levels, rows, columns, obs
        assert columns == 128 and levels == 16 and rows % 16 == 0 and obs % 256 == 0 and STEPS == 8
        self.field = levels * rows
        self.group = self.field // 2
        self.short = self.field // 8
        self.tiles = rows // SUB
        assert self.tiles == 8
        self.at_members = self.short
        self.at_coeff = self.at_members + rows
        self.at_obs = self.at_coeff + 3 * SUB
        self.obs_rows = obs // 128
        self.payload = self.at_obs + 2 * self.obs_rows


def overlay(pieces, window):
    value = pieces[0]
    for k in range(1, len(pieces)):
        value = jnp.where(window == k, pieces[k], value)
    return value


def pack_kernel(
    z, alpha_hbm, members_hbm, kappa_hbm, scale_hbm, ocean_hbm, cell_hbm, weight_hbm,
    out_right, out_left, alpha, members, kappa, scale, ocean, cell, weight, sems,
):
    pairs = (
        (members_hbm, members), (alpha_hbm, alpha), (kappa_hbm, kappa), (scale_hbm, scale), (ocean_hbm, ocean),
        (cell_hbm, cell), (weight_hbm, weight),
    )
    copies = [pltpu.make_async_copy(a, b, sems.at[k]) for k, (a, b) in enumerate(pairs)]
    for copy in copies:
        copy.start()

    def put(where, right, left):
        out_right[where, :] = right
        out_left[where, :] = left

    for copy in copies[2:]:
        copy.wait()
    lane = lanes(SUB)
    for k, ref in enumerate((kappa, scale, ocean)):
        right, left = [], []
        for t in range(z.tiles):
            value = ref[pl.ds(t * SUB, SUB), :].astype(F32)
            right.append(roll(value, EDGE * (t + 1)))
            left.append(roll(value, EDGE * t))
        put(pl.ds(z.at_coeff + k * SUB, SUB), overlay(right, lane >> 4), overlay(left, lane >> 4))
    n = z.obs_rows
    for at, value in ((z.at_obs, cell[...].astype(F32)), (z.at_obs + n, weight[...])):
        put(pl.ds(at, n), value, value)
    copies[0].wait()
    block = 2 * SUB
    lane = lanes(block)
    for t in range(z.rows // block):
        right, left = [], []
        for g in range(2):
            for part in range(SUB):
                value = members[pl.ds(g * z.group + part * z.rows + t * block, block), :].astype(F32)
                base = 64 * g + STEPS * part
                right.append(roll(value, base + STEPS))
                left.append(roll(value, base))
        put(pl.ds(z.at_members + t * block, block), overlay(right, lane >> 3), overlay(left, lane >> 3))
    copies[1].wait()
    for t in range(z.short // block):
        right, left = [], []
        for g in range(2):
            for h in range(4):
                value = alpha[pl.ds(g * z.group + h * z.short + t * block, block), :]
                base = 64 * g + EDGE * h
                right.append(roll(value, base + EDGE))
                left.append(roll(value, base))
        put(pl.ds(t * block, block), overlay(right, lane >> 4), overlay(left, lane >> 4))


def up(value):
    return roll(value, -1, 0)


def down(value):
    return roll(value, 1, 0)


def coefficients(kappa, scale, ocean, forward):
    row = lax.broadcasted_iota(jnp.int32, kappa.shape, 0)
    north = 0.5 * (kappa + up(kappa)) * ocean * up(ocean)
    north = jnp.where(row == kappa.shape[0] - 1, 0.0, north)
    east = 0.5 * (kappa + roll(kappa, -1)) * ocean * roll(ocean, -1)
    west, south = roll(east, 1), down(north)
    centre = 1.0 - (east + west) - (north + south)
    if forward:
        return (
            centre * scale,
            east * roll(scale, -1),
            west * roll(scale, 1),
            north * up(scale),
            south * down(scale),
        )
    return tuple(scale * c for c in (centre, east, west, north, south))


def put_coefficients(ref, values):
    for k, value in enumerate(values):
        ref[k] = value


def step_rows(source, target, coeff, rows, levels):
    for t in range(rows // SUB):
        c = [coeff[k, pl.ds(t * SUB, SUB), :] for k in range(5)]
        for level in range(levels):
            at = SUB + level * rows + t * SUB
            u = source[pl.ds(at, SUB), :]
            along = c[3] * source[pl.ds(at + 1, SUB), :] + c[4] * source[pl.ds(at - 1, SUB), :]
            across = c[1] * roll(u, -1) + c[2] * roll(u, 1)
            target[pl.ds(at, SUB), :] = c[0] * u + across + along


def clear_ends(*buffers):
    for ref in buffers:
        zero = jnp.zeros((SUB, 128), F32)
        ref[pl.ds(0, SUB), :] = zero
        ref[pl.ds(ref.shape[0] - SUB, SUB), :] = zero


def sweep(fields, rows):
    def two_steps(_, carry):
        for x, y, coeff, levels in fields:
            step_rows(x, y, coeff, rows, levels)
        for x, y, coeff, levels in fields:
            step_rows(y, x, coeff, rows, levels)
        return carry

    lax.fori_loop(0, STEPS // 2, two_steps, 0)


def cell_parts(z, cell):
    level, rest = div_mod(cell, z.rows * z.columns)
    row, column = div_mod(rest, z.columns)
    return level >> 3, level & 7, row, column


def own_index(z, cell):
    group, part, row, column = cell_parts(z, cell)
    return part * z.rows + row, group * 128 + column


def edge_index(z, cell, windows):
    group, part, row, column = cell_parts(z, cell)
    inside, lane = False, 0
    for first, at in windows:
        here = (column >= first) & (column < first + STEPS)
        inside = here | inside
        lane = jnp.where(here, at - first, lane)
    lane = lane + column + 64 * group + 16 * (part >> 1)
    return jnp.where(inside, (part & 1) * z.rows + row, -1), lane & 127


def own_edges(z):
    return (0, 48), (z.columns - STEPS, 8)


def windows_of(z):
    return own_edges(z), ((0, 16),), ((z.columns - STEPS, 40),)


def quarters(unit, first, second):
    even, odd = (first, second) if first % 2 == 0 else (second, first)
    return jnp.where((unit & 1) == 0, ((unit - even) >> 1) & 3, ((unit - odd) >> 1) & 3)


def one_hot(index, size):
    rows = lax.broadcasted_iota(jnp.int32, (size, index.shape[1]), 0)
    return jnp.where(rows == index, 1.0, 0.0).astype(BF16)


def read_off(field, hot, j):
    value = lax.dot_general(field, hot, (((0,), (0,)), ((), ())), preferred_element_type=F32)
    n = value.shape[0] // 2
    value = value[:n] + value[n:]
    rows = lax.broadcasted_iota(jnp.int32, value.shape, 0)
    return jnp.sum(jnp.where(rows == j, value, 0.0), axis=0, keepdims=True)


def gather(z, out, at, field, cell, index, keep=None, start=0):
    for n in range(z.obs_rows // 2):
        row = jnp.concatenate([cell[2 * n : 2 * n + 1, :], cell[2 * n + 1 : 2 * n + 2, :]], axis=1)
        i, j = index(row)
        hot = one_hot(i, field.shape[0])
        if keep is not None:
            keep[:, pl.ds(start + 256 * n, 256)] = hot
        value = read_off(field, hot, j)
        out[at + 2 * n : at + 2 * n + 1, :] = value[:, :128]
        out[at + 2 * n + 1 : at + 2 * n + 2, :] = value[:, 128:]


def forward_sweep(z, alpha, kappa, scale, ocean, coeff, x, y):
    put_coefficients(coeff, coefficients(kappa[...], scale[...], ocean[...].astype(F32), True))
    clear_ends(x, y)
    x[pl.ds(SUB, z.field), :] = alpha[...]
    sweep([(x, y, coeff, z.levels)], z.rows)


def main_kernel(z, alpha, members, kappa, scale, ocean, cell, out, hot, x, coeff, y, both):
    forward_sweep(z, alpha, kappa, scale, ocean, coeff, x, y)
    lane = lanes(z.group)
    inner = (lane >= STEPS) & (lane < z.columns - STEPS)
    for g in range(2):
        rows = pl.ds(g * z.group, z.group)
        value = x[pl.ds(SUB + g * z.group, z.group), :] * members[rows, :].astype(F32)
        high, low = split(jnp.where(inner, value, 0.0))
        both[:, pl.ds(g * 128, 128)] = high
        both[:, pl.ds(256 + g * 128, 128)] = low
    gather(z, out, 0, both[...], cell[...], lambda c: own_index(z, c), hot)


def strip_kernel(
    z, inner, members, own_right, own_left, from_left, from_right, cell, weight,
    out, strip_members, strip_coeff, hot, coeff, x, y, outer, beside,
):

    def parts(rows):
        return own_right[rows, :], from_right[rows, :], from_left[rows, :], own_left[rows, :]

    clear_ends(x, y)
    lane = lanes(SUB)
    part_of, side = (lane >> 4) & 3, lane >> 6
    for k in range(3):
        four = parts(pl.ds(z.at_coeff + k * SUB, SUB))
        for t in range(z.tiles):
            pieces = [roll(four[p], EDGE * p + 64 * g - EDGE * t) for g in range(2) for p in range(4)]
            strip_coeff[k, pl.ds(t * SUB, SUB), :] = overlay(pieces, lane >> 4)
    for q in range(z.short // SUB):
        four = parts(pl.ds(q * SUB, SUB))
        for h in range(4):
            pieces = [roll(four[p], EDGE * (p - h)) for p in range(4)]
            x[pl.ds(SUB + h * z.short + q * SUB, SUB), :] = overlay(pieces, part_of)
    block = 2 * SUB
    wide_lane = lanes(block)
    for t in range(z.rows // block):
        rows = pl.ds(z.at_members + t * block, block)
        _, right, left, _ = parts(rows)
        for part in range(SUB):
            at = part * z.rows + t * block
            value = jnp.where(
                (wide_lane & 32) == 0,
                roll(right, EDGE - STEPS * part),
                roll(left, 2 * EDGE + STEPS - STEPS * part),
            )
            for g in range(2):
                own = members[pl.ds(g * z.group + at, block), :].astype(F32)
                mine = (wide_lane >> 6) == g
                inside = (wide_lane >> 4) & 3
                value = jnp.where(mine & (inside == 0), roll(own, EDGE + 64 * g), value)
                value = jnp.where(mine & (inside == 3), roll(own, 48 + 64 * g), value)
            strip_members[pl.ds(at, block), :] = value
    put_coefficients(coeff, coefficients(strip_coeff[0], strip_coeff[1], strip_coeff[2], True))
    sweep([(x, y, coeff, z.levels // 2)], z.rows)
    unit = lanes(z.short) >> 3
    for ref, first, second in ((outer, 1, 6), (beside, 2, 5)):
        quarter = quarters(unit, first, second)
        pieces = []
        for k in range(4):
            rows = pl.ds(k * z.short, z.short)
            pieces.append(roll(x[pl.ds(SUB + k * z.short, z.short), :] * strip_members[rows, :], 16 * k))
        value = overlay(pieces, quarter)
        if ref is outer:
            rights = ((0, value),)
        else:
            rights = ((0, jnp.where((unit & 1) == 0, value, 0.0)), (z.short, jnp.where((unit & 1) == 1, value, 0.0)))
        for at, value in rights:
            high, low = split(value)
            ref[pl.ds(at, z.short), :128] = high
            ref[pl.ds(at, z.short), 128:] = low
    n = z.obs_rows
    own_window, right_window, left_window = windows_of(z)
    gather(z, out, 0, outer[...], cell[...], lambda c: edge_index(z, c, own_window))
    out[:n, :] = (out[:n, :] + inner[...]) * weight[0:1, :]
    right = from_right[pl.ds(z.at_obs, n), :].astype(jnp.int32)
    left = from_left[pl.ds(z.at_obs, n), :].astype(jnp.int32)
    field = beside[...]
    for r in range(0, n, 2):
        pair = lambda v: jnp.concatenate([v[r : r + 1, :], v[r + 1 : r + 2, :]], axis=1)
        i_right, j_right = edge_index(z, pair(right), right_window)
        i_left, j_left = edge_index(z, pair(left), left_window)
        both = jnp.concatenate([one_hot(i_right, z.short), one_hot(i_left, z.short)], axis=0)
        hot[:, pl.ds(r * 128, 256)] = both
        value = lax.dot_general(field, both, (((0,), (0,)), ((), ())), preferred_element_type=F32)
        value = value[:128] + value[128:]
        rows = lax.broadcasted_iota(jnp.int32, (SUB, 256), 0)
        for side, j in enumerate((j_right, j_left)):
            total = None
            for t in range(side, 16, 2):
                piece = jnp.where(rows == j - t * SUB, value[t * SUB : (t + 1) * SUB], 0.0)
                total = piece if total is None else total + piece
            total = jnp.sum(total, axis=0, keepdims=True) * weight[0:1, 0:1]
            at = (1 + side) * n + r
            out[at : at + 1, :] = total[:, :128]
            out[at + 1 : at + 2, :] = total[:, 128:]


def ready_kernel(z, kappa, scale, ocean, cell, from_left, from_right, strip_coeff, coeff, strip_c, own_lane, beside_lane):
    put_coefficients(coeff, coefficients(kappa[...], scale[...], ocean[...].astype(F32), False))
    put_coefficients(strip_c, coefficients(strip_coeff[0], strip_coeff[1], strip_coeff[2], False))
    _, right_window, left_window = windows_of(z)
    n = z.obs_rows
    right = from_right[pl.ds(z.at_obs, n), :].astype(jnp.int32)
    left = from_left[pl.ds(z.at_obs, n), :].astype(jnp.int32)
    rows = lax.broadcasted_iota(jnp.int32, (128, 128), 0)
    for r in range(n):
        at = pl.ds(r * 128, 128)
        own_lane[:, at] = one_hot(own_index(z, cell[r : r + 1, :])[1], 256)
        j_right = edge_index(z, right[r : r + 1, :], right_window)[1]
        j_left = edge_index(z, left[r : r + 1, :], left_window)[1]
        lane = jnp.where((rows & SUB) == 0, j_right, j_left)
        beside_lane[:, at] = jnp.where(rows == lane, 1.0, 0.0).astype(BF16)


def adjoint_kernel(
    z, alpha, members, weight, obs_weight, from_left, from_right, strip_members, coeff, strip_c,
    own_row, own_lane, beside_row, beside_lane, v0, v1, v2, v3,
    out_hbm, x, y, strip, spare, beside, spread, out, sems,
):
    clear_ends(x, y, strip, spare)
    value = (v0[...] + v1[...]) + (v2[...] + v3[...])
    n = z.obs_rows
    weights = pl.ds(z.at_obs + n, n)

    def spread_out(tops, bottoms, row_hot, lane_hot):
        wide = lane_hot.shape[0]
        for k, (top, bottom) in enumerate(zip(split(tops), split(bottoms))):
            for r in range(n):
                at = pl.ds(r * 128, 128)
                line = jnp.concatenate(
                    [jnp.broadcast_to(v[r : r + 1, :].astype(F32), (SUB, 128)) for v in (top, bottom)], axis=0
                ).astype(BF16)
                for t in range(wide // (2 * SUB)):
                    rows = pl.ds(t * 2 * SUB, 2 * SUB)
                    spread[pl.ds(k * wide + t * 2 * SUB, 2 * SUB), at] = lane_hot[rows, at] * line
        dims = (((1,), (1,)), ((), ()))
        total = lax.dot_general(row_hot[...], spread[: 2 * wide, :], dims, preferred_element_type=F32)
        return total[:, :wide] + total[:, wide:]

    amount = obs_weight[...] * value[:n]
    field = spread_out(amount, amount, own_row, own_lane)
    for g in range(2):
        x[pl.ds(SUB + g * z.group, z.group), :] = field[:, g * 128 : (g + 1) * 128]
    right, left = from_right[weights, :] * value[n : 2 * n], from_left[weights, :] * value[2 * n :]
    field = spread_out(right, left, beside_row, beside_lane)
    beside[...] = jnp.where((lanes(z.short) & SUB) == 0, field[: z.short], field[z.short :])
    lane = lanes(SUB)
    part = (lane >> 4) & 3
    within = lane & 15
    outside = ((part == 1) & (within < STEPS)) | ((part == 2) & (within >= STEPS))
    for q in range(z.group // SUB):
        k, rest = divmod(q * SUB, z.short)
        value = jnp.where(outside, roll(beside[pl.ds(rest, SUB), :], -16 * k), 0.0)
        for g in range(2):
            at = g * z.group + q * SUB
            here = pl.ds(SUB + at, SUB)
            field = x[here, :]
            mine = (lane >> 6) == g
            value = jnp.where(mine & (part == 0), roll(field, EDGE + 64 * g), value)
            value = jnp.where(mine & (part == 3), roll(field, 48 + 64 * g), value)
        strip[pl.ds(SUB + q * SUB, SUB), :] = value * (strip_members[pl.ds(q * SUB, SUB), :] * weight[...])
    here = pl.ds(SUB, z.field)
    x[here, :] = x[here, :] * (members[...].astype(F32) * weight[0:1, :])
    sweep([(x, y, coeff, z.levels), (strip, spare, strip_c, z.levels // 2)], z.rows)
    sent = []
    for part in range(z.levels // 2):
        for t in range(z.rows // SUB):
            q = part * z.rows + t * SUB
            value = strip[pl.ds(SUB + q, SUB), :]
            for g in range(2):
                at = g * z.group + q
                fixed = x[pl.ds(SUB + at, SUB), :]
                fixed = jnp.where(lane >= z.columns - STEPS, roll(value, 112 - 64 * g), fixed)
                fixed = jnp.where(lane < STEPS, roll(value, -48 - 64 * g), fixed)
                out[pl.ds(at, SUB), :] = alpha[pl.ds(at, SUB), :] + fixed
        if part % 2:
            for g in range(2):
                rows = pl.ds(g * z.group + (part - 1) * z.rows, 2 * z.rows)
                sent.append(pltpu.make_async_copy(out.at[rows, :], out_hbm.at[rows, :], sems.at[len(sent)]))
                sent[-1].start()
    for copy in sent:
        copy.wait()


def local(alpha, members, mem_weight, kappa, norm_scale, land_sea, obs_cell, obs_weight):
    shape = alpha.shape
    z = Sizes(shape[1], shape[2], shape[3], obs_cell.shape[0])
    tiles, holders = lax.axis_size("tile"), lax.axis_size("mem")
    assert holders == 4 and shape[0] == 1
    alpha = alpha.reshape(z.field, z.columns)
    members = members.reshape(z.field, z.columns)
    cell = obs_cell.reshape(z.obs_rows, 128)
    weight = obs_weight.reshape(z.obs_rows, 128)
    whole = pl.BlockSpec(memory_space=pltpu.VMEM)
    stays = pl.BlockSpec(memory_space=pltpu.HBM)
    sds = jax.ShapeDtypeStruct
    main_field = pltpu.VMEM((z.field + 2 * SUB, 128), F32)
    strip_field = pltpu.VMEM((z.group + 2 * SUB, 128), F32)
    coeff = pltpu.VMEM((5, z.rows, 128), F32)
    packed = pltpu.VMEM((z.short, 256), BF16)
    payload = sds((z.payload, 128), F32)
    limit = pltpu.CompilerParams(vmem_limit_bytes=24 << 20)
    call = functools.partial(pl.pallas_call, compiler_params=limit)
    given = (alpha, members, kappa, norm_scale, land_sea, cell, weight)
    sent_right, sent_left, *given = call(
        functools.partial(pack_kernel, z),
        out_shape=(payload, payload, *(sds(v.shape, v.dtype) for v in given)),
        in_specs=[stays] * 7,
        out_specs=(whole,) * 9,
        scratch_shapes=[pltpu.SemaphoreType.DMA((7,))],
        name="pack",
    )(*(pltpu.with_memory_space_constraint(v, pltpu.HBM) for v in given))
    alpha, members, kappa, norm_scale, land_sea, cell, weight = given
    up_ring = [(i, (i + 1) % tiles) for i in range(tiles)]
    from_left = lax.ppermute(sent_right, "tile", up_ring)
    from_right = lax.ppermute(sent_left, "tile", [(b, a) for a, b in up_ring])
    inner, own_row = call(
        functools.partial(main_kernel, z),
        out_shape=(sds((z.obs_rows, 128), F32), sds((z.group, z.obs), BF16)),
        in_specs=[whole] * 6,
        out_specs=(whole, whole),
        scratch_shapes=[main_field, coeff, main_field, pltpu.VMEM((z.group, 512), BF16)],
        name="main",
    )(alpha, members, kappa, norm_scale, land_sea, cell)
    mem_weight, inner = lax.optimization_barrier((mem_weight, inner))
    factor = jnp.broadcast_to(mem_weight, (SUB, 128))
    values, strip_members, strip_coeff, beside_row = call(
        functools.partial(strip_kernel, z),
        out_shape=(
            sds((3 * z.obs_rows, 128), F32),
            sds((z.group, 128), F32),
            sds((3, z.rows, 128), F32),
            sds((2 * z.short, z.obs), BF16),
        ),
        in_specs=[whole] * 8,
        out_specs=(whole,) * 4,
        scratch_shapes=[coeff, strip_field, strip_field, packed, pltpu.VMEM((2 * z.short, 256), BF16)],
        name="strip",
    )(inner, members, sent_right, sent_left, from_left, from_right, cell, factor)
    others = [lax.ppermute(values, "mem", [(i, i ^ k) for i in range(holders)]) for k in range(1, holders)]
    main_c, strip_c, own_lane, beside_lane = call(
        functools.partial(ready_kernel, z),
        out_shape=(
            sds((5, z.rows, 128), F32),
            sds((5, z.rows, 128), F32),
            sds((2 * 128, z.obs), BF16),
            sds((128, z.obs), BF16),
        ),
        in_specs=[whole] * 7,
        out_specs=(whole,) * 4,
        name="ready",
    )(kappa, norm_scale, land_sea, cell, from_left, from_right, strip_coeff)
    product = call(
        functools.partial(adjoint_kernel, z),
        out_shape=sds((z.field, z.columns), F32),
        in_specs=[whole] * 17,
        out_specs=stays,
        scratch_shapes=[
            main_field,
            main_field,
            strip_field,
            strip_field,
            pltpu.VMEM((z.short, 128), F32),
            pltpu.VMEM((512, z.obs), BF16),
            pltpu.VMEM((z.field, 128), F32),
            pltpu.SemaphoreType.DMA((z.levels // 2,)),
        ],
        name="adjoint",
    )(
        alpha, members, factor, weight, from_left, from_right, strip_members, main_c, strip_c,
        own_row, own_lane, beside_row, beside_lane, values, *others,
    )
    return product.reshape(shape)


def solution(mesh):
    placed = (
        P("mem", None, None, "tile"),
        P("mem", None, None, "tile"),
        P("mem"),
        P(None, "tile"),
        P(None, "tile"),
        P(None, "tile"),
        P("tile"),
        P("tile"),
    )
    return jax.shard_map(
        local, mesh=mesh, in_specs=placed, out_specs=P("mem", None, None, "tile"), check_vma=False
    )
```

```python
import functools

import jax
import jax.numpy as jnp
from jax import lax
from jax.experimental import pallas as pl
from jax.experimental.pallas import tpu as pltpu
from jax.sharding import PartitionSpec as P

STEPS = 8
SUB = 8
EDGE = 2 * STEPS
ASSISTED = 5
F32 = jnp.float32
BF16 = jnp.bfloat16


def div_mod(value, size):
    if size & (size - 1) == 0:
        return value >> (size.bit_length() - 1), value & (size - 1)
    return lax.div(value, size), lax.rem(value, size)


def roll(value, shift, axis=1):
    shift %= value.shape[axis]
    return pltpu.roll(value, shift, axis) if shift else value


def lanes(rows):
    return lax.broadcasted_iota(jnp.int32, (rows, 128), 1)


def split(value):
    high = value.astype(BF16)
    return high, (value - high.astype(F32)).astype(BF16)


class Sizes:
    def __init__(self, levels, rows, columns, obs):
        self.levels, self.rows, self.columns, self.obs = levels, rows, columns, obs
        assert columns == 128 and levels == 16 and rows % 16 == 0 and obs % 256 == 0 and STEPS == 8
        self.field = levels * rows
        self.group = self.field // 2
        self.short = self.field // 8
        self.tiles = rows // SUB
        assert self.tiles == 8
        self.at_members = self.short
        self.at_coeff = self.at_members + rows
        self.at_obs = self.at_coeff + 3 * SUB
        self.obs_rows = obs // 128
        self.payload = self.at_obs + 2 * self.obs_rows


def overlay(pieces, window):
    value = pieces[0]
    for k in range(1, len(pieces)):
        value = jnp.where(window == k, pieces[k], value)
    return value


def pack_kernel(
    z, alpha_hbm, members_hbm, kappa_hbm, scale_hbm, ocean_hbm, cell_hbm, weight_hbm,
    out_right, out_left, alpha, members, kappa, scale, ocean, cell, weight, sems,
):
    pairs = (
        (members_hbm, members), (alpha_hbm, alpha), (kappa_hbm, kappa), (scale_hbm, scale), (ocean_hbm, ocean),
        (cell_hbm, cell), (weight_hbm, weight),
    )
    copies = [pltpu.make_async_copy(a, b, sems.at[k]) for k, (a, b) in enumerate(pairs)]
    for copy in copies:
        copy.start()

    def put(where, right, left):
        out_right[where, :] = right
        out_left[where, :] = left

    for copy in copies[2:]:
        copy.wait()
    lane = lanes(SUB)
    for k, ref in enumerate((kappa, scale, ocean)):
        right, left = [], []
        for t in range(z.tiles):
            value = ref[pl.ds(t * SUB, SUB), :].astype(F32)
            right.append(roll(value, EDGE * (t + 1)))
            left.append(roll(value, EDGE * t))
        put(pl.ds(z.at_coeff + k * SUB, SUB), overlay(right, lane >> 4), overlay(left, lane >> 4))
    n = z.obs_rows
    for at, value in ((z.at_obs, cell[...].astype(F32)), (z.at_obs + n, weight[...])):
        put(pl.ds(at, n), value, value)
    copies[0].wait()
    block = 2 * SUB
    lane = lanes(block)
    for t in range(z.rows // block):
        right, left = [], []
        for g in range(2):
            for part in range(SUB):
                value = members[pl.ds(g * z.group + part * z.rows + t * block, block), :].astype(F32)
                base = 64 * g + STEPS * part
                right.append(roll(value, base + STEPS))
                left.append(roll(value, base))
        put(pl.ds(z.at_members + t * block, block), overlay(right, lane >> 3), overlay(left, lane >> 3))
    copies[1].wait()
    for t in range(z.short // block):
        right, left = [], []
        for g in range(2):
            for h in range(4):
                value = alpha[pl.ds(g * z.group + h * z.short + t * block, block), :]
                base = 64 * g + EDGE * h
                right.append(roll(value, base + EDGE))
                left.append(roll(value, base))
        put(pl.ds(t * block, block), overlay(right, lane >> 4), overlay(left, lane >> 4))


def up(value):
    return roll(value, -1, 0)


def down(value):
    return roll(value, 1, 0)


def coefficients(kappa, scale, ocean, forward):
    row = lax.broadcasted_iota(jnp.int32, kappa.shape, 0)
    north = 0.5 * (kappa + up(kappa)) * ocean * up(ocean)
    north = jnp.where(row == kappa.shape[0] - 1, 0.0, north)
    east = 0.5 * (kappa + roll(kappa, -1)) * ocean * roll(ocean, -1)
    west, south = roll(east, 1), down(north)
    centre = 1.0 - (east + west) - (north + south)
    if forward:
        return (
            centre * scale,
            east * roll(scale, -1),
            west * roll(scale, 1),
            north * up(scale),
            south * down(scale),
        )
    return tuple(scale * c for c in (centre, east, west, north, south))


def put_coefficients(ref, values):
    for k, value in enumerate(values):
        ref[k] = value


def shift_matrix():
    row = lax.broadcasted_iota(jnp.int32, (256, 256), 0)
    column = lax.broadcasted_iota(jnp.int32, (256, 256), 1)
    wanted = jnp.where(column < 128, column + 1, column - 1)
    return jnp.where((row & 127) == (wanted & 127), 1.0, 0.0).astype(BF16)


def step_rows(source, target, coeff, rows, levels, shift):
    assisted = 0
    if shift is not None:
        assisted = ASSISTED
        both = jnp.concatenate(split(source[pl.ds(SUB, assisted * rows), :]), axis=1)
        beside = jnp.dot(both, shift[...], preferred_element_type=F32)
    for t in range(rows // SUB):
        c = [coeff[k, pl.ds(t * SUB, SUB), :] for k in range(5)]
        for level in range(levels):
            r = level * rows + t * SUB
            at = SUB + r
            u = source[pl.ds(at, SUB), :]
            along = c[3] * source[pl.ds(at + 1, SUB), :] + c[4] * source[pl.ds(at - 1, SUB), :]
            if level < assisted:
                across = c[1] * beside[r : r + SUB, :128] + c[2] * beside[r : r + SUB, 128:]
            else:
                across = c[1] * roll(u, -1) + c[2] * roll(u, 1)
            target[pl.ds(at, SUB), :] = c[0] * u + across + along


def clear_ends(*buffers):
    for ref in buffers:
        zero = jnp.zeros((SUB, 128), F32)
        ref[pl.ds(0, SUB), :] = zero
        ref[pl.ds(ref.shape[0] - SUB, SUB), :] = zero


def sweep(fields, rows):
    for step in range(STEPS):
        for x, y, coeff, levels, shift in fields:
            source, target = (y, x) if step % 2 else (x, y)
            step_rows(source, target, coeff, rows, levels, shift)


def cell_parts(z, cell):
    level, rest = div_mod(cell, z.rows * z.columns)
    row, column = div_mod(rest, z.columns)
    return level >> 3, level & 7, row, column


def own_index(z, cell):
    group, part, row, column = cell_parts(z, cell)
    return part * z.rows + row, group * 128 + column


def edge_index(z, cell, windows):
    group, part, row, column = cell_parts(z, cell)
    inside, lane = False, 0
    for first, at in windows:
        here = (column >= first) & (column < first + STEPS)
        inside = here | inside
        lane = jnp.where(here, at - first, lane)
    lane = lane + column + 64 * group + 16 * (part >> 1)
    return jnp.where(inside, (part & 1) * z.rows + row, -1), lane & 127


def own_edges(z):
    return (0, 48), (z.columns - STEPS, 8)


def windows_of(z):
    return own_edges(z), ((0, 16),), ((z.columns - STEPS, 40),)


def quarters(unit, first, second):
    even, odd = (first, second) if first % 2 == 0 else (second, first)
    return jnp.where((unit & 1) == 0, ((unit - even) >> 1) & 3, ((unit - odd) >> 1) & 3)


def one_hot(index, size):
    rows = lax.broadcasted_iota(jnp.int32, (size, index.shape[1]), 0)
    return jnp.where(rows == index, 1.0, 0.0).astype(BF16)


def read_off(field, hot, j):
    value = lax.dot_general(field, hot, (((0,), (0,)), ((), ())), preferred_element_type=F32)
    n = value.shape[0] // 2
    value = value[:n] + value[n:]
    rows = lax.broadcasted_iota(jnp.int32, value.shape, 0)
    return jnp.sum(jnp.where(rows == j, value, 0.0), axis=0, keepdims=True)


def gather(z, out, at, field, cell, index, keep=None, start=0):
    for n in range(z.obs_rows // 2):
        row = jnp.concatenate([cell[2 * n : 2 * n + 1, :], cell[2 * n + 1 : 2 * n + 2, :]], axis=1)
        i, j = index(row)
        hot = one_hot(i, field.shape[0])
        if keep is not None:
            keep[:, pl.ds(start + 256 * n, 256)] = hot
        value = read_off(field, hot, j)
        out[at + 2 * n : at + 2 * n + 1, :] = value[:, :128]
        out[at + 2 * n + 1 : at + 2 * n + 2, :] = value[:, 128:]


def forward_sweep(z, alpha, kappa, scale, ocean, coeff, x, y, shift):
    put_coefficients(coeff, coefficients(kappa[...], scale[...], ocean[...].astype(F32), True))
    clear_ends(x, y)
    x[pl.ds(SUB, z.field), :] = alpha[...]
    shift[...] = shift_matrix()
    sweep([(x, y, coeff, z.levels, shift)], z.rows)


def main_kernel(z, alpha, members, kappa, scale, ocean, cell, out, hot, x, coeff, y, both, shift):
    forward_sweep(z, alpha, kappa, scale, ocean, coeff, x, y, shift)
    lane = lanes(z.group)
    inner = (lane >= STEPS) & (lane < z.columns - STEPS)
    for g in range(2):
        rows = pl.ds(g * z.group, z.group)
        value = x[pl.ds(SUB + g * z.group, z.group), :] * members[rows, :].astype(F32)
        high, low = split(jnp.where(inner, value, 0.0))
        both[:, pl.ds(g * 128, 128)] = high
        both[:, pl.ds(256 + g * 128, 128)] = low
    gather(z, out, 0, both[...], cell[...], lambda c: own_index(z, c), hot)


def strip_kernel(
    z, inner, members, own_right, own_left, from_left, from_right, cell, weight,
    out, strip_members, strip_coeff, hot, coeff, x, y, outer, beside,
):

    def parts(rows):
        return own_right[rows, :], from_right[rows, :], from_left[rows, :], own_left[rows, :]

    clear_ends(x, y)
    lane = lanes(SUB)
    part_of, side = (lane >> 4) & 3, lane >> 6
    for k in range(3):
        four = parts(pl.ds(z.at_coeff + k * SUB, SUB))
        for t in range(z.tiles):
            pieces = [roll(four[p], EDGE * p + 64 * g - EDGE * t) for g in range(2) for p in range(4)]
            strip_coeff[k, pl.ds(t * SUB, SUB), :] = overlay(pieces, lane >> 4)
    for q in range(z.short // SUB):
        four = parts(pl.ds(q * SUB, SUB))
        for h in range(4):
            pieces = [roll(four[p], EDGE * (p - h)) for p in range(4)]
            x[pl.ds(SUB + h * z.short + q * SUB, SUB), :] = overlay(pieces, part_of)
    block = 2 * SUB
    wide_lane = lanes(block)
    for t in range(z.rows // block):
        rows = pl.ds(z.at_members + t * block, block)
        _, right, left, _ = parts(rows)
        for part in range(SUB):
            at = part * z.rows + t * block
            value = jnp.where(
                (wide_lane & 32) == 0,
                roll(right, EDGE - STEPS * part),
                roll(left, 2 * EDGE + STEPS - STEPS * part),
            )
            for g in range(2):
                own = members[pl.ds(g * z.group + at, block), :].astype(F32)
                mine = (wide_lane >> 6) == g
                inside = (wide_lane >> 4) & 3
                value = jnp.where(mine & (inside == 0), roll(own, EDGE + 64 * g), value)
                value = jnp.where(mine & (inside == 3), roll(own, 48 + 64 * g), value)
            strip_members[pl.ds(at, block), :] = value
    put_coefficients(coeff, coefficients(strip_coeff[0], strip_coeff[1], strip_coeff[2], True))
    sweep([(x, y, coeff, z.levels // 2, None)], z.rows)
    unit = lanes(z.short) >> 3
    for ref, first, second in ((outer, 1, 6), (beside, 2, 5)):
        quarter = quarters(unit, first, second)
        pieces = []
        for k in range(4):
            rows = pl.ds(k * z.short, z.short)
            pieces.append(roll(x[pl.ds(SUB + k * z.short, z.short), :] * strip_members[rows, :], 16 * k))
        value = overlay(pieces, quarter)
        if ref is outer:
            rights = ((0, value),)
        else:
            rights = ((0, jnp.where((unit & 1) == 0, value, 0.0)), (z.short, jnp.where((unit & 1) == 1, value, 0.0)))
        for at, value in rights:
            high, low = split(value)
            ref[pl.ds(at, z.short), :128] = high
            ref[pl.ds(at, z.short), 128:] = low
    n = z.obs_rows
    own_window, right_window, left_window = windows_of(z)
    gather(z, out, 0, outer[...], cell[...], lambda c: edge_index(z, c, own_window))
    out[:n, :] = (out[:n, :] + inner[...]) * weight[0:1, :]
    right = from_right[pl.ds(z.at_obs, n), :].astype(jnp.int32)
    left = from_left[pl.ds(z.at_obs, n), :].astype(jnp.int32)
    field = beside[...]
    for r in range(0, n, 2):
        pair = lambda v: jnp.concatenate([v[r : r + 1, :], v[r + 1 : r + 2, :]], axis=1)
        i_right, j_right = edge_index(z, pair(right), right_window)
        i_left, j_left = edge_index(z, pair(left), left_window)
        both = jnp.concatenate([one_hot(i_right, z.short), one_hot(i_left, z.short)], axis=0)
        hot[:, pl.ds(r * 128, 256)] = both
        value = lax.dot_general(field, both, (((0,), (0,)), ((), ())), preferred_element_type=F32)
        value = value[:128] + value[128:]
        rows = lax.broadcasted_iota(jnp.int32, (SUB, 256), 0)
        for side, j in enumerate((j_right, j_left)):
            total = None
            for t in range(side, 16, 2):
                piece = jnp.where(rows == j - t * SUB, value[t * SUB : (t + 1) * SUB], 0.0)
                total = piece if total is None else total + piece
            total = jnp.sum(total, axis=0, keepdims=True) * weight[0:1, 0:1]
            at = (1 + side) * n + r
            out[at : at + 1, :] = total[:, :128]
            out[at + 1 : at + 2, :] = total[:, 128:]


def ready_kernel(z, kappa, scale, ocean, cell, from_left, from_right, strip_coeff, coeff, strip_c, own_lane, beside_lane):
    put_coefficients(coeff, coefficients(kappa[...], scale[...], ocean[...].astype(F32), False))
    put_coefficients(strip_c, coefficients(strip_coeff[0], strip_coeff[1], strip_coeff[2], False))
    _, right_window, left_window = windows_of(z)
    n = z.obs_rows
    right = from_right[pl.ds(z.at_obs, n), :].astype(jnp.int32)
    left = from_left[pl.ds(z.at_obs, n), :].astype(jnp.int32)
    rows = lax.broadcasted_iota(jnp.int32, (128, 128), 0)
    for r in range(n):
        at = pl.ds(r * 128, 128)
        own_lane[:, at] = one_hot(own_index(z, cell[r : r + 1, :])[1], 256)
        j_right = edge_index(z, right[r : r + 1, :], right_window)[1]
        j_left = edge_index(z, left[r : r + 1, :], left_window)[1]
        lane = jnp.where((rows & SUB) == 0, j_right, j_left)
        beside_lane[:, at] = jnp.where(rows == lane, 1.0, 0.0).astype(BF16)


def adjoint_kernel(
    z, alpha, members, weight, obs_weight, from_left, from_right, strip_members, coeff, strip_c,
    own_row, own_lane, beside_row, beside_lane, v0, v1, v2, v3,
    out_hbm, x, y, strip, spare, beside, spread, out, shift, sems,
):
    clear_ends(x, y, strip, spare)
    shift[...] = shift_matrix()
    value = (v0[...] + v1[...]) + (v2[...] + v3[...])
    n = z.obs_rows
    weights = pl.ds(z.at_obs + n, n)

    def spread_out(tops, bottoms, row_hot, lane_hot):
        wide = lane_hot.shape[0]
        for k, (top, bottom) in enumerate(zip(split(tops), split(bottoms))):
            for r in range(n):
                at = pl.ds(r * 128, 128)
                line = jnp.concatenate(
                    [jnp.broadcast_to(v[r : r + 1, :].astype(F32), (SUB, 128)) for v in (top, bottom)], axis=0
                ).astype(BF16)
                for t in range(wide // (2 * SUB)):
                    rows = pl.ds(t * 2 * SUB, 2 * SUB)
                    spread[pl.ds(k * wide + t * 2 * SUB, 2 * SUB), at] = lane_hot[rows, at] * line
        dims = (((1,), (1,)), ((), ()))
        total = lax.dot_general(row_hot[...], spread[: 2 * wide, :], dims, preferred_element_type=F32)
        return total[:, :wide] + total[:, wide:]

    amount = obs_weight[...] * value[:n]
    field = spread_out(amount, amount, own_row, own_lane)
    for g in range(2):
        x[pl.ds(SUB + g * z.group, z.group), :] = field[:, g * 128 : (g + 1) * 128]
    right, left = from_right[weights, :] * value[n : 2 * n], from_left[weights, :] * value[2 * n :]
    field = spread_out(right, left, beside_row, beside_lane)
    beside[...] = jnp.where((lanes(z.short) & SUB) == 0, field[: z.short], field[z.short :])
    lane = lanes(SUB)
    part = (lane >> 4) & 3
    within = lane & 15
    outside = ((part == 1) & (within < STEPS)) | ((part == 2) & (within >= STEPS))
    for q in range(z.group // SUB):
        k, rest = divmod(q * SUB, z.short)
        value = jnp.where(outside, roll(beside[pl.ds(rest, SUB), :], -16 * k), 0.0)
        for g in range(2):
            at = g * z.group + q * SUB
            here = pl.ds(SUB + at, SUB)
            field = x[here, :]
            mine = (lane >> 6) == g
            value = jnp.where(mine & (part == 0), roll(field, EDGE + 64 * g), value)
            value = jnp.where(mine & (part == 3), roll(field, 48 + 64 * g), value)
        strip[pl.ds(SUB + q * SUB, SUB), :] = value * (strip_members[pl.ds(q * SUB, SUB), :] * weight[...])
    here = pl.ds(SUB, z.field)
    x[here, :] = x[here, :] * (members[...].astype(F32) * weight[0:1, :])
    sweep([(x, y, coeff, z.levels, shift), (strip, spare, strip_c, z.levels // 2, None)], z.rows)
    sent = []
    for part in range(z.levels // 2):
        for t in range(z.rows // SUB):
            q = part * z.rows + t * SUB
            value = strip[pl.ds(SUB + q, SUB), :]
            for g in range(2):
                at = g * z.group + q
                fixed = x[pl.ds(SUB + at, SUB), :]
                fixed = jnp.where(lane >= z.columns - STEPS, roll(value, 112 - 64 * g), fixed)
                fixed = jnp.where(lane < STEPS, roll(value, -48 - 64 * g), fixed)
                out[pl.ds(at, SUB), :] = alpha[pl.ds(at, SUB), :] + fixed
        if part % 2:
            for g in range(2):
                rows = pl.ds(g * z.group + (part - 1) * z.rows, 2 * z.rows)
                sent.append(pltpu.make_async_copy(out.at[rows, :], out_hbm.at[rows, :], sems.at[len(sent)]))
                sent[-1].start()
    for copy in sent:
        copy.wait()


def local(alpha, members, mem_weight, kappa, norm_scale, land_sea, obs_cell, obs_weight):
    shape = alpha.shape
    z = Sizes(shape[1], shape[2], shape[3], obs_cell.shape[0])
    tiles, holders = lax.axis_size("tile"), lax.axis_size("mem")
    assert holders == 4 and shape[0] == 1
    alpha = alpha.reshape(z.field, z.columns)
    members = members.reshape(z.field, z.columns)
    cell = obs_cell.reshape(z.obs_rows, 128)
    weight = obs_weight.reshape(z.obs_rows, 128)
    whole = pl.BlockSpec(memory_space=pltpu.VMEM)
    stays = pl.BlockSpec(memory_space=pltpu.HBM)
    sds = jax.ShapeDtypeStruct
    main_field = pltpu.VMEM((z.field + 2 * SUB, 128), F32)
    strip_field = pltpu.VMEM((z.group + 2 * SUB, 128), F32)
    coeff = pltpu.VMEM((5, z.rows, 128), F32)
    square = pltpu.VMEM((256, 256), BF16)
    packed = pltpu.VMEM((z.short, 256), BF16)
    payload = sds((z.payload, 128), F32)
    limit = pltpu.CompilerParams(vmem_limit_bytes=24 << 20)
    call = functools.partial(pl.pallas_call, compiler_params=limit)
    given = (alpha, members, kappa, norm_scale, land_sea, cell, weight)
    sent_right, sent_left, *given = call(
        functools.partial(pack_kernel, z),
        out_shape=(payload, payload, *(sds(v.shape, v.dtype) for v in given)),
        in_specs=[stays] * 7,
        out_specs=(whole,) * 9,
        scratch_shapes=[pltpu.SemaphoreType.DMA((7,))],
        name="pack",
    )(*(pltpu.with_memory_space_constraint(v, pltpu.HBM) for v in given))
    alpha, members, kappa, norm_scale, land_sea, cell, weight = given
    up_ring = [(i, (i + 1) % tiles) for i in range(tiles)]
    from_left = lax.ppermute(sent_right, "tile", up_ring)
    from_right = lax.ppermute(sent_left, "tile", [(b, a) for a, b in up_ring])
    inner, own_row = call(
        functools.partial(main_kernel, z),
        out_shape=(sds((z.obs_rows, 128), F32), sds((z.group, z.obs), BF16)),
        in_specs=[whole] * 6,
        out_specs=(whole, whole),
        scratch_shapes=[main_field, coeff, main_field, pltpu.VMEM((z.group, 512), BF16), square],
        name="main",
    )(alpha, members, kappa, norm_scale, land_sea, cell)
    mem_weight, inner = lax.optimization_barrier((mem_weight, inner))
    factor = jnp.broadcast_to(mem_weight, (SUB, 128))
    values, strip_members, strip_coeff, beside_row = call(
        functools.partial(strip_kernel, z),
        out_shape=(
            sds((3 * z.obs_rows, 128), F32),
            sds((z.group, 128), F32),
            sds((3, z.rows, 128), F32),
            sds((2 * z.short, z.obs), BF16),
        ),
        in_specs=[whole] * 8,
        out_specs=(whole,) * 4,
        scratch_shapes=[coeff, strip_field, strip_field, packed, pltpu.VMEM((2 * z.short, 256), BF16)],
        name="strip",
    )(inner, members, sent_right, sent_left, from_left, from_right, cell, factor)
    others = [lax.ppermute(values, "mem", [(i, i ^ k) for i in range(holders)]) for k in range(1, holders)]
    main_c, strip_c, own_lane, beside_lane = call(
        functools.partial(ready_kernel, z),
        out_shape=(
            sds((5, z.rows, 128), F32),
            sds((5, z.rows, 128), F32),
            sds((2 * 128, z.obs), BF16),
            sds((128, z.obs), BF16),
        ),
        in_specs=[whole] * 7,
        out_specs=(whole,) * 4,
        name="ready",
    )(kappa, norm_scale, land_sea, cell, from_left, from_right, strip_coeff)
    product = call(
        functools.partial(adjoint_kernel, z),
        out_shape=sds((z.field, z.columns), F32),
        in_specs=[whole] * 17,
        out_specs=stays,
        scratch_shapes=[
            main_field,
            main_field,
            strip_field,
            strip_field,
            pltpu.VMEM((z.short, 128), F32),
            pltpu.VMEM((512, z.obs), BF16),
            pltpu.VMEM((z.field, 128), F32),
            square,
            pltpu.SemaphoreType.DMA((z.levels // 2,)),
        ],
        name="adjoint",
    )(
        alpha, members, factor, weight, from_left, from_right, strip_members, main_c, strip_c,
        own_row, own_lane, beside_row, beside_lane, values, *others,
    )
    return product.reshape(shape)


def solution(mesh):
    placed = (
        P("mem", None, None, "tile"),
        P("mem", None, None, "tile"),
        P("mem"),
        P(None, "tile"),
        P(None, "tile"),
        P(None, "tile"),
        P("tile"),
        P("tile"),
    )
    return jax.shard_map(
        local, mesh=mesh, in_specs=placed, out_specs=P("mem", None, None, "tile"), check_vma=False
    )
```

```python
import functools

import jax
import jax.numpy as jnp
from jax import lax
from jax.experimental import pallas as pl
from jax.experimental.pallas import tpu as pltpu
from jax.sharding import PartitionSpec as P

STEPS = 8
SUB = 8
EDGE = 2 * STEPS
ASSISTED = 5
F32 = jnp.float32
BF16 = jnp.bfloat16


def div_mod(value, size):
    if size & (size - 1) == 0:
        return value >> (size.bit_length() - 1), value & (size - 1)
    return lax.div(value, size), lax.rem(value, size)


def roll(value, shift, axis=1):
    shift %= value.shape[axis]
    return pltpu.roll(value, shift, axis) if shift else value


def lanes(rows):
    return lax.broadcasted_iota(jnp.int32, (rows, 128), 1)


def split(value):
    high = value.astype(BF16)
    return high, (value - high.astype(F32)).astype(BF16)


class Sizes:
    def __init__(self, levels, rows, columns, obs):
        self.levels, self.rows, self.columns, self.obs = levels, rows, columns, obs
        assert columns == 128 and levels == 16 and rows % 16 == 0 and obs % 256 == 0 and STEPS == 8
        self.field = levels * rows
        self.group = self.field // 2
        self.short = self.field // 8
        self.tiles = rows // SUB
        assert self.tiles == 8
        self.at_members = self.short
        self.at_coeff = self.at_members + rows
        self.at_obs = self.at_coeff + 3 * SUB
        self.obs_rows = obs // 128
        self.payload = self.at_obs + 2 * self.obs_rows


def overlay(pieces, window):
    value = pieces[0]
    for k in range(1, len(pieces)):
        value = jnp.where(window == k, pieces[k], value)
    return value


def pack_kernel(
    z, alpha_hbm, members_hbm, kappa_hbm, scale_hbm, ocean_hbm, cell_hbm, weight_hbm,
    out_right, out_left, alpha, members, kappa, scale, ocean, cell, weight, sems,
):
    pairs = (
        (members_hbm, members), (alpha_hbm, alpha), (kappa_hbm, kappa), (scale_hbm, scale), (ocean_hbm, ocean),
        (cell_hbm, cell), (weight_hbm, weight),
    )
    copies = [pltpu.make_async_copy(a, b, sems.at[k]) for k, (a, b) in enumerate(pairs)]
    for copy in copies:
        copy.start()

    def put(where, right, left):
        out_right[where, :] = right
        out_left[where, :] = left

    for copy in copies[2:]:
        copy.wait()
    lane = lanes(SUB)
    for k, ref in enumerate((kappa, scale, ocean)):
        right, left = [], []
        for t in range(z.tiles):
            value = ref[pl.ds(t * SUB, SUB), :].astype(F32)
            right.append(roll(value, EDGE * (t + 1)))
            left.append(roll(value, EDGE * t))
        put(pl.ds(z.at_coeff + k * SUB, SUB), overlay(right, lane >> 4), overlay(left, lane >> 4))
    n = z.obs_rows
    for at, value in ((z.at_obs, cell[...].astype(F32)), (z.at_obs + n, weight[...])):
        put(pl.ds(at, n), value, value)
    copies[0].wait()
    block = 2 * SUB
    lane = lanes(block)
    for t in range(z.rows // block):
        right, left = [], []
        for g in range(2):
            for part in range(SUB):
                value = members[pl.ds(g * z.group + part * z.rows + t * block, block), :].astype(F32)
                base = 64 * g + STEPS * part
                right.append(roll(value, base + STEPS))
                left.append(roll(value, base))
        put(pl.ds(z.at_members + t * block, block), overlay(right, lane >> 3), overlay(left, lane >> 3))
    copies[1].wait()
    for t in range(z.short // block):
        right, left = [], []
        for g in range(2):
            for h in range(4):
                value = alpha[pl.ds(g * z.group + h * z.short + t * block, block), :]
                base = 64 * g + EDGE * h
                right.append(roll(value, base + EDGE))
                left.append(roll(value, base))
        put(pl.ds(t * block, block), overlay(right, lane >> 4), overlay(left, lane >> 4))


def up(value):
    return roll(value, -1, 0)


def down(value):
    return roll(value, 1, 0)


def coefficients(kappa, scale, ocean, forward):
    row = lax.broadcasted_iota(jnp.int32, kappa.shape, 0)
    north = 0.5 * (kappa + up(kappa)) * ocean * up(ocean)
    north = jnp.where(row == kappa.shape[0] - 1, 0.0, north)
    east = 0.5 * (kappa + roll(kappa, -1)) * ocean * roll(ocean, -1)
    west, south = roll(east, 1), down(north)
    centre = 1.0 - (east + west) - (north + south)
    if forward:
        return (
            centre * scale,
            east * roll(scale, -1),
            west * roll(scale, 1),
            north * up(scale),
            south * down(scale),
        )
    return tuple(scale * c for c in (centre, east, west, north, south))


def put_coefficients(ref, values):
    for k, value in enumerate(values):
        ref[k] = value


def shift_matrix():
    row = lax.broadcasted_iota(jnp.int32, (256, 256), 0)
    column = lax.broadcasted_iota(jnp.int32, (256, 256), 1)
    wanted = jnp.where(column < 128, column + 1, column - 1)
    return jnp.where((row & 127) == (wanted & 127), 1.0, 0.0).astype(BF16)


def step_rows(source, target, coeff, rows, levels, shift):
    assisted = 0
    if shift is not None:
        assisted = ASSISTED
        both = jnp.concatenate(split(source[pl.ds(SUB, assisted * rows), :]), axis=1)
        beside = jnp.dot(both, shift[...], preferred_element_type=F32)
    for t in range(rows // SUB):
        c = [coeff[k, pl.ds(t * SUB, SUB), :] for k in range(5)]
        for level in range(levels):
            r = level * rows + t * SUB
            at = SUB + r
            u = source[pl.ds(at, SUB), :]
            along = c[3] * source[pl.ds(at + 1, SUB), :] + c[4] * source[pl.ds(at - 1, SUB), :]
            if level < assisted:
                across = c[1] * beside[r : r + SUB, :128] + c[2] * beside[r : r + SUB, 128:]
            else:
                across = c[1] * roll(u, -1) + c[2] * roll(u, 1)
            target[pl.ds(at, SUB), :] = c[0] * u + across + along


def clear_ends(*buffers):
    for ref in buffers:
        zero = jnp.zeros((SUB, 128), F32)
        ref[pl.ds(0, SUB), :] = zero
        ref[pl.ds(ref.shape[0] - SUB, SUB), :] = zero


def sweep(fields, rows):
    for step in range(STEPS):
        for x, y, coeff, levels, shift in fields:
            source, target = (y, x) if step % 2 else (x, y)
            step_rows(source, target, coeff, rows, levels, shift)


def cell_parts(z, cell):
    level, rest = div_mod(cell, z.rows * z.columns)
    row, column = div_mod(rest, z.columns)
    return level >> 3, level & 7, row, column


def own_index(z, cell):
    group, part, row, column = cell_parts(z, cell)
    return part * z.rows + row, group * 128 + column


def edge_index(z, cell, windows):
    group, part, row, column = cell_parts(z, cell)
    inside, lane = False, 0
    for first, at in windows:
        here = (column >= first) & (column < first + STEPS)
        inside = here | inside
        lane = jnp.where(here, at - first, lane)
    lane = lane + column + 64 * group + 16 * (part >> 1)
    return jnp.where(inside, (part & 1) * z.rows + row, -1), lane & 127


def own_edges(z):
    return (0, 48), (z.columns - STEPS, 8)


def windows_of(z):
    return own_edges(z), ((0, 16),), ((z.columns - STEPS, 40),)


def quarters(unit, first, second):
    even, odd = (first, second) if first % 2 == 0 else (second, first)
    return jnp.where((unit & 1) == 0, ((unit - even) >> 1) & 3, ((unit - odd) >> 1) & 3)


def one_hot(index, size):
    rows = lax.broadcasted_iota(jnp.int32, (size, index.shape[1]), 0)
    return jnp.where(rows == index, 1.0, 0.0).astype(BF16)


def read_off(field, hot, j):
    value = lax.dot_general(field, hot, (((0,), (0,)), ((), ())), preferred_element_type=F32)
    n = value.shape[0] // 2
    value = value[:n] + value[n:]
    rows = lax.broadcasted_iota(jnp.int32, value.shape, 0)
    return jnp.sum(jnp.where(rows == j, value, 0.0), axis=0, keepdims=True)


def gather(z, out, at, field, cell, index, keep=None, start=0):
    for n in range(z.obs_rows // 2):
        row = jnp.concatenate([cell[2 * n : 2 * n + 1, :], cell[2 * n + 1 : 2 * n + 2, :]], axis=1)
        i, j = index(row)
        hot = one_hot(i, field.shape[0])
        if keep is not None:
            keep[:, pl.ds(start + 256 * n, 256)] = hot
        value = read_off(field, hot, j)
        out[at + 2 * n : at + 2 * n + 1, :] = value[:, :128]
        out[at + 2 * n + 1 : at + 2 * n + 2, :] = value[:, 128:]


def forward_sweep(z, alpha, kappa, scale, ocean, coeff, x, y, shift):
    put_coefficients(coeff, coefficients(kappa[...], scale[...], ocean[...].astype(F32), True))
    clear_ends(x, y)
    x[pl.ds(SUB, z.field), :] = alpha[...]
    shift[...] = shift_matrix()
    sweep([(x, y, coeff, z.levels, shift)], z.rows)


def own_columns(pair, lane):
    pieces = []
    for g, value in enumerate(pair):
        pieces += [roll(value, EDGE + 64 * g), roll(value, 48 + 64 * g)]
    return overlay(pieces, (lane >> 6) * 2 + ((lane >> 5) & 1))


def main_kernel(
    z, alpha, members, kappa, scale, ocean, cell, out, hot, strip_x, strip_members, strip_coeff,
    x, coeff, y, both, shift,
):
    forward_sweep(z, alpha, kappa, scale, ocean, coeff, x, y, shift)
    lane = lanes(z.group)
    inner = (lane >= STEPS) & (lane < z.columns - STEPS)
    for g in range(2):
        rows = pl.ds(g * z.group, z.group)
        value = x[pl.ds(SUB + g * z.group, z.group), :] * members[rows, :].astype(F32)
        high, low = split(jnp.where(inner, value, 0.0))
        both[:, pl.ds(g * 128, 128)] = high
        both[:, pl.ds(256 + g * 128, 128)] = low
    gather(z, out, 0, both[...], cell[...], lambda c: own_index(z, c), hot)
    block = 2 * SUB
    lane = lanes(block)
    for t in range(z.group // block):
        rows = [pl.ds(g * z.group + t * block, block) for g in range(2)]
        strip_x[pl.ds(t * block, block), :] = own_columns([alpha[r, :] for r in rows], lane)
        strip_members[pl.ds(t * block, block), :] = own_columns([members[r, :].astype(F32) for r in rows], lane)
    lane = lanes(z.rows)
    for k, ref in enumerate((kappa, scale, ocean)):
        value = ref[...].astype(F32)
        strip_coeff[k] = own_columns([value, value], lane)


def strip_kernel(
    z, inner, own_x, own_members, own_coeff, from_left, from_right, cell, weight,
    out, strip_members, strip_coeff, hot, coeff, x, y, outer, beside,
):
    clear_ends(x, y)
    lane = lanes(SUB)
    part_of = (lane >> 4) & 3
    for k in range(3):
        rows = pl.ds(z.at_coeff + k * SUB, SUB)
        right, left = from_right[rows, :], from_left[rows, :]
        for t in range(z.tiles):
            pieces = []
            for g in range(2):
                pieces += [roll(right, EDGE * (1 - t) + 64 * g), roll(left, EDGE * (2 - t) + 64 * g)]
            value = overlay(pieces, (lane >> 6) * 2 + ((lane >> 5) & 1))
            at = pl.ds(t * SUB, SUB)
            strip_coeff[k, at, :] = jnp.where((part_of == 1) | (part_of == 2), value, own_coeff[k, at, :])
    for q in range(z.short // SUB):
        right, left = from_right[pl.ds(q * SUB, SUB), :], from_left[pl.ds(q * SUB, SUB), :]
        for h in range(4):
            at = h * z.short + q * SUB
            value = jnp.where(part_of == 1, roll(right, EDGE * (1 - h)), own_x[pl.ds(at, SUB), :])
            x[pl.ds(SUB + at, SUB), :] = jnp.where(part_of == 2, roll(left, EDGE * (2 - h)), value)
    for t in range(z.tiles):
        rows = pl.ds(z.at_members + t * SUB, SUB)
        right, left = from_right[rows, :], from_left[rows, :]
        for part in range(SUB):
            at = pl.ds(part * z.rows + t * SUB, SUB)
            value = jnp.where(part_of == 1, roll(right, EDGE - STEPS * part), own_members[at, :])
            strip_members[at, :] = jnp.where(
                part_of == 2, roll(left, 2 * EDGE + STEPS - STEPS * part), value
            )
    put_coefficients(coeff, coefficients(strip_coeff[0], strip_coeff[1], strip_coeff[2], True))
    sweep([(x, y, coeff, z.levels // 2, None)], z.rows)
    unit = lanes(z.short) >> 3
    for ref, first, second in ((outer, 1, 6), (beside, 2, 5)):
        quarter = quarters(unit, first, second)
        pieces = []
        for k in range(4):
            rows = pl.ds(k * z.short, z.short)
            pieces.append(roll(x[pl.ds(SUB + k * z.short, z.short), :] * strip_members[rows, :], 16 * k))
        value = overlay(pieces, quarter)
        if ref is outer:
            rights = ((0, value),)
        else:
            rights = ((0, jnp.where((unit & 1) == 0, value, 0.0)), (z.short, jnp.where((unit & 1) == 1, value, 0.0)))
        for at, value in rights:
            high, low = split(value)
            ref[pl.ds(at, z.short), :128] = high
            ref[pl.ds(at, z.short), 128:] = low
    n = z.obs_rows
    own_window, right_window, left_window = windows_of(z)
    gather(z, out, 0, outer[...], cell[...], lambda c: edge_index(z, c, own_window))
    out[:n, :] = (out[:n, :] + inner[...]) * weight[0:1, :]
    right = from_right[pl.ds(z.at_obs, n), :].astype(jnp.int32)
    left = from_left[pl.ds(z.at_obs, n), :].astype(jnp.int32)
    field = beside[...]
    for r in range(0, n, 2):
        pair = lambda v: jnp.concatenate([v[r : r + 1, :], v[r + 1 : r + 2, :]], axis=1)
        i_right, j_right = edge_index(z, pair(right), right_window)
        i_left, j_left = edge_index(z, pair(left), left_window)
        both = jnp.concatenate([one_hot(i_right, z.short), one_hot(i_left, z.short)], axis=0)
        hot[:, pl.ds(r * 128, 256)] = both
        value = lax.dot_general(field, both, (((0,), (0,)), ((), ())), preferred_element_type=F32)
        value = value[:128] + value[128:]
        rows = lax.broadcasted_iota(jnp.int32, (SUB, 256), 0)
        for side, j in enumerate((j_right, j_left)):
            total = None
            for t in range(side, 16, 2):
                piece = jnp.where(rows == j - t * SUB, value[t * SUB : (t + 1) * SUB], 0.0)
                total = piece if total is None else total + piece
            total = jnp.sum(total, axis=0, keepdims=True) * weight[0:1, 0:1]
            at = (1 + side) * n + r
            out[at : at + 1, :] = total[:, :128]
            out[at + 1 : at + 2, :] = total[:, 128:]


def ready_kernel(z, kappa, scale, ocean, cell, from_left, from_right, strip_coeff, coeff, strip_c, own_lane, beside_lane):
    put_coefficients(coeff, coefficients(kappa[...], scale[...], ocean[...].astype(F32), False))
    put_coefficients(strip_c, coefficients(strip_coeff[0], strip_coeff[1], strip_coeff[2], False))
    _, right_window, left_window = windows_of(z)
    n = z.obs_rows
    right = from_right[pl.ds(z.at_obs, n), :].astype(jnp.int32)
    left = from_left[pl.ds(z.at_obs, n), :].astype(jnp.int32)
    rows = lax.broadcasted_iota(jnp.int32, (128, 128), 0)
    for r in range(n):
        at = pl.ds(r * 128, 128)
        own_lane[:, at] = one_hot(own_index(z, cell[r : r + 1, :])[1], 256)
        j_right = edge_index(z, right[r : r + 1, :], right_window)[1]
        j_left = edge_index(z, left[r : r + 1, :], left_window)[1]
        lane = jnp.where((rows & SUB) == 0, j_right, j_left)
        beside_lane[:, at] = jnp.where(rows == lane, 1.0, 0.0).astype(BF16)


def adjoint_kernel(
    z, alpha, members, weight, obs_weight, from_left, from_right, strip_members, coeff, strip_c,
    own_row, own_lane, beside_row, beside_lane, v0, v1, v2, v3,
    out_hbm, x, y, strip, spare, beside, spread, out, shift, sems,
):
    clear_ends(x, y, strip, spare)
    shift[...] = shift_matrix()
    value = (v0[...] + v1[...]) + (v2[...] + v3[...])
    n = z.obs_rows
    weights = pl.ds(z.at_obs + n, n)

    def spread_out(tops, bottoms, row_hot, lane_hot):
        wide = lane_hot.shape[0]
        for k, (top, bottom) in enumerate(zip(split(tops), split(bottoms))):
            for r in range(n):
                at = pl.ds(r * 128, 128)
                line = jnp.concatenate(
                    [jnp.broadcast_to(v[r : r + 1, :].astype(F32), (SUB, 128)) for v in (top, bottom)], axis=0
                ).astype(BF16)
                for t in range(wide // (2 * SUB)):
                    rows = pl.ds(t * 2 * SUB, 2 * SUB)
                    spread[pl.ds(k * wide + t * 2 * SUB, 2 * SUB), at] = lane_hot[rows, at] * line
        dims = (((1,), (1,)), ((), ()))
        total = lax.dot_general(row_hot[...], spread[: 2 * wide, :], dims, preferred_element_type=F32)
        return total[:, :wide] + total[:, wide:]

    amount = obs_weight[...] * value[:n]
    field = spread_out(amount, amount, own_row, own_lane)
    for g in range(2):
        x[pl.ds(SUB + g * z.group, z.group), :] = field[:, g * 128 : (g + 1) * 128]
    right, left = from_right[weights, :] * value[n : 2 * n], from_left[weights, :] * value[2 * n :]
    field = spread_out(right, left, beside_row, beside_lane)
    beside[...] = jnp.where((lanes(z.short) & SUB) == 0, field[: z.short], field[z.short :])
    lane = lanes(SUB)
    part = (lane >> 4) & 3
    within = lane & 15
    outside = ((part == 1) & (within < STEPS)) | ((part == 2) & (within >= STEPS))
    for q in range(z.group // SUB):
        k, rest = divmod(q * SUB, z.short)
        value = jnp.where(outside, roll(beside[pl.ds(rest, SUB), :], -16 * k), 0.0)
        for g in range(2):
            at = g * z.group + q * SUB
            here = pl.ds(SUB + at, SUB)
            field = x[here, :]
            mine = (lane >> 6) == g
            value = jnp.where(mine & (part == 0), roll(field, EDGE + 64 * g), value)
            value = jnp.where(mine & (part == 3), roll(field, 48 + 64 * g), value)
        strip[pl.ds(SUB + q * SUB, SUB), :] = value * (strip_members[pl.ds(q * SUB, SUB), :] * weight[...])
    here = pl.ds(SUB, z.field)
    x[here, :] = x[here, :] * (members[...].astype(F32) * weight[0:1, :])
    sweep([(x, y, coeff, z.levels, shift), (strip, spare, strip_c, z.levels // 2, None)], z.rows)
    sent = []
    for part in range(z.levels // 2):
        for t in range(z.rows // SUB):
            q = part * z.rows + t * SUB
            value = strip[pl.ds(SUB + q, SUB), :]
            for g in range(2):
                at = g * z.group + q
                fixed = x[pl.ds(SUB + at, SUB), :]
                fixed = jnp.where(lane >= z.columns - STEPS, roll(value, 112 - 64 * g), fixed)
                fixed = jnp.where(lane < STEPS, roll(value, -48 - 64 * g), fixed)
                out[pl.ds(at, SUB), :] = alpha[pl.ds(at, SUB), :] + fixed
        if part % 2:
            for g in range(2):
                rows = pl.ds(g * z.group + (part - 1) * z.rows, 2 * z.rows)
                sent.append(pltpu.make_async_copy(out.at[rows, :], out_hbm.at[rows, :], sems.at[len(sent)]))
                sent[-1].start()
    for copy in sent:
        copy.wait()


def local(alpha, members, mem_weight, kappa, norm_scale, land_sea, obs_cell, obs_weight):
    shape = alpha.shape
    z = Sizes(shape[1], shape[2], shape[3], obs_cell.shape[0])
    tiles, holders = lax.axis_size("tile"), lax.axis_size("mem")
    assert holders == 4 and shape[0] == 1
    alpha = alpha.reshape(z.field, z.columns)
    members = members.reshape(z.field, z.columns)
    cell = obs_cell.reshape(z.obs_rows, 128)
    weight = obs_weight.reshape(z.obs_rows, 128)
    whole = pl.BlockSpec(memory_space=pltpu.VMEM)
    stays = pl.BlockSpec(memory_space=pltpu.HBM)
    sds = jax.ShapeDtypeStruct
    main_field = pltpu.VMEM((z.field + 2 * SUB, 128), F32)
    strip_field = pltpu.VMEM((z.group + 2 * SUB, 128), F32)
    coeff = pltpu.VMEM((5, z.rows, 128), F32)
    square = pltpu.VMEM((256, 256), BF16)
    packed = pltpu.VMEM((z.short, 256), BF16)
    payload = sds((z.payload, 128), F32)
    limit = pltpu.CompilerParams(vmem_limit_bytes=24 << 20)
    call = functools.partial(pl.pallas_call, compiler_params=limit)
    given = (alpha, members, kappa, norm_scale, land_sea, cell, weight)
    sent_right, sent_left, *given = call(
        functools.partial(pack_kernel, z),
        out_shape=(payload, payload, *(sds(v.shape, v.dtype) for v in given)),
        in_specs=[stays] * 7,
        out_specs=(whole,) * 9,
        scratch_shapes=[pltpu.SemaphoreType.DMA((7,))],
        name="pack",
    )(*(pltpu.with_memory_space_constraint(v, pltpu.HBM) for v in given))
    alpha, members, kappa, norm_scale, land_sea, cell, weight = given
    up_ring = [(i, (i + 1) % tiles) for i in range(tiles)]
    from_left = lax.ppermute(sent_right, "tile", up_ring)
    from_right = lax.ppermute(sent_left, "tile", [(b, a) for a, b in up_ring])
    inner, own_row, own_x, own_members, own_coeff = call(
        functools.partial(main_kernel, z),
        out_shape=(
            sds((z.obs_rows, 128), F32),
            sds((z.group, z.obs), BF16),
            sds((z.group, 128), F32),
            sds((z.group, 128), F32),
            sds((3, z.rows, 128), F32),
        ),
        in_specs=[whole] * 6,
        out_specs=(whole,) * 5,
        scratch_shapes=[main_field, coeff, main_field, pltpu.VMEM((z.group, 512), BF16), square],
        name="main",
    )(alpha, members, kappa, norm_scale, land_sea, cell)
    factor = jnp.broadcast_to(mem_weight, (SUB, 128))
    values, strip_members, strip_coeff, beside_row = call(
        functools.partial(strip_kernel, z),
        out_shape=(
            sds((3 * z.obs_rows, 128), F32),
            sds((z.group, 128), F32),
            sds((3, z.rows, 128), F32),
            sds((2 * z.short, z.obs), BF16),
        ),
        in_specs=[whole] * 8,
        out_specs=(whole,) * 4,
        scratch_shapes=[coeff, strip_field, strip_field, packed, pltpu.VMEM((2 * z.short, 256), BF16)],
        name="strip",
    )(inner, own_x, own_members, own_coeff, from_left, from_right, cell, factor)
    others = [lax.ppermute(values, "mem", [(i, i ^ k) for i in range(holders)]) for k in range(1, holders)]
    main_c, strip_c, own_lane, beside_lane = call(
        functools.partial(ready_kernel, z),
        out_shape=(
            sds((5, z.rows, 128), F32),
            sds((5, z.rows, 128), F32),
            sds((2 * 128, z.obs), BF16),
            sds((128, z.obs), BF16),
        ),
        in_specs=[whole] * 7,
        out_specs=(whole,) * 4,
        name="ready",
    )(kappa, norm_scale, land_sea, cell, from_left, from_right, strip_coeff)
    product = call(
        functools.partial(adjoint_kernel, z),
        out_shape=sds((z.field, z.columns), F32),
        in_specs=[whole] * 17,
        out_specs=stays,
        scratch_shapes=[
            main_field,
            main_field,
            strip_field,
            strip_field,
            pltpu.VMEM((z.short, 128), F32),
            pltpu.VMEM((512, z.obs), BF16),
            pltpu.VMEM((z.field, 128), F32),
            square,
            pltpu.SemaphoreType.DMA((z.levels // 2,)),
        ],
        name="adjoint",
    )(
        alpha, members, factor, weight, from_left, from_right, strip_members, main_c, strip_c,
        own_row, own_lane, beside_row, beside_lane, values, *others,
    )
    return product.reshape(shape)


def solution(mesh):
    placed = (
        P("mem", None, None, "tile"),
        P("mem", None, None, "tile"),
        P("mem"),
        P(None, "tile"),
        P(None, "tile"),
        P(None, "tile"),
        P("tile"),
        P("tile"),
    )
    return jax.shard_map(
        local, mesh=mesh, in_specs=placed, out_specs=P("mem", None, None, "tile"), check_vma=False
    )
```

```python
import functools

import jax
import jax.numpy as jnp
from jax import lax
from jax.experimental import pallas as pl
from jax.experimental.pallas import tpu as pltpu
from jax.sharding import PartitionSpec as P

STEPS = 8
SUB = 8
EDGE = 2 * STEPS
ASSISTED = 5
F32 = jnp.float32
BF16 = jnp.bfloat16


def div_mod(value, size):
    if size & (size - 1) == 0:
        return value >> (size.bit_length() - 1), value & (size - 1)
    return lax.div(value, size), lax.rem(value, size)


def roll(value, shift, axis=1):
    shift %= value.shape[axis]
    return pltpu.roll(value, shift, axis) if shift else value


def lanes(rows):
    return lax.broadcasted_iota(jnp.int32, (rows, 128), 1)


def split(value):
    high = value.astype(BF16)
    return high, (value - high.astype(F32)).astype(BF16)


class Sizes:
    def __init__(self, levels, rows, columns, obs):
        self.levels, self.rows, self.columns, self.obs = levels, rows, columns, obs
        assert columns == 128 and levels == 16 and rows % 16 == 0 and obs % 256 == 0 and STEPS == 8
        self.field = levels * rows
        self.group = self.field // 2
        self.short = self.field // 8
        self.tiles = rows // SUB
        assert self.tiles == 8
        self.at_members = self.short
        self.at_coeff = self.at_members + rows
        self.at_obs = self.at_coeff + 3 * SUB
        self.obs_rows = obs // 128
        self.payload = self.at_obs + 2 * self.obs_rows


def overlay(pieces, window):
    value = pieces[0]
    for k in range(1, len(pieces)):
        value = jnp.where(window == k, pieces[k], value)
    return value


def pack_kernel(
    z, alpha_hbm, members_hbm, kappa_hbm, scale_hbm, ocean_hbm, cell_hbm, weight_hbm,
    out_right, out_left, alpha, members, kappa, scale, ocean, cell, weight, sems,
):
    pairs = (
        (members_hbm, members), (alpha_hbm, alpha), (kappa_hbm, kappa), (scale_hbm, scale), (ocean_hbm, ocean),
        (cell_hbm, cell), (weight_hbm, weight),
    )
    copies = [pltpu.make_async_copy(a, b, sems.at[k]) for k, (a, b) in enumerate(pairs)]
    for copy in copies:
        copy.start()

    def put(where, right, left):
        out_right[where, :] = right
        out_left[where, :] = left

    for copy in copies[2:]:
        copy.wait()
    lane = lanes(SUB)
    for k, ref in enumerate((kappa, scale, ocean)):
        right, left = [], []
        for t in range(z.tiles):
            value = ref[pl.ds(t * SUB, SUB), :].astype(F32)
            right.append(roll(value, EDGE * (t + 1)))
            left.append(roll(value, EDGE * t))
        put(pl.ds(z.at_coeff + k * SUB, SUB), overlay(right, lane >> 4), overlay(left, lane >> 4))
    n = z.obs_rows
    for at, value in ((z.at_obs, cell[...].astype(F32)), (z.at_obs + n, weight[...])):
        put(pl.ds(at, n), value, value)
    copies[0].wait()
    block = 2 * SUB
    lane = lanes(block)
    for t in range(z.rows // block):
        right, left = [], []
        for g in range(2):
            for part in range(SUB):
                value = members[pl.ds(g * z.group + part * z.rows + t * block, block), :].astype(F32)
                base = 64 * g + STEPS * part
                right.append(roll(value, base + STEPS))
                left.append(roll(value, base))
        put(pl.ds(z.at_members + t * block, block), overlay(right, lane >> 3), overlay(left, lane >> 3))
    copies[1].wait()
    for t in range(z.short // block):
        right, left = [], []
        for g in range(2):
            for h in range(4):
                value = alpha[pl.ds(g * z.group + h * z.short + t * block, block), :]
                base = 64 * g + EDGE * h
                right.append(roll(value, base + EDGE))
                left.append(roll(value, base))
        put(pl.ds(t * block, block), overlay(right, lane >> 4), overlay(left, lane >> 4))


def up(value):
    return roll(value, -1, 0)


def down(value):
    return roll(value, 1, 0)


def coefficients(kappa, scale, ocean, forward):
    row = lax.broadcasted_iota(jnp.int32, kappa.shape, 0)
    north = 0.5 * (kappa + up(kappa)) * ocean * up(ocean)
    north = jnp.where(row == kappa.shape[0] - 1, 0.0, north)
    east = 0.5 * (kappa + roll(kappa, -1)) * ocean * roll(ocean, -1)
    west, south = roll(east, 1), down(north)
    centre = 1.0 - (east + west) - (north + south)
    if forward:
        return (
            centre * scale,
            east * roll(scale, -1),
            west * roll(scale, 1),
            north * up(scale),
            south * down(scale),
        )
    return tuple(scale * c for c in (centre, east, west, north, south))


def put_coefficients(ref, values):
    for k, value in enumerate(values):
        ref[k] = value


def shift_matrix():
    row = lax.broadcasted_iota(jnp.int32, (256, 256), 0)
    column = lax.broadcasted_iota(jnp.int32, (256, 256), 1)
    wanted = jnp.where(column < 128, column + 1, column - 1)
    return jnp.where((row & 127) == (wanted & 127), 1.0, 0.0).astype(BF16)


def step_rows(source, target, coeff, rows, levels, shift):
    assisted = 0
    if shift is not None:
        assisted = ASSISTED
        both = jnp.concatenate(split(source[pl.ds(SUB, assisted * rows), :]), axis=1)
        beside = jnp.dot(both, shift[...], preferred_element_type=F32)
    for t in range(rows // SUB):
        c = [coeff[k, pl.ds(t * SUB, SUB), :] for k in range(5)]
        for level in range(levels):
            r = level * rows + t * SUB
            at = SUB + r
            u = source[pl.ds(at, SUB), :]
            along = c[3] * source[pl.ds(at + 1, SUB), :] + c[4] * source[pl.ds(at - 1, SUB), :]
            if level < assisted:
                across = c[1] * beside[r : r + SUB, :128] + c[2] * beside[r : r + SUB, 128:]
            else:
                across = c[1] * roll(u, -1) + c[2] * roll(u, 1)
            target[pl.ds(at, SUB), :] = c[0] * u + across + along


def clear_ends(*buffers):
    for ref in buffers:
        zero = jnp.zeros((SUB, 128), F32)
        ref[pl.ds(0, SUB), :] = zero
        ref[pl.ds(ref.shape[0] - SUB, SUB), :] = zero


def sweep(fields, rows):
    for step in range(STEPS):
        for x, y, coeff, levels, shift in fields:
            source, target = (y, x) if step % 2 else (x, y)
            step_rows(source, target, coeff, rows, levels, shift)


def cell_parts(z, cell):
    level, rest = div_mod(cell, z.rows * z.columns)
    row, column = div_mod(rest, z.columns)
    return level >> 3, level & 7, row, column


def own_index(z, cell):
    group, part, row, column = cell_parts(z, cell)
    return part * z.rows + row, group * 128 + column


def edge_index(z, cell, windows):
    group, part, row, column = cell_parts(z, cell)
    inside, lane = False, 0
    for first, at in windows:
        here = (column >= first) & (column < first + STEPS)
        inside = here | inside
        lane = jnp.where(here, at - first, lane)
    lane = lane + column + 64 * group + 16 * (part >> 1)
    return jnp.where(inside, (part & 1) * z.rows + row, -1), lane & 127


def own_edges(z):
    return (0, 48), (z.columns - STEPS, 8)


def windows_of(z):
    return own_edges(z), ((0, 16),), ((z.columns - STEPS, 40),)


def quarters(unit, first, second):
    even, odd = (first, second) if first % 2 == 0 else (second, first)
    return jnp.where((unit & 1) == 0, ((unit - even) >> 1) & 3, ((unit - odd) >> 1) & 3)


def one_hot(index, size):
    rows = lax.broadcasted_iota(jnp.int32, (size, index.shape[1]), 0)
    return jnp.where(rows == index, 1.0, 0.0).astype(BF16)


def read_off(field, hot, j):
    value = lax.dot_general(field, hot, (((0,), (0,)), ((), ())), preferred_element_type=F32)
    n = value.shape[0] // 2
    value = value[:n] + value[n:]
    rows = lax.broadcasted_iota(jnp.int32, value.shape, 0)
    return jnp.sum(jnp.where(rows == j, value, 0.0), axis=0, keepdims=True)


def gather(z, out, at, field, cell, index, keep=None, start=0):
    for n in range(z.obs_rows // 2):
        row = jnp.concatenate([cell[2 * n : 2 * n + 1, :], cell[2 * n + 1 : 2 * n + 2, :]], axis=1)
        i, j = index(row)
        hot = one_hot(i, field.shape[0])
        if keep is not None:
            keep[:, pl.ds(start + 256 * n, 256)] = hot
        value = read_off(field, hot, j)
        out[at + 2 * n : at + 2 * n + 1, :] = value[:, :128]
        out[at + 2 * n + 1 : at + 2 * n + 2, :] = value[:, 128:]


def forward_sweep(z, alpha, kappa, scale, ocean, coeff, x, y, shift):
    put_coefficients(coeff, coefficients(kappa[...], scale[...], ocean[...].astype(F32), True))
    clear_ends(x, y)
    x[pl.ds(SUB, z.field), :] = alpha[...]
    shift[...] = shift_matrix()
    sweep([(x, y, coeff, z.levels, shift)], z.rows)


def own_columns(pair, lane):
    pieces = []
    for g, value in enumerate(pair):
        pieces += [roll(value, EDGE + 64 * g), roll(value, 48 + 64 * g)]
    return overlay(pieces, (lane >> 6) * 2 + ((lane >> 5) & 1))


def main_kernel(
    z, alpha, members, kappa, scale, ocean, cell, out, hot, strip_x, strip_members, strip_coeff,
    x, coeff, y, both, shift,
):
    forward_sweep(z, alpha, kappa, scale, ocean, coeff, x, y, shift)
    lane = lanes(z.group)
    inner = (lane >= STEPS) & (lane < z.columns - STEPS)
    for g in range(2):
        rows = pl.ds(g * z.group, z.group)
        value = x[pl.ds(SUB + g * z.group, z.group), :] * members[rows, :].astype(F32)
        high, low = split(jnp.where(inner, value, 0.0))
        both[:, pl.ds(g * 128, 128)] = high
        both[:, pl.ds(256 + g * 128, 128)] = low
    gather(z, out, 0, both[...], cell[...], lambda c: own_index(z, c), hot)
    block = 2 * SUB
    lane = lanes(block)
    for t in range(z.group // block):
        rows = [pl.ds(g * z.group + t * block, block) for g in range(2)]
        strip_x[pl.ds(t * block, block), :] = own_columns([alpha[r, :] for r in rows], lane)
        strip_members[pl.ds(t * block, block), :] = own_columns([members[r, :].astype(F32) for r in rows], lane)
    lane = lanes(z.rows)
    for k, ref in enumerate((kappa, scale, ocean)):
        value = ref[...].astype(F32)
        strip_coeff[k] = own_columns([value, value], lane)


def strip_kernel(
    z, inner, own_x, own_members, own_coeff, from_left, from_right, cell, weight,
    out, strip_members, strip_coeff, hot, coeff, x, y, outer, beside,
):
    clear_ends(x, y)
    lane = lanes(SUB)
    part_of = (lane >> 4) & 3
    for k in range(3):
        rows = pl.ds(z.at_coeff + k * SUB, SUB)
        right, left = from_right[rows, :], from_left[rows, :]
        for t in range(z.tiles):
            pieces = []
            for g in range(2):
                pieces += [roll(right, EDGE * (1 - t) + 64 * g), roll(left, EDGE * (2 - t) + 64 * g)]
            value = overlay(pieces, (lane >> 6) * 2 + ((lane >> 5) & 1))
            at = pl.ds(t * SUB, SUB)
            strip_coeff[k, at, :] = jnp.where((part_of == 1) | (part_of == 2), value, own_coeff[k, at, :])
    for q in range(z.short // SUB):
        right, left = from_right[pl.ds(q * SUB, SUB), :], from_left[pl.ds(q * SUB, SUB), :]
        for h in range(4):
            at = h * z.short + q * SUB
            value = jnp.where(part_of == 1, roll(right, EDGE * (1 - h)), own_x[pl.ds(at, SUB), :])
            x[pl.ds(SUB + at, SUB), :] = jnp.where(part_of == 2, roll(left, EDGE * (2 - h)), value)
    for t in range(z.tiles):
        rows = pl.ds(z.at_members + t * SUB, SUB)
        right, left = from_right[rows, :], from_left[rows, :]
        for part in range(SUB):
            at = pl.ds(part * z.rows + t * SUB, SUB)
            value = jnp.where(part_of == 1, roll(right, EDGE - STEPS * part), own_members[at, :])
            strip_members[at, :] = jnp.where(
                part_of == 2, roll(left, 2 * EDGE + STEPS - STEPS * part), value
            )
    put_coefficients(coeff, coefficients(strip_coeff[0], strip_coeff[1], strip_coeff[2], True))
    sweep([(x, y, coeff, z.levels // 2, None)], z.rows)
    unit = lanes(z.short) >> 3
    for ref, first, second in ((outer, 1, 6), (beside, 2, 5)):
        quarter = quarters(unit, first, second)
        pieces = []
        for k in range(4):
            rows = pl.ds(k * z.short, z.short)
            pieces.append(roll(x[pl.ds(SUB + k * z.short, z.short), :] * strip_members[rows, :], 16 * k))
        value = overlay(pieces, quarter)
        if ref is outer:
            rights = ((0, value),)
        else:
            rights = ((0, jnp.where((unit & 1) == 0, value, 0.0)), (z.short, jnp.where((unit & 1) == 1, value, 0.0)))
        for at, value in rights:
            high, low = split(value)
            ref[pl.ds(at, z.short), :128] = high
            ref[pl.ds(at, z.short), 128:] = low
    n = z.obs_rows
    own_window, right_window, left_window = windows_of(z)
    gather(z, out, 0, outer[...], cell[...], lambda c: edge_index(z, c, own_window))
    out[:n, :] = (out[:n, :] + inner[...]) * weight[0:1, :]
    right = from_right[pl.ds(z.at_obs, n), :].astype(jnp.int32)
    left = from_left[pl.ds(z.at_obs, n), :].astype(jnp.int32)
    field = beside[...]
    for r in range(0, n, 2):
        pair = lambda v: jnp.concatenate([v[r : r + 1, :], v[r + 1 : r + 2, :]], axis=1)
        i_right, j_right = edge_index(z, pair(right), right_window)
        i_left, j_left = edge_index(z, pair(left), left_window)
        both = jnp.concatenate([one_hot(i_right, z.short), one_hot(i_left, z.short)], axis=0)
        hot[:, pl.ds(r * 128, 256)] = both
        value = lax.dot_general(field, both, (((0,), (0,)), ((), ())), preferred_element_type=F32)
        value = value[:128] + value[128:]
        rows = lax.broadcasted_iota(jnp.int32, (SUB, 256), 0)
        for side, j in enumerate((j_right, j_left)):
            total = None
            for t in range(side, 16, 2):
                piece = jnp.where(rows == j - t * SUB, value[t * SUB : (t + 1) * SUB], 0.0)
                total = piece if total is None else total + piece
            total = jnp.sum(total, axis=0, keepdims=True) * weight[0:1, 0:1]
            at = (1 + side) * n + r
            out[at : at + 1, :] = total[:, :128]
            out[at + 1 : at + 2, :] = total[:, 128:]


def lane_choice(rows, columns, source):
    row = lax.broadcasted_iota(jnp.int32, (rows, columns), 0)
    column = lax.broadcasted_iota(jnp.int32, (rows, columns), 1)
    return jnp.where(row == source(row, column), 1.0, 0.0).astype(BF16)


def strip_to_ends(row, column):
    group, x = column >> 7, column & 127
    lane = 64 * group + jnp.where(x < STEPS, 48 + x, jnp.where(x >= 128 - STEPS, x - 112, 512))
    return (row & 128) + lane


def ready_kernel(z, kappa, scale, ocean, cell, from_left, from_right, strip_coeff, coeff, strip_c, own_lane, beside_lane):
    put_coefficients(coeff, coefficients(kappa[...], scale[...], ocean[...].astype(F32), False))
    put_coefficients(strip_c, coefficients(strip_coeff[0], strip_coeff[1], strip_coeff[2], False))
    _, right_window, left_window = windows_of(z)
    n = z.obs_rows
    right = from_right[pl.ds(z.at_obs, n), :].astype(jnp.int32)
    left = from_left[pl.ds(z.at_obs, n), :].astype(jnp.int32)
    rows = lax.broadcasted_iota(jnp.int32, (128, 128), 0)
    for r in range(n):
        at = pl.ds(r * 128, 128)
        own_lane[:, at] = one_hot(own_index(z, cell[r : r + 1, :])[1], 256)
        j_right = edge_index(z, right[r : r + 1, :], right_window)[1]
        j_left = edge_index(z, left[r : r + 1, :], left_window)[1]
        lane = jnp.where((rows & SUB) == 0, j_right, j_left)
        beside_lane[:, at] = jnp.where(rows == lane, 1.0, 0.0).astype(BF16)


def adjoint_kernel(
    z, alpha, members, weight, obs_weight, from_left, from_right, strip_members, coeff, strip_c,
    own_row, own_lane, beside_row, beside_lane, v0, v1, v2, v3,
    out_hbm, x, y, strip, spare, beside, spread, spread_beside, out, shift, choice, sems,
):
    clear_ends(x, y, strip, spare)
    shift[...] = shift_matrix()
    choice[...] = lane_choice(256, 256, strip_to_ends)
    value = (v0[...] + v1[...]) + (v2[...] + v3[...])
    n = z.obs_rows
    weights = pl.ds(z.at_obs + n, n)

    def spread_out(tops, bottoms, row_hot, lane_hot, start, spread):
        wide = 128
        for k, (top, bottom) in enumerate(zip(split(tops), split(bottoms))):
            for r in range(n):
                at = pl.ds(r * 128, 128)
                line = jnp.concatenate(
                    [jnp.broadcast_to(v[r : r + 1, :].astype(F32), (SUB, 128)) for v in (top, bottom)], axis=0
                ).astype(BF16)
                for t in range(wide // (2 * SUB)):
                    rows = pl.ds(start + t * 2 * SUB, 2 * SUB)
                    spread[pl.ds(k * wide + t * 2 * SUB, 2 * SUB), at] = lane_hot[rows, at] * line
        dims = (((1,), (1,)), ((), ()))
        total = lax.dot_general(row_hot[...], spread[...], dims, preferred_element_type=F32)
        return total[:, :wide] + total[:, wide:]

    amount = obs_weight[...] * value[:n]
    for g in range(2):
        x[pl.ds(SUB + g * z.group, z.group), :] = spread_out(
            amount, amount, own_row, own_lane, g * 128, spread.at[pl.ds(g * 256, 256), :]
        )
    right, left = from_right[weights, :] * value[n : 2 * n], from_left[weights, :] * value[2 * n :]
    field = spread_out(right, left, beside_row, beside_lane, 0, spread_beside)
    beside[...] = jnp.where((lanes(z.short) & SUB) == 0, field[: z.short], field[z.short :])
    lane = lanes(SUB)
    part = (lane >> 4) & 3
    within = lane & 15
    outside = ((part == 1) & (within < STEPS)) | ((part == 2) & (within >= STEPS))
    for q in range(z.group // SUB):
        k, rest = divmod(q * SUB, z.short)
        value = jnp.where(outside, roll(beside[pl.ds(rest, SUB), :], -16 * k), 0.0)
        for g in range(2):
            at = g * z.group + q * SUB
            here = pl.ds(SUB + at, SUB)
            field = x[here, :]
            mine = (lane >> 6) == g
            value = jnp.where(mine & (part == 0), roll(field, EDGE + 64 * g), value)
            value = jnp.where(mine & (part == 3), roll(field, 48 + 64 * g), value)
        strip[pl.ds(SUB + q * SUB, SUB), :] = value * (strip_members[pl.ds(q * SUB, SUB), :] * weight[...])
    here = pl.ds(SUB, z.field)
    x[here, :] = x[here, :] * (members[...].astype(F32) * weight[0:1, :])
    sweep([(x, y, coeff, z.levels, shift), (strip, spare, strip_c, z.levels // 2, None)], z.rows)
    ends = jnp.concatenate(split(strip[pl.ds(SUB, z.group), :]), axis=1)
    ends = jnp.dot(ends, choice[...], preferred_element_type=F32)
    middle = (lane >= STEPS) & (lane < z.columns - STEPS)
    sent = []
    for part in range(z.levels // 2):
        for t in range(z.rows // SUB):
            q = part * z.rows + t * SUB
            for g in range(2):
                at = g * z.group + q
                fixed = jnp.where(middle, x[pl.ds(SUB + at, SUB), :], ends[q : q + SUB, g * 128 : (g + 1) * 128])
                out[pl.ds(at, SUB), :] = alpha[pl.ds(at, SUB), :] + fixed
        if part % 2:
            for g in range(2):
                rows = pl.ds(g * z.group + (part - 1) * z.rows, 2 * z.rows)
                sent.append(pltpu.make_async_copy(out.at[rows, :], out_hbm.at[rows, :], sems.at[len(sent)]))
                sent[-1].start()
    for copy in sent:
        copy.wait()


def local(alpha, members, mem_weight, kappa, norm_scale, land_sea, obs_cell, obs_weight):
    shape = alpha.shape
    z = Sizes(shape[1], shape[2], shape[3], obs_cell.shape[0])
    tiles, holders = lax.axis_size("tile"), lax.axis_size("mem")
    assert holders == 4 and shape[0] == 1
    alpha = alpha.reshape(z.field, z.columns)
    members = members.reshape(z.field, z.columns)
    cell = obs_cell.reshape(z.obs_rows, 128)
    weight = obs_weight.reshape(z.obs_rows, 128)
    whole = pl.BlockSpec(memory_space=pltpu.VMEM)
    stays = pl.BlockSpec(memory_space=pltpu.HBM)
    sds = jax.ShapeDtypeStruct
    main_field = pltpu.VMEM((z.field + 2 * SUB, 128), F32)
    strip_field = pltpu.VMEM((z.group + 2 * SUB, 128), F32)
    coeff = pltpu.VMEM((5, z.rows, 128), F32)
    square = pltpu.VMEM((256, 256), BF16)
    packed = pltpu.VMEM((z.short, 256), BF16)
    payload = sds((z.payload, 128), F32)
    limit = pltpu.CompilerParams(vmem_limit_bytes=24 << 20)
    call = functools.partial(pl.pallas_call, compiler_params=limit)
    given = (alpha, members, kappa, norm_scale, land_sea, cell, weight)
    sent_right, sent_left, *given = call(
        functools.partial(pack_kernel, z),
        out_shape=(payload, payload, *(sds(v.shape, v.dtype) for v in given)),
        in_specs=[stays] * 7,
        out_specs=(whole,) * 9,
        scratch_shapes=[pltpu.SemaphoreType.DMA((7,))],
        name="pack",
    )(*(pltpu.with_memory_space_constraint(v, pltpu.HBM) for v in given))
    alpha, members, kappa, norm_scale, land_sea, cell, weight = given
    up_ring = [(i, (i + 1) % tiles) for i in range(tiles)]
    from_left = lax.ppermute(sent_right, "tile", up_ring)
    from_right = lax.ppermute(sent_left, "tile", [(b, a) for a, b in up_ring])
    inner, own_row, own_x, own_members, own_coeff = call(
        functools.partial(main_kernel, z),
        out_shape=(
            sds((z.obs_rows, 128), F32),
            sds((z.group, z.obs), BF16),
            sds((z.group, 128), F32),
            sds((z.group, 128), F32),
            sds((3, z.rows, 128), F32),
        ),
        in_specs=[whole] * 6,
        out_specs=(whole,) * 5,
        scratch_shapes=[main_field, coeff, main_field, pltpu.VMEM((z.group, 512), BF16), square],
        name="main",
    )(alpha, members, kappa, norm_scale, land_sea, cell)
    factor = jnp.broadcast_to(mem_weight, (SUB, 128))
    values, strip_members, strip_coeff, beside_row = call(
        functools.partial(strip_kernel, z),
        out_shape=(
            sds((3 * z.obs_rows, 128), F32),
            sds((z.group, 128), F32),
            sds((3, z.rows, 128), F32),
            sds((2 * z.short, z.obs), BF16),
        ),
        in_specs=[whole] * 8,
        out_specs=(whole,) * 4,
        scratch_shapes=[coeff, strip_field, strip_field, packed, pltpu.VMEM((2 * z.short, 256), BF16)],
        compiler_params=pltpu.CompilerParams(
            vmem_limit_bytes=24 << 20
        ),
        name="strip",
    )(inner, own_x, own_members, own_coeff, from_left, from_right, cell, factor)
    others = [lax.ppermute(values, "mem", [(i, i ^ k) for i in range(holders)]) for k in range(1, holders)]
    main_c, strip_c, own_lane, beside_lane = call(
        functools.partial(ready_kernel, z),
        out_shape=(
            sds((5, z.rows, 128), F32),
            sds((5, z.rows, 128), F32),
            sds((2 * 128, z.obs), BF16),
            sds((128, z.obs), BF16),
        ),
        in_specs=[whole] * 7,
        out_specs=(whole,) * 4,
        name="ready",
    )(kappa, norm_scale, land_sea, cell, from_left, from_right, strip_coeff)
    product = call(
        functools.partial(adjoint_kernel, z),
        out_shape=sds((z.field, z.columns), F32),
        in_specs=[whole] * 17,
        out_specs=stays,
        scratch_shapes=[
            main_field,
            main_field,
            strip_field,
            strip_field,
            pltpu.VMEM((z.short, 128), F32),
            pltpu.VMEM((512, z.obs), BF16),
            pltpu.VMEM((256, z.obs), BF16),
            pltpu.VMEM((z.field, 128), F32),
            square,
            square,
            pltpu.SemaphoreType.DMA((z.levels // 2,)),
        ],
        name="adjoint",
    )(
        alpha, members, factor, weight, from_left, from_right, strip_members, main_c, strip_c,
        own_row, own_lane, beside_row, beside_lane, values, *others,
    )
    return product.reshape(shape)


def solution(mesh):
    placed = (
        P("mem", None, None, "tile"),
        P("mem", None, None, "tile"),
        P("mem"),
        P(None, "tile"),
        P(None, "tile"),
        P(None, "tile"),
        P("tile"),
        P("tile"),
    )
    return jax.shard_map(
        local, mesh=mesh, in_specs=placed, out_specs=P("mem", None, None, "tile"), check_vma=False
    )
```

```python
import functools

import jax
import jax.numpy as jnp
from jax import lax
from jax.experimental import pallas as pl
from jax.experimental.pallas import tpu as pltpu
from jax.sharding import PartitionSpec as P

STEPS = 8
SUB = 8
EDGE = 2 * STEPS
ASSISTED = 5
F32 = jnp.float32
BF16 = jnp.bfloat16


def div_mod(value, size):
    if size & (size - 1) == 0:
        return value >> (size.bit_length() - 1), value & (size - 1)
    return lax.div(value, size), lax.rem(value, size)


def roll(value, shift, axis=1):
    shift %= value.shape[axis]
    return pltpu.roll(value, shift, axis) if shift else value


def lanes(rows):
    return lax.broadcasted_iota(jnp.int32, (rows, 128), 1)


def split(value):
    high = value.astype(BF16)
    return high, (value - high.astype(F32)).astype(BF16)


class Sizes:
    def __init__(self, levels, rows, columns, obs):
        self.levels, self.rows, self.columns, self.obs = levels, rows, columns, obs
        assert columns == 128 and levels == 16 and rows % 16 == 0 and obs % 256 == 0 and STEPS == 8
        self.field = levels * rows
        self.group = self.field // 2
        self.short = self.field // 8
        self.tiles = rows // SUB
        assert self.tiles == 8
        self.at_members = self.short
        self.at_coeff = self.at_members + rows
        self.at_obs = self.at_coeff + 3 * SUB
        self.obs_rows = obs // 128
        self.payload = self.at_obs + 2 * self.obs_rows


def overlay(pieces, window):
    value = pieces[0]
    for k in range(1, len(pieces)):
        value = jnp.where(window == k, pieces[k], value)
    return value


def pack_kernel(
    z, alpha_hbm, members_hbm, kappa_hbm, scale_hbm, ocean_hbm, cell_hbm, weight_hbm,
    out_right, out_left, alpha, members, kappa, scale, ocean, cell, weight, sems,
):
    pairs = (
        (members_hbm, members), (alpha_hbm, alpha), (kappa_hbm, kappa), (scale_hbm, scale), (ocean_hbm, ocean),
        (cell_hbm, cell), (weight_hbm, weight),
    )
    copies = [pltpu.make_async_copy(a, b, sems.at[k]) for k, (a, b) in enumerate(pairs)]
    for copy in copies:
        copy.start()

    def put(where, right, left):
        out_right[where, :] = right
        out_left[where, :] = left

    for copy in copies[2:]:
        copy.wait()
    lane = lanes(SUB)
    for k, ref in enumerate((kappa, scale, ocean)):
        right, left = [], []
        for t in range(z.tiles):
            value = ref[pl.ds(t * SUB, SUB), :].astype(F32)
            right.append(roll(value, EDGE * (t + 1)))
            left.append(roll(value, EDGE * t))
        put(pl.ds(z.at_coeff + k * SUB, SUB), overlay(right, lane >> 4), overlay(left, lane >> 4))
    n = z.obs_rows
    for at, value in ((z.at_obs, cell[...].astype(F32)), (z.at_obs + n, weight[...])):
        put(pl.ds(at, n), value, value)
    copies[0].wait()
    block = 2 * SUB
    lane = lanes(block)
    for t in range(z.rows // block):
        right, left = [], []
        for g in range(2):
            for part in range(SUB):
                value = members[pl.ds(g * z.group + part * z.rows + t * block, block), :].astype(F32)
                base = 64 * g + STEPS * part
                right.append(roll(value, base + STEPS))
                left.append(roll(value, base))
        put(pl.ds(z.at_members + t * block, block), overlay(right, lane >> 3), overlay(left, lane >> 3))
    copies[1].wait()
    for t in range(z.short // block):
        right, left = [], []
        for g in range(2):
            for h in range(4):
                value = alpha[pl.ds(g * z.group + h * z.short + t * block, block), :]
                base = 64 * g + EDGE * h
                right.append(roll(value, base + EDGE))
                left.append(roll(value, base))
        put(pl.ds(t * block, block), overlay(right, lane >> 4), overlay(left, lane >> 4))


def up(value):
    return roll(value, -1, 0)


def down(value):
    return roll(value, 1, 0)


def coefficients(kappa, scale, ocean, forward):
    row = lax.broadcasted_iota(jnp.int32, kappa.shape, 0)
    north = 0.5 * (kappa + up(kappa)) * ocean * up(ocean)
    north = jnp.where(row == kappa.shape[0] - 1, 0.0, north)
    east = 0.5 * (kappa + roll(kappa, -1)) * ocean * roll(ocean, -1)
    west, south = roll(east, 1), down(north)
    centre = 1.0 - (east + west) - (north + south)
    if forward:
        return (
            centre * scale,
            east * roll(scale, -1),
            west * roll(scale, 1),
            north * up(scale),
            south * down(scale),
        )
    return tuple(scale * c for c in (centre, east, west, north, south))


def put_coefficients(ref, values):
    for k, value in enumerate(values):
        ref[k] = value


def shift_matrix():
    row = lax.broadcasted_iota(jnp.int32, (256, 256), 0)
    column = lax.broadcasted_iota(jnp.int32, (256, 256), 1)
    wanted = jnp.where(column < 128, column + 1, column - 1)
    return jnp.where((row & 127) == (wanted & 127), 1.0, 0.0).astype(BF16)


def step_rows(source, target, coeff, rows, levels, shift):
    assisted = 0
    if shift is not None:
        assisted = ASSISTED
        both = jnp.concatenate(split(source[pl.ds(SUB, assisted * rows), :]), axis=1)
        beside = jnp.dot(both, shift[...], preferred_element_type=F32)
    for t in range(rows // SUB):
        c = [coeff[k, pl.ds(t * SUB, SUB), :] for k in range(5)]
        for level in range(levels):
            r = level * rows + t * SUB
            at = SUB + r
            u = source[pl.ds(at, SUB), :]
            along = c[3] * source[pl.ds(at + 1, SUB), :] + c[4] * source[pl.ds(at - 1, SUB), :]
            if level < assisted:
                across = c[1] * beside[r : r + SUB, :128] + c[2] * beside[r : r + SUB, 128:]
            else:
                across = c[1] * roll(u, -1) + c[2] * roll(u, 1)
            target[pl.ds(at, SUB), :] = c[0] * u + across + along


def clear_ends(*buffers):
    for ref in buffers:
        zero = jnp.zeros((SUB, 128), F32)
        ref[pl.ds(0, SUB), :] = zero
        ref[pl.ds(ref.shape[0] - SUB, SUB), :] = zero


def sweep(fields, rows):
    for step in range(STEPS):
        for x, y, coeff, levels, shift in fields:
            source, target = (y, x) if step % 2 else (x, y)
            step_rows(source, target, coeff, rows, levels, shift)


def cell_parts(z, cell):
    level, rest = div_mod(cell, z.rows * z.columns)
    row, column = div_mod(rest, z.columns)
    return level >> 3, level & 7, row, column


def own_index(z, cell):
    group, part, row, column = cell_parts(z, cell)
    return part * z.rows + row, group * 128 + column


def edge_index(z, cell, windows):
    group, part, row, column = cell_parts(z, cell)
    inside, lane = False, 0
    for first, at in windows:
        here = (column >= first) & (column < first + STEPS)
        inside = here | inside
        lane = jnp.where(here, at - first, lane)
    lane = lane + column + 64 * group + 16 * (part >> 1)
    return jnp.where(inside, (part & 1) * z.rows + row, -1), lane & 127


def own_edges(z):
    return (0, 48), (z.columns - STEPS, 8)


def windows_of(z):
    return own_edges(z), ((0, 16),), ((z.columns - STEPS, 40),)


def quarters(unit, first, second):
    even, odd = (first, second) if first % 2 == 0 else (second, first)
    return jnp.where((unit & 1) == 0, ((unit - even) >> 1) & 3, ((unit - odd) >> 1) & 3)


def one_hot(index, size):
    rows = lax.broadcasted_iota(jnp.int32, (size, index.shape[1]), 0)
    return jnp.where(rows == index, 1.0, 0.0).astype(BF16)


def read_off(field, hot, j):
    value = lax.dot_general(field, hot, (((0,), (0,)), ((), ())), preferred_element_type=F32)
    n = value.shape[0] // 2
    value = value[:n] + value[n:]
    rows = lax.broadcasted_iota(jnp.int32, value.shape, 0)
    return jnp.sum(jnp.where(rows == j, value, 0.0), axis=0, keepdims=True)


def gather(z, out, at, field, cell, index, keep=None, start=0):
    for n in range(z.obs_rows // 2):
        row = jnp.concatenate([cell[2 * n : 2 * n + 1, :], cell[2 * n + 1 : 2 * n + 2, :]], axis=1)
        i, j = index(row)
        hot = one_hot(i, field.shape[0])
        if keep is not None:
            keep[:, pl.ds(start + 256 * n, 256)] = hot
        value = read_off(field, hot, j)
        out[at + 2 * n : at + 2 * n + 1, :] = value[:, :128]
        out[at + 2 * n + 1 : at + 2 * n + 2, :] = value[:, 128:]


def forward_sweep(z, alpha, kappa, scale, ocean, coeff, x, y, shift):
    put_coefficients(coeff, coefficients(kappa[...], scale[...], ocean[...].astype(F32), True))
    clear_ends(x, y)
    x[pl.ds(SUB, z.field), :] = alpha[...]
    shift[...] = shift_matrix()
    sweep([(x, y, coeff, z.levels, shift)], z.rows)


def own_columns(pair, lane):
    pieces = []
    for g, value in enumerate(pair):
        pieces += [roll(value, EDGE + 64 * g), roll(value, 48 + 64 * g)]
    return overlay(pieces, (lane >> 6) * 2 + ((lane >> 5) & 1))


def main_kernel(
    z, alpha, members, kappa, scale, ocean, cell, out, hot, strip_x, strip_members, strip_coeff,
    x, coeff, y, both, shift,
):
    forward_sweep(z, alpha, kappa, scale, ocean, coeff, x, y, shift)
    lane = lanes(z.group)
    inner = (lane >= STEPS) & (lane < z.columns - STEPS)
    for g in range(2):
        rows = pl.ds(g * z.group, z.group)
        value = x[pl.ds(SUB + g * z.group, z.group), :] * members[rows, :].astype(F32)
        high, low = split(jnp.where(inner, value, 0.0))
        both[:, pl.ds(g * 128, 128)] = high
        both[:, pl.ds(256 + g * 128, 128)] = low
    gather(z, out, 0, both[...], cell[...], lambda c: own_index(z, c), hot)
    block = 2 * SUB
    lane = lanes(block)
    for t in range(z.group // block):
        rows = [pl.ds(g * z.group + t * block, block) for g in range(2)]
        strip_x[pl.ds(t * block, block), :] = own_columns([alpha[r, :] for r in rows], lane)
        strip_members[pl.ds(t * block, block), :] = own_columns([members[r, :].astype(F32) for r in rows], lane)
    lane = lanes(z.rows)
    for k, ref in enumerate((kappa, scale, ocean)):
        value = ref[...].astype(F32)
        strip_coeff[k] = own_columns([value, value], lane)


def strip_kernel(
    z, inner, own_x, own_members, own_coeff, from_left, from_right, cell, weight,
    out, strip_members, strip_coeff, coeff, x, y, outer, beside,
):
    clear_ends(x, y)
    lane = lanes(SUB)
    part_of = (lane >> 4) & 3
    for k in range(3):
        rows = pl.ds(z.at_coeff + k * SUB, SUB)
        right, left = from_right[rows, :], from_left[rows, :]
        for t in range(z.tiles):
            pieces = []
            for g in range(2):
                pieces += [roll(right, EDGE * (1 - t) + 64 * g), roll(left, EDGE * (2 - t) + 64 * g)]
            value = overlay(pieces, (lane >> 6) * 2 + ((lane >> 5) & 1))
            at = pl.ds(t * SUB, SUB)
            strip_coeff[k, at, :] = jnp.where((part_of == 1) | (part_of == 2), value, own_coeff[k, at, :])
    for q in range(z.short // SUB):
        right, left = from_right[pl.ds(q * SUB, SUB), :], from_left[pl.ds(q * SUB, SUB), :]
        for h in range(4):
            at = h * z.short + q * SUB
            value = jnp.where(part_of == 1, roll(right, EDGE * (1 - h)), own_x[pl.ds(at, SUB), :])
            x[pl.ds(SUB + at, SUB), :] = jnp.where(part_of == 2, roll(left, EDGE * (2 - h)), value)
    for t in range(z.tiles):
        rows = pl.ds(z.at_members + t * SUB, SUB)
        right, left = from_right[rows, :], from_left[rows, :]
        for part in range(SUB):
            at = pl.ds(part * z.rows + t * SUB, SUB)
            value = jnp.where(part_of == 1, roll(right, EDGE - STEPS * part), own_members[at, :])
            strip_members[at, :] = jnp.where(
                part_of == 2, roll(left, 2 * EDGE + STEPS - STEPS * part), value
            )
    put_coefficients(coeff, coefficients(strip_coeff[0], strip_coeff[1], strip_coeff[2], True))
    sweep([(x, y, coeff, z.levels // 2, None)], z.rows)
    unit = lanes(z.short) >> 3
    for ref, first, second in ((outer, 1, 6), (beside, 2, 5)):
        quarter = quarters(unit, first, second)
        pieces = []
        for k in range(4):
            rows = pl.ds(k * z.short, z.short)
            pieces.append(roll(x[pl.ds(SUB + k * z.short, z.short), :] * strip_members[rows, :], 16 * k))
        value = overlay(pieces, quarter)
        if ref is outer:
            rights = ((0, value),)
        else:
            rights = ((0, jnp.where((unit & 1) == 0, value, 0.0)), (z.short, jnp.where((unit & 1) == 1, value, 0.0)))
        for at, value in rights:
            high, low = split(value)
            ref[pl.ds(at, z.short), :128] = high
            ref[pl.ds(at, z.short), 128:] = low
    n = z.obs_rows
    own_window, right_window, left_window = windows_of(z)
    gather(z, out, 0, outer[...], cell[...], lambda c: edge_index(z, c, own_window))
    out[:n, :] = (out[:n, :] + inner[...]) * weight[0:1, :]
    right = from_right[pl.ds(z.at_obs, n), :].astype(jnp.int32)
    left = from_left[pl.ds(z.at_obs, n), :].astype(jnp.int32)
    field = beside[...]
    for r in range(0, n, 2):
        pair = lambda v: jnp.concatenate([v[r : r + 1, :], v[r + 1 : r + 2, :]], axis=1)
        i_right, j_right = edge_index(z, pair(right), right_window)
        i_left, j_left = edge_index(z, pair(left), left_window)
        both = jnp.concatenate([one_hot(i_right, z.short), one_hot(i_left, z.short)], axis=0)
        value = lax.dot_general(field, both, (((0,), (0,)), ((), ())), preferred_element_type=F32)
        value = value[:128] + value[128:]
        rows = lax.broadcasted_iota(jnp.int32, (SUB, 256), 0)
        for side, j in enumerate((j_right, j_left)):
            total = None
            for t in range(side, 16, 2):
                piece = jnp.where(rows == j - t * SUB, value[t * SUB : (t + 1) * SUB], 0.0)
                total = piece if total is None else total + piece
            total = jnp.sum(total, axis=0, keepdims=True) * weight[0:1, 0:1]
            at = (1 + side) * n + r
            out[at : at + 1, :] = total[:, :128]
            out[at + 1 : at + 2, :] = total[:, 128:]


def lane_choice(rows, columns, source):
    row = lax.broadcasted_iota(jnp.int32, (rows, columns), 0)
    column = lax.broadcasted_iota(jnp.int32, (rows, columns), 1)
    return jnp.where(row == source(row, column), 1.0, 0.0).astype(BF16)


def strip_to_ends(row, column):
    group, x = column >> 7, column & 127
    lane = 64 * group + jnp.where(x < STEPS, 48 + x, jnp.where(x >= 128 - STEPS, x - 112, 512))
    return (row & 128) + lane


def ready_kernel(z, kappa, scale, ocean, cell, from_left, from_right, strip_coeff, coeff, strip_c, own_lane, beside_row, beside_lane):
    put_coefficients(coeff, coefficients(kappa[...], scale[...], ocean[...].astype(F32), False))
    put_coefficients(strip_c, coefficients(strip_coeff[0], strip_coeff[1], strip_coeff[2], False))
    _, right_window, left_window = windows_of(z)
    n = z.obs_rows
    right = from_right[pl.ds(z.at_obs, n), :].astype(jnp.int32)
    left = from_left[pl.ds(z.at_obs, n), :].astype(jnp.int32)
    rows = lax.broadcasted_iota(jnp.int32, (128, 128), 0)
    for r in range(n):
        at = pl.ds(r * 128, 128)
        own_lane[:, at] = one_hot(own_index(z, cell[r : r + 1, :])[1], 256)
        i_right, j_right = edge_index(z, right[r : r + 1, :], right_window)
        i_left, j_left = edge_index(z, left[r : r + 1, :], left_window)
        beside_row[pl.ds(0, z.short), at] = one_hot(i_right, z.short)
        beside_row[pl.ds(z.short, z.short), at] = one_hot(i_left, z.short)
        lane = jnp.where((rows & SUB) == 0, j_right, j_left)
        beside_lane[:, at] = jnp.where(rows == lane, 1.0, 0.0).astype(BF16)


def adjoint_kernel(
    z, alpha, members, weight, obs_weight, from_left, from_right, strip_members, coeff, strip_c,
    own_row, own_lane, beside_row, beside_lane, v0, v1, v2, v3,
    out_hbm, x, y, strip, spare, beside, spread, spread_beside, out, shift, choice, sems,
):
    clear_ends(x, y, strip, spare)
    shift[...] = shift_matrix()
    choice[...] = lane_choice(256, 256, strip_to_ends)
    value = (v0[...] + v1[...]) + (v2[...] + v3[...])
    n = z.obs_rows
    weights = pl.ds(z.at_obs + n, n)

    def spread_out(tops, bottoms, row_hot, lane_hot, start, spread):
        wide = 128
        for k, (top, bottom) in enumerate(zip(split(tops), split(bottoms))):
            for r in range(n):
                at = pl.ds(r * 128, 128)
                line = jnp.concatenate(
                    [jnp.broadcast_to(v[r : r + 1, :].astype(F32), (SUB, 128)) for v in (top, bottom)], axis=0
                ).astype(BF16)
                for t in range(wide // (2 * SUB)):
                    rows = pl.ds(start + t * 2 * SUB, 2 * SUB)
                    spread[pl.ds(k * wide + t * 2 * SUB, 2 * SUB), at] = lane_hot[rows, at] * line
        dims = (((1,), (1,)), ((), ()))
        total = lax.dot_general(row_hot[...], spread[...], dims, preferred_element_type=F32)
        return total[:, :wide] + total[:, wide:]

    amount = obs_weight[...] * value[:n]
    for g in range(2):
        x[pl.ds(SUB + g * z.group, z.group), :] = spread_out(
            amount, amount, own_row, own_lane, g * 128, spread.at[pl.ds(g * 256, 256), :]
        )
    right, left = from_right[weights, :] * value[n : 2 * n], from_left[weights, :] * value[2 * n :]
    field = spread_out(right, left, beside_row, beside_lane, 0, spread_beside)
    beside[...] = jnp.where((lanes(z.short) & SUB) == 0, field[: z.short], field[z.short :])
    lane = lanes(SUB)
    part = (lane >> 4) & 3
    within = lane & 15
    outside = ((part == 1) & (within < STEPS)) | ((part == 2) & (within >= STEPS))
    for q in range(z.group // SUB):
        k, rest = divmod(q * SUB, z.short)
        value = jnp.where(outside, roll(beside[pl.ds(rest, SUB), :], -16 * k), 0.0)
        for g in range(2):
            at = g * z.group + q * SUB
            here = pl.ds(SUB + at, SUB)
            field = x[here, :]
            mine = (lane >> 6) == g
            value = jnp.where(mine & (part == 0), roll(field, EDGE + 64 * g), value)
            value = jnp.where(mine & (part == 3), roll(field, 48 + 64 * g), value)
        strip[pl.ds(SUB + q * SUB, SUB), :] = value * (strip_members[pl.ds(q * SUB, SUB), :] * weight[...])
    here = pl.ds(SUB, z.field)
    x[here, :] = x[here, :] * (members[...].astype(F32) * weight[0:1, :])
    sweep([(x, y, coeff, z.levels, shift), (strip, spare, strip_c, z.levels // 2, None)], z.rows)
    ends = jnp.concatenate(split(strip[pl.ds(SUB, z.group), :]), axis=1)
    ends = jnp.dot(ends, choice[...], preferred_element_type=F32)
    middle = (lane >= STEPS) & (lane < z.columns - STEPS)
    sent = []
    for part in range(z.levels // 2):
        for t in range(z.rows // SUB):
            q = part * z.rows + t * SUB
            for g in range(2):
                at = g * z.group + q
                fixed = jnp.where(middle, x[pl.ds(SUB + at, SUB), :], ends[q : q + SUB, g * 128 : (g + 1) * 128])
                out[pl.ds(at, SUB), :] = alpha[pl.ds(at, SUB), :] + fixed
        if part % 2:
            for g in range(2):
                rows = pl.ds(g * z.group + (part - 1) * z.rows, 2 * z.rows)
                sent.append(pltpu.make_async_copy(out.at[rows, :], out_hbm.at[rows, :], sems.at[len(sent)]))
                sent[-1].start()
    for copy in sent:
        copy.wait()


def local(alpha, members, mem_weight, kappa, norm_scale, land_sea, obs_cell, obs_weight):
    shape = alpha.shape
    z = Sizes(shape[1], shape[2], shape[3], obs_cell.shape[0])
    tiles, holders = lax.axis_size("tile"), lax.axis_size("mem")
    assert holders == 4 and shape[0] == 1
    alpha = alpha.reshape(z.field, z.columns)
    members = members.reshape(z.field, z.columns)
    cell = obs_cell.reshape(z.obs_rows, 128)
    weight = obs_weight.reshape(z.obs_rows, 128)
    whole = pl.BlockSpec(memory_space=pltpu.VMEM)
    stays = pl.BlockSpec(memory_space=pltpu.HBM)
    sds = jax.ShapeDtypeStruct
    main_field = pltpu.VMEM((z.field + 2 * SUB, 128), F32)
    strip_field = pltpu.VMEM((z.group + 2 * SUB, 128), F32)
    coeff = pltpu.VMEM((5, z.rows, 128), F32)
    square = pltpu.VMEM((256, 256), BF16)
    packed = pltpu.VMEM((z.short, 256), BF16)
    payload = sds((z.payload, 128), F32)
    limit = pltpu.CompilerParams(vmem_limit_bytes=24 << 20)
    call = functools.partial(pl.pallas_call, compiler_params=limit)
    given = (alpha, members, kappa, norm_scale, land_sea, cell, weight)
    sent_right, sent_left, *given = call(
        functools.partial(pack_kernel, z),
        out_shape=(payload, payload, *(sds(v.shape, v.dtype) for v in given)),
        in_specs=[stays] * 7,
        out_specs=(whole,) * 9,
        scratch_shapes=[pltpu.SemaphoreType.DMA((7,))],
        name="pack",
    )(*(pltpu.with_memory_space_constraint(v, pltpu.HBM) for v in given))
    alpha, members, kappa, norm_scale, land_sea, cell, weight = given
    up_ring = [(i, (i + 1) % tiles) for i in range(tiles)]
    from_left = lax.ppermute(sent_right, "tile", up_ring)
    from_right = lax.ppermute(sent_left, "tile", [(b, a) for a, b in up_ring])
    inner, own_row, own_x, own_members, own_coeff = call(
        functools.partial(main_kernel, z),
        out_shape=(
            sds((z.obs_rows, 128), F32),
            sds((z.group, z.obs), BF16),
            sds((z.group, 128), F32),
            sds((z.group, 128), F32),
            sds((3, z.rows, 128), F32),
        ),
        in_specs=[whole] * 6,
        out_specs=(whole,) * 5,
        scratch_shapes=[main_field, coeff, main_field, pltpu.VMEM((z.group, 512), BF16), square],
        name="main",
    )(alpha, members, kappa, norm_scale, land_sea, cell)
    factor = jnp.broadcast_to(mem_weight, (SUB, 128))
    values, strip_members, strip_coeff = call(
        functools.partial(strip_kernel, z),
        out_shape=(
            sds((3 * z.obs_rows, 128), F32),
            sds((z.group, 128), F32),
            sds((3, z.rows, 128), F32),
        ),
        in_specs=[whole] * 8,
        out_specs=(whole,) * 3,
        scratch_shapes=[coeff, strip_field, strip_field, packed, pltpu.VMEM((2 * z.short, 256), BF16)],
        compiler_params=pltpu.CompilerParams(
            vmem_limit_bytes=24 << 20
        ),
        name="strip",
    )(inner, own_x, own_members, own_coeff, from_left, from_right, cell, factor)
    others = [lax.ppermute(values, "mem", [(i, i ^ k) for i in range(holders)]) for k in range(1, holders)]
    main_c, strip_c, own_lane, beside_row, beside_lane = call(
        functools.partial(ready_kernel, z),
        out_shape=(
            sds((5, z.rows, 128), F32),
            sds((5, z.rows, 128), F32),
            sds((2 * 128, z.obs), BF16),
            sds((2 * z.short, z.obs), BF16),
            sds((128, z.obs), BF16),
        ),
        in_specs=[whole] * 7,
        out_specs=(whole,) * 5,
        name="ready",
    )(kappa, norm_scale, land_sea, cell, from_left, from_right, strip_coeff)
    product = call(
        functools.partial(adjoint_kernel, z),
        out_shape=sds((z.field, z.columns), F32),
        in_specs=[whole] * 17,
        out_specs=stays,
        scratch_shapes=[
            main_field,
            main_field,
            strip_field,
            strip_field,
            pltpu.VMEM((z.short, 128), F32),
            pltpu.VMEM((512, z.obs), BF16),
            pltpu.VMEM((256, z.obs), BF16),
            pltpu.VMEM((z.field, 128), F32),
            square,
            square,
            pltpu.SemaphoreType.DMA((z.levels // 2,)),
        ],
        name="adjoint",
    )(
        alpha, members, factor, weight, from_left, from_right, strip_members, main_c, strip_c,
        own_row, own_lane, beside_row, beside_lane, values, *others,
    )
    return product.reshape(shape)


def solution(mesh):
    placed = (
        P("mem", None, None, "tile"),
        P("mem", None, None, "tile"),
        P("mem"),
        P(None, "tile"),
        P(None, "tile"),
        P(None, "tile"),
        P("tile"),
        P("tile"),
    )
    return jax.shard_map(
        local, mesh=mesh, in_specs=placed, out_specs=P("mem", None, None, "tile"), check_vma=False
    )
```
